32 devices in a mesh: dp: 8 (over z, y), rep: 4 (over x, core).
Axes of the slice: x: 2, y: 2, z: 4, core: 2. Of those that a mesh axis runs over, the one named last changes fastest.
Arguments:
- x_in: bfloat16 [16384, 768], P(('dp', 'rep')), may hold values from -6 to 6
- seq_lens: int32 [32, 3], P(('dp', 'rep')), may hold values from 1 to 384, 512 in all within a row
- routes: int32 [16384, 2], P(('dp', 'rep')), may hold values from 0 to 11, all different within a row; in each aligned block of 512 rows (0 to 511, 512 to 1023, ...) at most 128 rows name the same one
- positions: int32 [4096], P(('dp', 'rep')), may hold values from 0 to 511, as said below
- targets: int32 [4, 8, 128], P('rep'), may hold values from 0 to 65535
- dense_w: float32 [768, 3072], P(None, ('dp', 'rep')), may hold values from -0.3125 to 0.3125
- small_w: float32 [21, 768], P(None, ('dp', 'rep'))
- expert_in: float32 [2, 768, 16384], P(None, 'rep', 'dp'), may hold values from -0.21875 to 0.21875
- expert_out: float32 [16384, 768], P(('dp', 'rep')), may hold values from -0.75 to 0.75
- table: float32 [65536, 768], P(('dp', 'rep')), may hold values from -0.4375 to 0.4375
- dense_m: float32 [768, 3072], P(None, ('dp', 'rep')), may hold values from -0.21875 to 0.21875
- small_m: float32 [21, 768], P(None, ('dp', 'rep')), may hold values from -0.21875 to 0.21875
- expin_m: float32 [2, 768, 16384], P(None, 'rep', 'dp'), may hold values from -0.0546875 to 0.0546875
- expout_m: float32 [16384, 768], P(('dp', 'rep')), may hold values from -0.0068359375 to 0.0068359375
- table_m: float32 [65536, 768], P(('dp', 'rep')), may hold values from -0.00036621094 to 0.00036621094
- dense_v: float32 [768, 3072], P(None, ('dp', 'rep')), may hold values from 0.0013020834 to 0.0052083335
- small_v: float32 [21, 768], P(None, ('dp', 'rep')), may hold values from 0.0013020834 to 0.0052083335
- expin_v: float32 [2, 768, 16384], P(None, 'rep', 'dp'), may hold values from 3.2958986e-05 to 0.00013061524
- expout_v: float32 [16384, 768], P(('dp', 'rep')), may hold values from 3.2552084e-06 to 1.3020834e-05
- table_v: float32 [65536, 768], P(('dp', 'rep')), may hold values from 3.2014214e-09 to 1.2805685e-08
Outputs:
- loss: float32 [], replicated
- lamb_norms: float32 [3, 7], replicated
- dense_m_new: float32 [768, 3072], P(None, ('dp', 'rep'))
- dense_v_new: float32 [768, 3072], P(None, ('dp', 'rep'))
- dense_w_new: float32 [768, 3072], P(None, ('dp', 'rep'))
- dense_w_low: bfloat16 [768, 3072], P(None, ('dp', 'rep'))
- small_m_new: float32 [21, 768], P(None, ('dp', 'rep'))
- small_v_new: float32 [21, 768], P(None, ('dp', 'rep'))
- small_w_new: float32 [21, 768], P(None, ('dp', 'rep'))
- small_w_low: bfloat16 [21, 768], P(None, ('dp', 'rep'))
- expin_m_new: float32 [2, 768, 16384], P(None, 'rep', 'dp')
- expin_v_new: float32 [2, 768, 16384], P(None, 'rep', 'dp')
- expin_w_new: float32 [2, 768, 16384], P(None, 'rep', 'dp')
- expin_w_low: bfloat16 [2, 768, 16384], P(None, 'rep', 'dp')
- expout_m_new: float32 [16384, 768], P(('dp', 'rep'))
- expout_v_new: float32 [16384, 768], P(('dp', 'rep'))
- expout_w_new: float32 [16384, 768], P(('dp', 'rep'))
- expout_w_low: bfloat16 [16384, 768], P(('dp', 'rep'))
- table_m_new: float32 [65536, 768], P(('dp', 'rep'))
- table_v_new: float32 [65536, 768], P(('dp', 'rep'))
- table_w_new: float32 [65536, 768], P(('dp', 'rep'))
- table_w_low: bfloat16 [65536, 768], P(('dp', 'rep'))
The draws below stay inside these ranges and needn't reach their ends.
Inputs may be any that keep to these rules, and one draw needn't show every extreme that they name: `seq_lens`: each row sums to 512; the longest sequence is exactly 384. `routes`: the two experts of a token differ. No expert is named by more than 128 rows of one device; some device has an expert named by exactly 128 rows. The 128 positions of one device are distinct.
All inputs are finite; a program needn't handle non-finite values.
Results may differ from the reference program's by a relative error of at most 0.018.
Values may be sent and summed in bfloat16 or wider, within the bound.
No kernel may reach another device: no remote copies, remote signals or barrier semaphores. Data moves between devices by JAX's collectives and lax.ppermute only.
A program may use at most 256 MiB of HBM per device.

```python
import math
import jax
import jax.numpy as jnp
import numpy as np
from jax import lax

D = 768
HEADS = 12
HDIM = 64
FF = 2048
EXPERTS = 8
NULLS = 4
VOCAB = 65536
TOP = 2
NSEQ = 3
STEP = 5
TOK_DEV = 512
CAP = 96
ROUTE_MOST = 128
POS_DEV = 128
SEQ_MOST = 384
TOKENS = 16384
NPOS = 4096
N_DP = 8
N_REP = 4
DEVICES = 32


def draw_positions(key, part):
    keys = jax.random.split(key, DEVICES)
    picks = jax.vmap(lambda k: jax.random.permutation(k, TOK_DEV)[:POS_DEV])(keys)
    return picks.reshape(NPOS).astype(jnp.int32)


def draw_small_w(key, part):
    key_gain = jax.random.fold_in(key, 11)
    key_route = jax.random.fold_in(key, 12)
    key_vector = jax.random.fold_in(key, 13)
    gains = 1.0 + 0.1 * jax.random.uniform(key_gain, (3, D), jnp.float32, -1.0, 1.0)
    vectors = jax.random.normal(key_vector, (2, D), jnp.float32)
    router = 0.75 * jax.random.normal(key_route, (16, D), jnp.float32) * D ** (-0.5)
    return jnp.concatenate([gains, vectors, router], 0).astype(jnp.float32)


def place_ends(array, own_key, smallest, top_value):
    longest = array.shape.index(max(array.shape))
    spots = []
    for shift in (0, 1):
        where = [jax.random.randint(jax.random.fold_in(own_key, axis), (), 0, length) for axis, length in enumerate(array.shape)]
        where[longest] = (where[longest] + shift) % array.shape[longest]
        spots.append(tuple(where))
    return array.at[spots[0]].set(smallest).at[spots[1]].set(top_value)


def block_scale(stream_key, shape, pieces, smallest, largest):
    level, own = 1.0, jax.random.fold_in(stream_key, 6)
    for dim, blocks in pieces:
        heights = jnp.exp(jax.random.uniform(jax.random.fold_in(own, dim), (blocks,), jnp.float32, smallest / len(pieces), largest / len(pieces)))
        level = level * jnp.repeat(heights, shape[dim] // blocks).reshape([-1 if axis == dim else 1 for axis in range(len(shape))])
    return level


def rank_table(amount, lean):
    loads = [(1 << 20) // math.isqrt(rank ** lean) + 1 for rank in range(1, amount + 1)]
    deviation = 1 + sum(loads) // (1 << 30)
    return np.cumsum(np.array([max(1, weight // deviation) for weight in loads]))


def ranked(rng, dims, number_of, slope):
    grid = rank_table(number_of, slope)
    ticket = jax.random.randint(jax.random.fold_in(rng, 1), dims, 0, int(grid[number_of - 1]))
    grade = jnp.searchsorted(jnp.asarray(grid, jnp.int32), ticket, side="right")
    return jax.random.permutation(jax.random.fold_in(rng, 2), number_of)[grade].astype(jnp.int32)


def split_up(count, total, bound, lean):
    loads = [(1 << 20) // math.isqrt(rank ** lean) + 1 for rank in range(2, count + 1)]
    spare, given = total - bound - (count - 1), [1] * (count - 1)
    while spare > 0:
        free = [i for i in range(count - 1) if given[i] < bound]
        pool, budget = sum([loads[i] for i in free]), spare
        for i in free:
            extra = min(bound - given[i], max(1, budget * loads[i] // pool), spare)
            given[i] = given[i] + extra
            spare = spare - extra
    return np.array([bound] + given)


def ragged(rng, amount, total, bound, lean):
    if amount == 2:
        one = jax.random.randint(rng, (), max(1, total - bound), min(bound, total - 1) + 1)
        return jnp.stack([one, total - one])
    tallies = jnp.asarray(split_up(amount, total, bound, lean), jnp.int32)
    couples = (amount - 1) // 2
    source_of, receiver = tallies[1:1 + 2 * couples:2], tallies[2:2 + 2 * couples:2]
    room = jnp.minimum(source_of - 1, bound - receiver)
    passed = jax.random.randint(jax.random.fold_in(rng, 1), (couples,), 0, 1 << 20) % (room + 1)
    tallies = tallies.at[1:1 + 2 * couples:2].set(source_of - passed).at[2:2 + 2 * couples:2].set(receiver + passed)
    return tallies[jax.random.permutation(jax.random.fold_in(rng, 2), amount)]


def shared_out(own_key, own, number, rows, count, top, bound, lean):
    sequence = jax.random.permutation(own_key, count)
    heavy_load, common = shares(count, rows * top, bound, lean, True), shares(count, rows * top, bound, lean, False)
    places = jnp.arange(count)

    def named(lengths, turn):
        used = int((lengths > 0).sum())
        fixed = max(1, used // 4)
        moved = fixed + (places - fixed + turn * (used - fixed)) % max(1, count - fixed)
        return jnp.zeros((count,), jnp.int32).at[sequence[jnp.where(places < fixed, places, moved)]].set(jnp.asarray(lengths, jnp.int32))

    lengths = jnp.where(number % 4 == 0, named(heavy_load, number // 4), named(common, number - number // 4 - 1))
    mixed = jax.random.permutation(jax.random.fold_in(own, 3), count)
    donor, sink = mixed[0:count // 2 * 2:2], mixed[1:count // 2 * 2:2]
    room = jnp.minimum(lengths[donor] - 1, bound - lengths[sink]) // 2
    room = jnp.where((donor == sequence[0]) | (sink == sequence[0]) | (lengths[sink] == 0), 0, jnp.maximum(room, 0))
    moved = jax.random.randint(jax.random.fold_in(own, 4), (count // 2,), 0, 1 << 20) % (room + 1)
    lengths = lengths.at[donor].add(-moved).at[sink].add(moved)
    labels = jnp.searchsorted(jnp.cumsum(lengths), jnp.arange(rows * top), side="right").astype(jnp.int32)
    grid = labels.reshape(top, rows).T
    grid = grid[jax.random.permutation(jax.random.fold_in(own, 1), rows)]
    turn = jax.random.randint(jax.random.fold_in(own, 2), (rows, 1), 0, top)
    return jnp.take_along_axis(grid, (jnp.arange(top)[None, :] + turn) % top, axis=1)


def shares(amount, total, limit, skew, full):
    weights = [(1 << 20) // math.isqrt(standing ** skew) + 1 for standing in range(1, amount + 1)]
    largest = limit if full else min(limit, max(-(-total // amount), total * weights[0] // sum(weights)))
    least = 1 if total - largest >= amount - 1 else 0
    holding, surplus = [largest] + [least] * (amount - 1), total - largest - least * (amount - 1)
    while surplus > 0:
        candidates = [i for i in range(1, amount) if holding[i] < largest] or [i for i in range(1, amount) if holding[i] < limit]
        mass, budget = sum([weights[i] for i in candidates]), surplus
        for i in candidates:
            extra = min(limit - holding[i], max(1, budget * weights[i] // mass), surplus)
            holding[i] = holding[i] + extra
            surplus = surplus - extra
    return np.array(holding)


def centred(stream_key, shape, width, reach, cuts=(), kind=jnp.bfloat16):
    values = jax.random.normal(stream_key, shape, jnp.float32) * width
    if len(cuts) > 0:
        values = block_scale(stream_key, shape, cuts, -0.22, 0.18) * values
    return jnp.clip(values, min=-reach, max=reach).astype(kind)


def setup_inputs(seed: int = 0) -> dict:
    seeds = jax.random.split(jax.random.key(seed), 21)
    x_in = centred(seeds[0], (TOKENS, D), 1.0, 6.0, ((0, 32),))
    seq_lens = jax.vmap(lambda own: ragged(own, NSEQ, TOK_DEV, SEQ_MOST, 2))(jax.random.split(seeds[1], DEVICES)).reshape((DEVICES, NSEQ)).astype(jnp.int32)
    routes_keys = jax.random.split(jax.random.fold_in(seeds[2], 1), TOKENS // TOK_DEV)
    routes_turns = jax.random.permutation(jax.random.fold_in(seeds[2], 3), TOKENS // TOK_DEV)
    routes = jax.vmap(lambda own, number: shared_out(jax.random.fold_in(seeds[2], 2), own, number, TOK_DEV, EXPERTS + NULLS, TOP, ROUTE_MOST, 2))(routes_keys, routes_turns).reshape((TOKENS, TOP))
    positions = draw_positions(jax.random.fold_in(seeds[20], 71), 0)
    targets = place_ends(ranked(seeds[4], (N_REP, N_DP, POS_DEV), VOCAB, 2), jax.random.fold_in(seeds[4], 3), 0, VOCAB - 1).astype(jnp.int32)
    dense_w = centred(seeds[5], (D, 4 * D), (D // 2) ** -0.5, 0.3125, ((1, 32),), jnp.float32)
    small_w = draw_small_w(jax.random.fold_in(seeds[20], 71), 0)
    expert_in = centred(seeds[7], (2, D, EXPERTS * FF), D ** -0.5, 0.21875, ((1, 4), (2, 8)), jnp.float32)
    expert_out = centred(seeds[8], (EXPERTS * FF, D), (FF // 32) ** -0.5, 0.75, ((0, 32),), jnp.float32)
    table = centred(seeds[9], (VOCAB, D), (D // 4) ** -0.5, 0.4375, ((0, 32),), jnp.float32)
    dense_m = centred(seeds[10], (D, 4 * D), (2.0 * NPOS ** 0.5 / (POS_DEV * D ** 0.5)), 0.21875, ((1, 32),), jnp.float32)
    small_m = centred(seeds[11], (21, D), (2.0 * NPOS ** 0.5 / (POS_DEV * D ** 0.5)), 0.21875, ((1, 32),), jnp.float32)
    expin_m = centred(seeds[12], (2, D, EXPERTS * FF), (0.82 * NPOS ** 0.5 / (POS_DEV * FF ** 0.5)), 0.0546875, ((1, 4), (2, 8)), jnp.float32)
    expout_m = centred(seeds[13], (EXPERTS * FF, D), (0.0625 * NPOS ** 0.5 / (POS_DEV * D ** 0.5)), 0.0068359375, ((0, 32),), jnp.float32)
    table_m = centred(seeds[14], (VOCAB, D), (7.4 * NPOS ** 0.5 / (VOCAB * POS_DEV)), 0.00036621094, ((0, 32),), jnp.float32)
    dense_v = jnp.clip(jnp.exp(math.log(0.0052083335) - 1.3862944 * jax.random.uniform(seeds[15], (D, 4 * D), jnp.float32) ** block_scale(seeds[15], (D, 4 * D), ((1, 32),), -0.2, 0.2)), 0.0013020834, 0.0052083335)
    small_v = jnp.clip(jnp.exp(math.log(0.0052083335) - 1.3862944 * jax.random.uniform(seeds[16], (21, D), jnp.float32) ** block_scale(seeds[16], (21, D), ((1, 32),), -0.2, 0.2)), 0.0013020834, 0.0052083335)
    expin_v = jnp.clip(jnp.exp(math.log(0.00013061524) - 1.376992 * jax.random.uniform(seeds[17], (2, D, EXPERTS * FF), jnp.float32) ** block_scale(seeds[17], (2, D, EXPERTS * FF), ((1, 4), (2, 8)), -0.2, 0.2)), 3.295898568467237e-05, 0.00013061524)
    expout_v = jnp.clip(jnp.exp(math.log(1.302083364862483e-05) - 1.3862944 * jax.random.uniform(seeds[18], (EXPERTS * FF, D), jnp.float32) ** block_scale(seeds[18], (EXPERTS * FF, D), ((0, 32),), -0.2, 0.2)), 3.2552084121562075e-06, 1.302083364862483e-05)
    table_v = jnp.clip(jnp.exp(math.log(1.280568540096283e-08) - 1.3862944 * jax.random.uniform(seeds[19], (VOCAB, D), jnp.float32) ** block_scale(seeds[19], (VOCAB, D), ((0, 32),), -0.2, 0.2)), 3.2014213502407074e-09, 1.280568540096283e-08)
    return {"x_in": x_in, "seq_lens": seq_lens, "routes": routes, "positions": positions, "targets": targets, "dense_w": dense_w, "small_w": small_w, "expert_in": expert_in, "expert_out": expert_out, "table": table, "dense_m": dense_m, "small_m": small_m, "expin_m": expin_m, "expout_m": expout_m, "table_m": table_m, "dense_v": dense_v, "small_v": small_v, "expin_v": expin_v, "expout_v": expout_v, "table_v": table_v}


EPS = 1e-06
HIGH = lax.Precision.HIGHEST

@jax.custom_vjp
def low(v):
    return lax.optimization_barrier(v.astype(jnp.bfloat16)).astype(jnp.float32)

@jax.custom_vjp
def low_back(v):
    return v

def low_keep(v):
    return (low(v), None)

def low_pass(kept, grad):
    return (grad,)

def back_keep(v):
    return (v, None)

def back_low(kept, grad):
    return (low(grad),)
low.defvjp(low_keep, low_pass)
low_back.defvjp(back_keep, back_low)

def matmul(left, right):
    return jnp.dot(left, right, precision=HIGH)

def rms(hidden, gain):
    return hidden * lax.rsqrt(lax.optimization_barrier(jnp.mean(hidden * hidden, -1, keepdims=True)) + EPS) * gain

def block_loss(weights, block):
    dense, small, ein, eout, tab = weights
    hidden, lens, rts, pos, tgt = block
    factor = HDIM ** (-0.5)
    normed = low(rms(hidden, small[0]))
    qkv = low(low_back(matmul(normed, dense[:, :3 * D])))
    query = qkv[:, :D].reshape(TOK_DEV, HEADS, HDIM)
    keys = qkv[:, D:2 * D].reshape(TOK_DEV, HEADS, HDIM)
    values = qkv[:, 2 * D:].reshape(TOK_DEV, HEADS, HDIM)
    scores = low_back(jnp.einsum('qhd,khd->hqk', query, keys, precision=HIGH) * factor)
    place = jnp.arange(TOK_DEV, dtype=jnp.int32)
    ends = jnp.cumsum(lens)
    segment = lax.optimization_barrier(jnp.sum((place[:, None] >= ends[None, :]).astype(jnp.int32), 1))
    mask = (segment[:, None] == segment[None, :]) & (place[None, :] <= place[:, None])
    probs = low(jax.nn.softmax(jnp.where(mask[None], scores, -1e+30), -1))
    mixed = jnp.einsum('hqk,khd->qhd', probs, values, precision=HIGH).reshape(TOK_DEV, D)
    mixed = low(low_back(mixed))
    first = hidden + low_back(matmul(mixed, dense[:, 3 * D:]))
    second_in = rms(first, small[1])
    second_low = low(second_in)
    route_p = jax.nn.softmax(matmul(second_low, small[5:17].T), -1)
    used = lax.optimization_barrier(jnp.sum((rts[:, :, None] == jnp.arange(EXPERTS + NULLS, dtype=jnp.int32)[None, None, :]).astype(jnp.float32), 1))
    weight = route_p * used
    hits = lax.optimization_barrier(jnp.sum((rts[:, :, None] == jnp.arange(EXPERTS, dtype=jnp.int32)[None, None, :]).astype(jnp.int32), 1))
    rank = (jnp.cumsum(hits, 0) - hits).astype(jnp.int32)
    keep = (hits * (rank < CAP).astype(jnp.int32)).astype(jnp.float32)
    const_p = jax.nn.softmax(matmul(second_low, small[17:21].T).reshape(TOK_DEV, 2, 2), -1)
    moe = weight[:, EXPERTS + 1:EXPERTS + 2] * second_in
    for j in range(2):
        const_out = const_p[:, j, 0:1] * second_in + const_p[:, j, 1:2] * small[3 + j][None, :]
        moe = moe + weight[:, EXPERTS + 2 + j:EXPERTS + 3 + j] * const_out
    shards = N_DP // EXPERTS
    each = FF // shards
    ein_e = ein.reshape(2, D, EXPERTS, shards, each).transpose(2, 0, 1, 3, 4)
    eout_e = eout.reshape(EXPERTS, shards, each, D)

    def expert(carry, item):
        w_in, w_out, gate_w = item
        copies = low_back(jnp.broadcast_to(second_low, (shards, TOK_DEV, D)))
        gate_pre = low_back(jnp.einsum('std,dsf->stf', copies, w_in[0], precision=HIGH))
        up_pre = low_back(jnp.einsum('std,dsf->stf', copies, w_in[1], precision=HIGH))
        inner = low(jax.nn.silu(gate_pre) * up_pre)
        part = low(low_back(jnp.einsum('stf,sfd->std', inner, w_out, precision=HIGH)))
        return (carry + gate_w[:, None] * lax.optimization_barrier(jnp.sum(part, 0)), None)
    moe, _ = lax.scan(jax.checkpoint(expert), moe, (ein_e, eout_e, (weight[:, :EXPERTS] * keep).T))
    third = first + moe
    chosen = low(rms(third, small[2])[pos])
    logits = low_back(matmul(chosen, tab.T))
    lse = jax.nn.logsumexp(logits, -1)
    aimed = jnp.take_along_axis(logits, tgt[:, None], 1)[:, 0]
    return jnp.sum(lse - aimed) / POS_DEV

def moments(weight, first, second, grad):
    first = 0.5 * first + 0.5 * grad
    second = 0.5 * second + 0.5 * grad * grad
    corr = 1.0 - 0.5 ** STEP
    update = first / corr / (jnp.sqrt(second / corr) + EPS) + 0.01 * weight
    return (first, second, update)

def squares(arrays):
    dense, small, ein, eout, tab = arrays
    return jnp.stack([jnp.sum(dense[:, :3 * D] ** 2), jnp.sum(dense[:, 3 * D:] ** 2), jnp.sum(small[:5] ** 2), jnp.sum(small[5:] ** 2), jnp.sum(ein ** 2), jnp.sum(eout ** 2), jnp.sum(tab ** 2)])

def reference(x_in, seq_lens, routes, positions, targets, dense_w, small_w, expert_in, expert_out, table, dense_m, small_m, expin_m, expout_m, table_m, dense_v, small_v, expin_v, expout_v, table_v):
    blocks = (x_in.astype(jnp.float32).reshape(DEVICES, TOK_DEV, D), seq_lens, routes.reshape(DEVICES, TOK_DEV, TOP), positions.reshape(DEVICES, POS_DEV), targets.transpose(1, 0, 2).reshape(DEVICES, POS_DEV))

    def total(dense, small, ein, eout, tab):
        weights = (low(dense), low(small), low(ein), low(eout), low(tab))
        losses = lax.map(jax.checkpoint(lambda blk: block_loss(weights, blk)), blocks)
        return jnp.sum(losses)
    masters = (dense_w, small_w, expert_in, expert_out, table)
    loss, pull = jax.vjp(total, *masters)
    grads = pull(jnp.ones((), jnp.float32))
    firsts = (dense_m, small_m, expin_m, expout_m, table_m)
    seconds = (dense_v, small_v, expin_v, expout_v, table_v)
    results = [moments(w, m, v, g) for w, m, v, g in zip(masters, firsts, seconds, grads)]
    updates = tuple((r[2] for r in results))
    weight_norm = jnp.sqrt(squares(masters))
    update_norm = jnp.sqrt(squares(updates))
    trust = weight_norm / update_norm
    column = jnp.arange(4 * D, dtype=jnp.int32)
    dense_scale = jnp.where(column < 3 * D, trust[0], trust[1])[None, :]
    small_scale = jnp.where(jnp.arange(21, dtype=jnp.int32) < 5, trust[2], trust[3])[:, None]
    scales = (dense_scale, small_scale, trust[4], trust[5], trust[6])
    outs = [loss, jnp.stack([weight_norm, update_norm, trust])]
    for w, r, sc in zip(masters, results, scales):
        fresh = w - 0.2 * sc * r[2]
        outs += [r[0], r[1], fresh, fresh.astype(jnp.bfloat16)]
    return tuple(outs)
```

```python
import jax
import jax.numpy as jnp
from jax import lax
from jax.sharding import PartitionSpec as P

D = 768
HDIM = 64
EXPERTS = 8
NULLS = 4
STEP = 5
CAP = 96


EPS = 1e-06
HIGH = lax.Precision.HIGHEST
LOWER = jnp.bfloat16
WIDE = jnp.float32
BOTH = ("dp", "rep")
LANES = 128


def contract_rows(left, right):
    return lax.dot_general(left, right, (((0,), (0,)), ((), ())), preferred_element_type=WIDE)


def contract_cols(left, right):
    return lax.dot_general(left, right, (((1,), (1,)), ((), ())), preferred_element_type=WIDE)


def plain(left, right):
    return jnp.dot(left, right, preferred_element_type=WIDE)


def rows_high(left, right):
    return lax.dot_general(left, right, (((0,), (0,)), ((), ())), precision=HIGH)


def swap(value, axis):
    return lax.all_to_all(value, axis, split_axis=0, concat_axis=0, tiled=True)


def share(value, axis, count):
    return swap(jnp.broadcast_to(value[None], (count,) + value.shape), axis)


def halve(buffer, axis, mask, size):
    own = (lax.axis_index(axis) & mask) // mask
    halves = buffer.reshape((buffer.shape[0] // 2, 2) + buffer.shape[1:])
    keep = lax.dynamic_index_in_dim(halves, own, 1, keepdims=False)
    give = lax.dynamic_index_in_dim(halves, 1 - own, 1, keepdims=False).astype(LOWER)
    take = lax.ppermute(give, axis, [(i, i ^ mask) for i in range(size)])
    return keep + take.astype(WIDE)


def scatter_sum(blocks, n_dp, n_rep):
    value = blocks.swapaxes(0, 1)
    mask = 1
    while mask < n_rep:
        value = halve(value, "rep", mask, n_rep)
        mask *= 2
    value = value[0]
    mask = 1
    while mask < n_dp:
        value = halve(value, "dp", mask, n_dp)
        mask *= 2
    return value[0]


def norm_fwd(hidden, gain):
    scale = lax.rsqrt(jnp.mean(hidden * hidden, -1, keepdims=True) + EPS)
    return (hidden * scale * gain, scale)


def norm_back(hidden, scale, gain, grad_out):
    normed = hidden * scale
    grad_gain = jnp.sum(grad_out * normed, 0)
    inner = grad_out * gain
    grad_in = scale * (inner - normed * jnp.mean(inner * normed, -1, keepdims=True))
    return (grad_in, grad_gain)


def seq_mask(lens, tokens):
    place = jnp.arange(tokens, dtype=jnp.int32)
    count = lens.shape[0]
    ends = [jnp.sum(lens[: i + 1]) for i in range(count)]
    segment = sum((place >= end).astype(jnp.int32) for end in ends)
    return (segment[:, None] == segment[None, :]) & (place[None, :] <= place[:, None])


def split_heads(qkv, which):
    return qkv[:, which * D : (which + 1) * D].reshape(qkv.shape[0], -1, HDIM)


def head_scores(qkv, mask):
    scores = jnp.einsum(
        "qhd,khd->hqk", split_heads(qkv, 0), split_heads(qkv, 1), preferred_element_type=WIDE
    )
    return jnp.where(mask[None], scores * HDIM ** (-0.5), -1e30)


def fan_out(buffer, shards):
    return jnp.broadcast_to(buffer[:, None], (EXPERTS, shards) + buffer.shape[1:]).reshape(
        (EXPERTS * shards,) + buffer.shape[1:]
    )


def pick_slots(picks, received, shards):
    parts = received.reshape((EXPERTS, shards) + received.shape[1:])
    total = plain(picks, parts[:, 0].reshape(-1, D))
    for s in range(1, shards):
        total = total + plain(picks, parts[:, s].reshape(-1, D))
    return total


def layer_forward(hidden, lens, routes, dense_t, small_all, w_in, w_out, shards):
    gains, const_vec, router, const_gate = (
        small_all[:3].astype(WIDE),
        small_all[3:5].astype(WIDE),
        small_all[5:17],
        small_all[17:21],
    )
    tokens = hidden.shape[0]
    mask = seq_mask(lens, tokens)
    normed, scale_one = norm_fwd(hidden, gains[0])
    normed_low = normed.astype(LOWER)
    qkv = contract_cols(normed_low, dense_t[: 3 * D]).astype(LOWER)
    scores = head_scores(qkv, mask)
    top = jnp.max(scores, -1, keepdims=True)
    expo = jnp.exp(scores - top)
    total = jnp.sum(expo, -1, keepdims=True)
    probs = (expo / total).astype(LOWER)
    mixed = jnp.einsum("hqk,khd->qhd", probs, split_heads(qkv, 2), preferred_element_type=WIDE)
    mixed = mixed.reshape(tokens, D).astype(LOWER)
    first = hidden + contract_cols(mixed, dense_t[3 * D :])
    second, scale_two = norm_fwd(first, gains[1])
    second_low = second.astype(LOWER)
    route_p = jax.nn.softmax(contract_cols(second_low, router), -1)
    hits = routes[:, :, None] == jnp.arange(EXPERTS + NULLS, dtype=jnp.int32)[None, None, :]
    used = jnp.sum(hits.astype(WIDE), 1)
    weight = route_p * used
    earlier = jnp.tril(jnp.ones((tokens, tokens), LOWER), -1)
    rank = plain(earlier, used[:, :EXPERTS].astype(LOWER)).astype(jnp.int32)
    place = jnp.arange(EXPERTS, dtype=jnp.int32)[None] * CAP + rank
    place = jnp.where(rank < CAP, place, -1)
    real_hits = hits[:, :, :EXPERTS]
    slot = jnp.max(jnp.where(real_hits, place[:, None, :], -1), -1)
    w_slot = jnp.sum(jnp.where(real_hits, weight[:, None, :EXPERTS], 0.0), -1)
    all_slots = jnp.arange(EXPERTS * CAP, dtype=jnp.int32)
    picks = [(slot[:, k : k + 1] == all_slots[None]).astype(LOWER) for k in range(2)]
    kept = [(slot[:, k : k + 1] >= 0).astype(WIDE) for k in range(2)]
    both = picks[0] + picks[1]
    buffer = contract_rows(both, second_low).astype(LOWER).reshape(EXPERTS, CAP, D)
    rows = swap(fan_out(buffer, shards), "dp").reshape(-1, D)
    gate_pre = plain(rows, w_in[0])
    up_pre = plain(rows, w_in[1])
    inner = (jax.nn.silu(gate_pre) * up_pre).astype(LOWER)
    part = plain(inner, w_out).astype(LOWER)
    returned = swap(part.reshape(EXPERTS * shards, CAP, D), "dp")
    outs = [pick_slots(picks[k], returned, shards) for k in range(2)]
    moe = w_slot[:, 0:1] * outs[0] + w_slot[:, 1:2] * outs[1]
    const_p = jax.nn.softmax(contract_cols(second_low, const_gate).reshape(tokens, 2, 2), -1)
    const_out = const_p[:, :, 0:1] * second[:, None, :] + const_p[:, :, 1:2] * const_vec[None]
    moe = moe + weight[:, EXPERTS + 1 : EXPERTS + 2] * second
    moe = (
        moe
        + weight[:, EXPERTS + 2 : EXPERTS + 3] * const_out[:, 0]
        + weight[:, EXPERTS + 3 :] * const_out[:, 1]
    )
    third = first + moe
    saved = dict(
        gains=gains,
        const_vec=const_vec,
        router=router,
        const_gate=const_gate,
        mask=mask,
        scale_one=scale_one,
        normed_low=normed_low,
        qkv=qkv,
        lse=top + jnp.log(total),
        mixed=mixed,
        first=first,
        second=second,
        scale_two=scale_two,
        second_low=second_low,
        route_p=route_p,
        hits=hits,
        used=used,
        weight=weight,
        w_slot=w_slot,
        picks=picks,
        kept=kept,
        both=both,
        rows=rows,
        gate_pre=gate_pre,
        up_pre=up_pre,
        inner=inner,
        outs=outs,
        const_p=const_p,
        const_out=const_out,
    )
    return (third, saved)


def head_step(third, positions, targets, table_all, gain, own, n_dp):
    final, scale_three = norm_fwd(third, gain)
    tokens = third.shape[0]
    count = positions.shape[0]
    pick = positions[:, None] == jnp.arange(tokens, dtype=jnp.int32)[None, :]
    chosen = plain(pick.astype(LOWER), final.astype(LOWER)).astype(LOWER)
    gathered = share(chosen, "dp", n_dp).reshape(-1, D)
    logits = contract_cols(gathered, table_all)
    local_rows = table_all.shape[0]
    aim = targets.reshape(-1)[:, None] - own * local_rows
    hit = aim == jnp.arange(local_rows, dtype=jnp.int32)[None, :]
    top = jnp.max(logits, -1)
    total = jnp.sum(jnp.exp(logits - top[:, None]), -1)
    aimed = jnp.sum(jnp.where(hit, logits, 0.0), -1)
    stats = jnp.stack([top, total, aimed]).reshape(-1, LANES)
    stats = share(stats, "dp", n_dp).reshape(n_dp, 3, -1)
    high = jnp.max(stats[:, 0], 0)
    sums = jnp.sum(stats[:, 1] * jnp.exp(stats[:, 0] - high[None]), 0)
    lse = high + jnp.log(sums)
    loss_rows = lse - jnp.sum(stats[:, 2], 0)
    loss_part = jnp.sum(lax.dynamic_slice_in_dim(loss_rows, own * count, count)) / count
    grad_logits = ((jnp.exp(logits - lse[:, None]) - hit.astype(WIDE)) / count).astype(LOWER)
    grad_rows = plain(grad_logits, table_all).astype(LOWER).reshape(n_dp, count, D)
    grad_chosen = jnp.sum(swap(grad_rows, "dp").astype(WIDE), 0)
    grad_table = contract_rows(grad_logits, gathered).astype(LOWER)
    grad_final = rows_high(pick.astype(WIDE), grad_chosen)
    grad_third, grad_gain = norm_back(third, scale_three, gain, grad_final)
    return (loss_part, grad_third, grad_gain, grad_table)


def layer_backward(hidden, grad_third, saved, dense_t, w_in, w_out, shards):
    gains, const_vec = saved["gains"], saved["const_vec"]
    router, const_gate = saved["router"], saved["const_gate"]
    tokens = hidden.shape[0]
    weight = saved["weight"]
    route_p = saved["route_p"]
    second_wide = saved["second_low"].astype(WIDE)
    w_slot, picks = saved["w_slot"], saved["picks"]
    grad_out = contract_rows(picks[0], (w_slot[:, 0:1] * grad_third).astype(LOWER))
    grad_out = grad_out + contract_rows(picks[1], (w_slot[:, 1:2] * grad_third).astype(LOWER))
    grad_out = grad_out.astype(LOWER).reshape(EXPERTS, CAP, D)
    grad_part = swap(fan_out(grad_out, shards), "dp").reshape(-1, D)
    gate_pre, up_pre = (saved["gate_pre"], saved["up_pre"])
    grad_inner = contract_cols(grad_part, w_out)
    sig = jax.nn.sigmoid(gate_pre)
    grad_gate = (grad_inner * up_pre * sig * (1.0 + gate_pre * (1.0 - sig))).astype(LOWER)
    grad_up = (grad_inner * gate_pre * sig).astype(LOWER)
    grad_rows = (contract_cols(grad_gate, w_in[0]) + contract_cols(grad_up, w_in[1])).astype(LOWER)
    came_back = swap(grad_rows.reshape(EXPERTS * shards, CAP, D), "dp")
    grad_w_out = contract_rows(saved["inner"], grad_part).astype(LOWER)
    grad_w_in = jnp.stack(
        [
            contract_rows(saved["rows"], grad_gate).astype(LOWER),
            contract_rows(saved["rows"], grad_up).astype(LOWER),
        ]
    )
    dots = [jnp.sum(saved["outs"][k] * grad_third, -1, keepdims=True) for k in range(2)]
    hits = saved["hits"].astype(WIDE)
    grad_real = (dots[0] * hits[:, 0] + dots[1] * hits[:, 1])[:, :EXPERTS]
    grad_copy = jnp.sum(grad_third * saved["second"], -1, keepdims=True)
    grad_const = jnp.sum(grad_third[:, None, :] * saved["const_out"], -1)
    grad_weight = jnp.concatenate(
        [grad_real, jnp.zeros((tokens, 1), WIDE), grad_copy, grad_const], 1
    )
    grad_p = grad_weight * saved["used"]
    grad_logit = route_p * (grad_p - jnp.sum(route_p * grad_p, -1, keepdims=True))
    const_p = saved["const_p"]
    w_const = weight[:, EXPERTS + 2 :]
    along_vec = jnp.dot(grad_third, const_vec.T, precision=HIGH)
    grad_alpha = w_const[:, :, None] * jnp.stack(
        [jnp.broadcast_to(grad_copy, along_vec.shape), along_vec], -1
    )
    grad_clog = (const_p * (grad_alpha - jnp.sum(const_p * grad_alpha, -1, keepdims=True))).reshape(
        tokens, 4
    )
    grad_cvec = rows_high(w_const * const_p[:, :, 1], grad_third)
    logit_all = jnp.concatenate([grad_logit, grad_clog], 1)
    grad_gates = rows_high(logit_all, second_wide)
    gates_all = jnp.concatenate([router, const_gate], 0).astype(WIDE)
    grad_second = jnp.dot(logit_all, gates_all, precision=HIGH)
    carry = weight[:, EXPERTS + 1 : EXPERTS + 2] + jnp.sum(
        w_const * const_p[:, :, 0], -1, keepdims=True
    )
    grad_second = grad_second + carry * grad_third
    grad_second = grad_second + pick_slots(saved["both"], came_back, shards)
    grad_first_norm, grad_gain_two = norm_back(
        saved["first"], saved["scale_two"], gains[1], grad_second
    )
    grad_first = grad_third + grad_first_norm
    grad_attn = grad_first.astype(LOWER)
    grad_wo = contract_rows(grad_attn, saved["mixed"])
    grad_mixed = plain(grad_attn, dense_t[3 * D :]).astype(LOWER).reshape(tokens, -1, HDIM)
    qkv = saved["qkv"]
    probs = jnp.exp(head_scores(qkv, saved["mask"]) - saved["lse"])
    grad_values = jnp.einsum(
        "hqk,qhd->khd", probs.astype(LOWER), grad_mixed, preferred_element_type=WIDE
    )
    grad_probs = jnp.einsum(
        "qhd,khd->hqk", grad_mixed, split_heads(qkv, 2), preferred_element_type=WIDE
    )
    grad_scores = (probs * (grad_probs - jnp.sum(probs * grad_probs, -1, keepdims=True))).astype(
        LOWER
    )
    grad_query = jnp.einsum(
        "hqk,khd->qhd", grad_scores, split_heads(qkv, 1), preferred_element_type=WIDE
    ) * HDIM ** (-0.5)
    grad_keys = jnp.einsum(
        "hqk,qhd->khd", grad_scores, split_heads(qkv, 0), preferred_element_type=WIDE
    ) * HDIM ** (-0.5)
    grad_qkv = jnp.concatenate(
        [
            grad_query.reshape(tokens, D),
            grad_keys.reshape(tokens, D),
            grad_values.reshape(tokens, D),
        ],
        1,
    ).astype(LOWER)
    grad_wqkv = contract_rows(grad_qkv, saved["normed_low"])
    grad_normed = plain(grad_qkv, dense_t[: 3 * D])
    unused, grad_gain_one = norm_back(hidden, saved["scale_one"], gains[0], grad_normed)
    dense_grad = jnp.concatenate([grad_wqkv, grad_wo], 0)
    return (dense_grad, grad_gain_one, grad_gain_two, grad_cvec, grad_gates, grad_w_in, grad_w_out)


def group_squares(arrays, device):
    dense, small, ein, eout, tab = arrays
    width = dense.shape[1]
    front = (device * width + jnp.arange(width, dtype=jnp.int32) < 3 * D).astype(WIDE)
    dense_sq = jnp.sum(dense * dense, 0)
    return jnp.stack(
        [
            jnp.sum(dense_sq * front),
            jnp.sum(dense_sq * (1.0 - front)),
            jnp.sum(small[:5] * small[:5]),
            jnp.sum(small[5:] * small[5:]),
            jnp.sum(ein * ein),
            jnp.sum(eout * eout),
            jnp.sum(tab * tab),
        ]
    )


def moments(weight, first, second, grad):
    first = 0.5 * first + 0.5 * grad
    second = 0.5 * second + 0.5 * grad * grad
    corr = 1.0 - 0.5**STEP
    update = first / corr / (jnp.sqrt(second / corr) + EPS) + 0.01 * weight
    return (first, second, update)


def local(
    x_in,
    seq_lens,
    routes,
    positions,
    targets,
    dense_w,
    small_w,
    expert_in,
    expert_out,
    table,
    dense_m,
    small_m,
    expin_m,
    expout_m,
    table_m,
    dense_v,
    small_v,
    expin_v,
    expout_v,
    table_v,
):
    n_dp, n_rep = lax.axis_size("dp"), lax.axis_size("rep")
    devices = n_dp * n_rep
    shards = n_dp // EXPERTS
    own = lax.axis_index("dp")
    device = own * n_rep + lax.axis_index("rep")
    masters = (dense_w, small_w, expert_in, expert_out, table)
    width, thin = dense_w.shape[1], small_w.shape[1]
    dense_t = lax.all_gather(dense_w.T.astype(LOWER), BOTH, axis=0, tiled=True)
    small_t = jnp.pad(small_w.T.astype(LOWER), ((0, 0), (0, LANES - small_w.shape[0])))
    small_all = share(small_t, BOTH, devices).reshape(-1, LANES).T
    w_in, w_out, table_all = (
        lax.all_gather(expert_in.astype(LOWER), "rep", axis=1, tiled=True),
        lax.all_gather(expert_out.astype(LOWER), "rep", axis=0, tiled=True),
        lax.all_gather(table.astype(LOWER), "rep", axis=0, tiled=True),
    )
    hidden = x_in.astype(WIDE)
    third, saved = layer_forward(
        hidden, seq_lens[0], routes, dense_t, small_all, w_in, w_out, shards
    )
    loss_part, grad_third, grad_gain_final, grad_table = head_step(
        third, positions, targets, table_all, saved["gains"][2], own, n_dp
    )
    table_g = lax.psum_scatter(grad_table, "rep", scatter_dimension=0, tiled=True)
    dense_grad, gain_one, gain_two, grad_cvec, grad_gates, grad_w_in, grad_w_out = layer_backward(
        hidden, grad_third, saved, dense_t, w_in, w_out, shards
    )
    ein_g, eout_g = (
        lax.psum_scatter(grad_w_in, "rep", scatter_dimension=1, tiled=True),
        lax.psum_scatter(grad_w_out, "rep", scatter_dimension=0, tiled=True),
    )
    small_grad = jnp.concatenate(
        [gain_one[None], gain_two[None], grad_gain_final[None], grad_cvec, grad_gates], 0
    )
    small_blocks = small_grad.reshape(-1, devices, thin).swapaxes(0, 1).reshape(devices, -1)
    extra = -(-small_blocks.shape[1] // (8 * D)) * 8 * D
    small_blocks = jnp.pad(small_blocks, ((0, 0), (0, extra - small_blocks.shape[1])))
    blocks = jnp.concatenate(
        [dense_grad.reshape(devices, width, D), small_blocks.reshape(devices, -1, D)], 1
    )
    block = scatter_sum(blocks.reshape((n_dp, n_rep) + blocks.shape[1:]), n_dp, n_rep)
    dense_g = block[:width].T
    small_g = block[width:].reshape(-1)[: small_w.size].reshape(small_w.shape)
    grads = (dense_g, small_g, ein_g.astype(WIDE), eout_g.astype(WIDE), table_g.astype(WIDE))
    firsts = (dense_m, small_m, expin_m, expout_m, table_m)
    seconds = (dense_v, small_v, expin_v, expout_v, table_v)
    results = [moments(w, m, v, g) for w, m, v, g in zip(masters, firsts, seconds, grads)]
    update_parts = group_squares(tuple((r[2] for r in results)), device)
    parts = jnp.concatenate([group_squares(masters, device), update_parts, loss_part[None]])
    parts = jnp.pad(parts, (0, 8 * LANES - parts.shape[0])).reshape(8, LANES)
    sums = jnp.sum(share(parts, BOTH, devices), 0).reshape(-1)
    loss = sums[14]
    weight_norm = jnp.sqrt(sums[:7])
    update_norm = jnp.sqrt(sums[7:14])
    trust = weight_norm / update_norm
    column = device * width + jnp.arange(width, dtype=jnp.int32)
    dense_scale = jnp.where(column < 3 * D, trust[0], trust[1])[None, :]
    small_scale = jnp.where(jnp.arange(21, dtype=jnp.int32) < 5, trust[2], trust[3])[:, None]
    scales = (dense_scale, small_scale, trust[4], trust[5], trust[6])
    outs = [loss, jnp.stack([weight_norm, update_norm, trust])]
    for w, r, factor in zip(masters, results, scales):
        fresh = w - 0.2 * factor * r[2]
        outs += [r[0], r[1], fresh, fresh.astype(LOWER)]
    return tuple(outs)


def solution(mesh):
    in_specs = (
        P(("dp", "rep"), None),
        P(("dp", "rep"), None),
        P(("dp", "rep"), None),
        P(("dp", "rep")),
        P("rep", None, None),
        P(None, ("dp", "rep")),
        P(None, ("dp", "rep")),
        P(None, "rep", "dp"),
        P(("dp", "rep"), None),
        P(("dp", "rep"), None),
        P(None, ("dp", "rep")),
        P(None, ("dp", "rep")),
        P(None, "rep", "dp"),
        P(("dp", "rep"), None),
        P(("dp", "rep"), None),
        P(None, ("dp", "rep")),
        P(None, ("dp", "rep")),
        P(None, "rep", "dp"),
        P(("dp", "rep"), None),
        P(("dp", "rep"), None),
    )
    out_specs = (
        P(),
        P(),
        P(None, ("dp", "rep")),
        P(None, ("dp", "rep")),
        P(None, ("dp", "rep")),
        P(None, ("dp", "rep")),
        P(None, ("dp", "rep")),
        P(None, ("dp", "rep")),
        P(None, ("dp", "rep")),
        P(None, ("dp", "rep")),
        P(None, "rep", "dp"),
        P(None, "rep", "dp"),
        P(None, "rep", "dp"),
        P(None, "rep", "dp"),
        P(("dp", "rep"), None),
        P(("dp", "rep"), None),
        P(("dp", "rep"), None),
        P(("dp", "rep"), None),
        P(("dp", "rep"), None),
        P(("dp", "rep"), None),
        P(("dp", "rep"), None),
        P(("dp", "rep"), None),
    )
    return jax.shard_map(local, mesh=mesh, in_specs=in_specs, out_specs=out_specs, check_vma=False)
```

```python
import functools

import jax
import jax.numpy as jnp
from jax import lax
from jax.experimental import pallas as pl
from jax.experimental.pallas import tpu as pltpu
from jax.sharding import PartitionSpec as P

D = 768
HDIM = 64
EXPERTS = 8
NULLS = 4
STEP = 5
CAP = 96


EPS = 1e-06
HIGH = lax.Precision.HIGHEST
LOWER = jnp.bfloat16
WIDE = jnp.float32
BOTH = ("dp", "rep")
LANES = 128
MOST_FLIPS = 8
ROWS = 256
VMEM_BYTES = 48 << 20


def contract_rows(left, right):
    return lax.dot_general(left, right, (((0,), (0,)), ((), ())), preferred_element_type=WIDE)


def contract_cols(left, right):
    return lax.dot_general(left, right, (((1,), (1,)), ((), ())), preferred_element_type=WIDE)


def plain(left, right):
    return jnp.dot(left, right, preferred_element_type=WIDE)


def rows_high(left, right):
    return lax.dot_general(left, right, (((0,), (0,)), ((), ())), precision=HIGH)


def swap(value, axis):
    return lax.all_to_all(value, axis, split_axis=0, concat_axis=0, tiled=True)


def share(value, axis, count):
    return swap(jnp.broadcast_to(value[None], (count,) + value.shape), axis)


def flip(value, axis, mask, size):
    return lax.ppermute(value, axis, [(i, i ^ mask) for i in range(size)])


def by_distance(value, own):
    shape = value.shape
    mask = 1
    while mask < shape[0]:
        pairs = value.reshape((shape[0] // (2 * mask), 2, mask) + shape[1:])
        value = jnp.where((own & mask) != 0, jnp.flip(pairs, 1), pairs).reshape(shape)
        mask *= 2
    return value


def trade(blocks, n_dp):
    if n_dp > MOST_FLIPS:
        own = lax.axis_index("dp")
        return list(by_distance(swap(by_distance(jnp.stack(blocks), own), "dp"), own))
    half = n_dp // 2
    far = [flip(blocks[m], "dp", m, n_dp) for m in range(half, n_dp)]
    return blocks[:1] + [flip(blocks[m], "dp", m, n_dp) for m in range(1, half)] + far


def gather_flips(block, n_dp):
    half = n_dp // 2
    if n_dp > MOST_FLIPS:
        pieces = list(by_distance(lax.all_gather(block, "dp"), lax.axis_index("dp")))
        return pieces[:half], pieces[half:]
    cross = flip(block, "dp", half, n_dp)
    near = [block] + [flip(block, "dp", m, n_dp) for m in range(1, half)]
    far = [cross] + [flip(cross, "dp", m, n_dp) for m in range(1, half)]
    return near, far


def sum_flips(parts, n_dp):
    half = n_dp // 2
    if n_dp > MOST_FLIPS:
        pieces = by_distance(jnp.stack(parts).astype(LOWER), lax.axis_index("dp"))
        return jnp.sum(swap(pieces, "dp").astype(WIDE), 0)
    aims = [flip(parts[half + m].astype(LOWER), "dp", m, n_dp) for m in range(1, half)]
    across = sum([a.astype(WIDE) for a in aims], parts[half].astype(WIDE)).astype(LOWER)
    cross = flip(across, "dp", half, n_dp)
    near = [flip(parts[m].astype(LOWER), "dp", m, n_dp) for m in range(1, half)]
    total = sum([a.astype(WIDE) for a in near], parts[0].astype(WIDE))
    return total + cross.astype(WIDE)


def halve(buffer, axis, mask, size):
    own = (lax.axis_index(axis) & mask) // mask
    halves = buffer.reshape((buffer.shape[0] // 2, 2) + buffer.shape[1:])
    keep = lax.dynamic_index_in_dim(halves, own, 1, keepdims=False)
    give = lax.dynamic_index_in_dim(halves, 1 - own, 1, keepdims=False).astype(LOWER)
    take = lax.ppermute(give, axis, [(i, i ^ mask) for i in range(size)])
    return keep + take.astype(WIDE)


def scatter_sum(blocks, n_dp, n_rep):
    value = blocks.swapaxes(0, 1)
    mask = 1
    while mask < n_rep:
        value = halve(value, "rep", mask, n_rep)
        mask *= 2
    value = value[0]
    mask = 1
    while mask < n_dp:
        value = halve(value, "dp", mask, n_dp)
        mask *= 2
    return value[0]


def pack_body(dense_ref, small_ref, out_ref):
    width = dense_ref.shape[1]
    rows, thin = small_ref.shape
    out_ref[:width, :] = dense_ref[...].T.astype(LOWER)
    out_ref[width:, :] = jnp.zeros((8, D), LOWER)
    turned = small_ref[...].T.astype(LOWER)
    for g in range(thin // 8):
        out_ref[width:, g * LANES : g * LANES + rows] = turned[g * 8 : g * 8 + 8, :]


def pack(dense_w, small_w):
    return pl.pallas_call(
        pack_body,
        out_shape=jax.ShapeDtypeStruct((dense_w.shape[1] + 8, D), LOWER),
        compiler_params=pltpu.CompilerParams(vmem_limit_bytes=VMEM_BYTES),
        name="pack",
    )(dense_w, small_w)


def assemble_body(place_ref, *refs, n_dp, width, thin):
    pieces = refs[: 2 * n_dp]
    dense_ref, small_ref, raw_ref, turned_ref, dense_sem, small_sem = refs[2 * n_dp :]
    own, rep = place_ref[0], place_ref[1]
    copies = []
    for m in range(n_dp):
        for pair in range(2):
            for core in range(2):
                piece = pieces[core * n_dp + m]
                device = (own ^ m) * 4 + (rep ^ (2 * pair + core))
                top = pair * (width + 8)
                number = m * 4 + pair * 2 + core
                copies.append(
                    pltpu.make_async_copy(
                        piece.at[pl.ds(top + width, 8), :],
                        raw_ref.at[device],
                        small_sem.at[number],
                    )
                )
                copies.append(
                    pltpu.make_async_copy(
                        piece.at[pl.ds(top, width), :],
                        dense_ref.at[device],
                        dense_sem.at[number],
                    )
                )
    for copy in copies:
        copy.start()
    for copy in copies[::2]:
        copy.wait()
    for device in range(4 * n_dp):
        for g in range(thin // 8):
            start = device * thin + g * 8
            tile = raw_ref[device, :, g * LANES : (g + 1) * LANES]
            turned_ref[start : start + 8, :] = tile.astype(WIDE)
    small_ref[...] = turned_ref[...].T[: small_ref.shape[0], :]
    for copy in copies[1::2]:
        copy.wait()


def assemble(pieces, place, n_dp, width, thin):
    return pl.pallas_call(
        functools.partial(assemble_body, n_dp=n_dp, width=width, thin=thin),
        in_specs=[pl.BlockSpec(memory_space=pltpu.SMEM)]
        + [pl.BlockSpec(memory_space=pl.ANY)] * len(pieces),
        out_specs=[
            pl.BlockSpec(memory_space=pl.ANY),
            pl.BlockSpec(memory_space=pltpu.VMEM),
        ],
        out_shape=[
            jax.ShapeDtypeStruct((4 * n_dp, width, D), LOWER),
            jax.ShapeDtypeStruct((24, D), WIDE),
        ],
        scratch_shapes=[
            pltpu.VMEM((4 * n_dp, 8, D), LOWER),
            pltpu.VMEM((4 * n_dp * thin, LANES), WIDE),
            pltpu.SemaphoreType.DMA((4 * n_dp,)),
            pltpu.SemaphoreType.DMA((4 * n_dp,)),
        ],
        compiler_params=pltpu.CompilerParams(vmem_limit_bytes=VMEM_BYTES),
        name="assemble",
    )(place, *pieces)


def gather_weights(dense_w, small_w, place, n_dp):
    width, thin = dense_w.shape[1], small_w.shape[1]
    block = pack(dense_w, small_w)
    both = jnp.concatenate([block, flip(block, "rep", 2, 4)])
    near, far = gather_flips(both, n_dp)
    mine = near + far
    theirs = [flip(piece, "rep", 1, 4) for piece in mine]
    dense, small = assemble(mine + theirs, place, n_dp, width, thin)
    return dense.reshape(-1, D), small


def dense_grad_body(
    place_ref, qkv_ref, attn_ref, normed_ref, mixed_ref, small_ref, mine_ref, other_ref, sum_ref
):
    j = pl.program_id(0)
    width, thin = mine_ref.shape[2] - 8, small_ref.shape[0] // (4 * pl.num_programs(0))
    front = 3 * D // (4 * width)

    @pl.when(j < front)
    def _():
        sum_ref[...] = contract_rows(qkv_ref[...], normed_ref[...])

    @pl.when(j >= front)
    def _():
        sum_ref[...] = contract_rows(attn_ref[...], mixed_ref[...])

    rep = place_ref[1]
    for pair in range(2):
        for core, out_ref in enumerate((mine_ref, other_ref)):
            r = rep ^ (2 * pair + core)
            rows = pl.multiple_of(r * width, 8)
            out_ref[0, pair, :width, :] = sum_ref[pl.ds(rows, width), :].astype(out_ref.dtype)
            out_ref[0, pair, width:, :] = jnp.zeros((8, D), out_ref.dtype)
            for g in range(thin // 8):
                start = pl.multiple_of((j * 4 + r) * thin + g * 8, 8)
                tile = small_ref[pl.ds(start, 8), :].astype(out_ref.dtype)
                out_ref[0, pair, width:, g * LANES : (g + 1) * LANES] = tile


def dense_grads(place, grad_qkv, grad_attn, normed, mixed, small_turned, n_dp, width):
    tokens = grad_qkv.shape[0]
    wide = 4 * width
    front = 3 * D // wide
    block = (1, 2, width + 8, D)
    whole = lambda shape: pl.BlockSpec(shape, lambda j, place: (0, 0))
    out_spec = pl.BlockSpec(block, lambda j, place: (j ^ place[0], 0, 0, 0))
    return pl.pallas_call(
        dense_grad_body,
        grid_spec=pltpu.PrefetchScalarGridSpec(
            num_scalar_prefetch=1,
            grid=(n_dp,),
            in_specs=[
                pl.BlockSpec((tokens, wide), lambda j, place: (0, jnp.minimum(j, front - 1))),
                pl.BlockSpec((tokens, wide), lambda j, place: (0, jnp.maximum(j - front, 0))),
                whole((tokens, D)),
                whole((tokens, D)),
                whole(small_turned.shape),
            ],
            out_specs=[out_spec, out_spec],
            scratch_shapes=[pltpu.VMEM((wide, D), WIDE)],
        ),
        out_shape=[
            jax.ShapeDtypeStruct((n_dp,) + block[1:], WIDE),
            jax.ShapeDtypeStruct((n_dp,) + block[1:], LOWER),
        ],
        compiler_params=pltpu.CompilerParams(vmem_limit_bytes=VMEM_BYTES),
        name="dense_grads",
    )(place, grad_qkv, grad_attn, normed, mixed, small_turned)


def sum_weights(mine, other, n_dp):
    both = mine + flip(other, "rep", 1, 4).astype(WIDE)
    pair = sum_flips([both[m] for m in range(n_dp)], n_dp)
    return pair[0] + flip(pair[1].astype(LOWER), "rep", 2, 4).astype(WIDE)


def norm_fwd(hidden, gain):
    scale = lax.rsqrt(jnp.mean(hidden * hidden, -1, keepdims=True) + EPS)
    return (hidden * scale * gain, scale)


def norm_back(hidden, scale, gain, grad_out):
    normed = hidden * scale
    grad_gain = jnp.sum(grad_out * normed, 0)
    inner = grad_out * gain
    grad_in = scale * (inner - normed * jnp.mean(inner * normed, -1, keepdims=True))
    return (grad_in, grad_gain)


def segments(lens, tokens):
    place = jnp.arange(tokens, dtype=jnp.int32)
    ends = [jnp.sum(lens[: i + 1]) for i in range(lens.shape[0])]
    return sum((place >= end).astype(jnp.int32) for end in ends)


def build_bias(bias_ref, key_dim):
    shape = bias_ref.shape
    query = lax.broadcasted_iota(jnp.int32, shape, 1 - key_dim)
    key = lax.broadcasted_iota(jnp.int32, shape, key_dim)
    return key <= query


def lane_masks():
    lane = lax.broadcasted_iota(jnp.int32, (1, 2 * HDIM), 1)
    low = (lane < HDIM).astype(WIDE)
    return (low.astype(LOWER), (1.0 - low).astype(LOWER))


def attend_body(seg_col, seg_row, q_ref, k_ref, v_ref, out_ref, bias_ref):
    tokens = q_ref.shape[0]

    @pl.when(pl.program_id(0) == 0)
    def _():
        counts = build_bias(bias_ref, 1) & (seg_col[...] == seg_row[...])
        bias_ref[...] = jnp.where(counts, 0.0, -1e30)

    masks = lane_masks()
    for start in range(0, tokens, ROWS):
        keys = start + ROWS
        k = k_ref[:keys, :]
        v = v_ref[:keys, :]
        q = q_ref[start : start + ROWS, :]
        acc = jnp.zeros((ROWS, 2 * HDIM), WIDE)
        for mine in masks:
            scores = contract_cols(q * mine, k) * HDIM ** (-0.5)
            scores = scores + bias_ref[start : start + ROWS, :keys]
            expo = jnp.exp(scores - jnp.max(scores, -1, keepdims=True))
            total = jnp.sum(expo, -1, keepdims=True)
            probs = (expo * (1.0 / total)).astype(LOWER)
            acc = acc + plain(probs, v * mine)
        out_ref[start : start + ROWS, :] = acc.astype(LOWER)


def head_specs(tokens, first):
    return [
        pl.BlockSpec((tokens, 2 * HDIM), lambda j, base=base: (0, base + j)) for base in first
    ]


def attend(qkv, segment):
    tokens = qkv.shape[0]
    pairs = D // (2 * HDIM)
    return pl.pallas_call(
        attend_body,
        grid=(pairs,),
        in_specs=[
            pl.BlockSpec((tokens, 1), lambda j: (0, 0)),
            pl.BlockSpec((1, tokens), lambda j: (0, 0)),
        ]
        + head_specs(tokens, (0, pairs, 2 * pairs)),
        out_specs=pl.BlockSpec((tokens, 2 * HDIM), lambda j: (0, j)),
        out_shape=jax.ShapeDtypeStruct((tokens, D), LOWER),
        scratch_shapes=[pltpu.VMEM((tokens, tokens), WIDE)],
        compiler_params=pltpu.CompilerParams(vmem_limit_bytes=VMEM_BYTES),
        name="attend",
    )(segment[:, None], segment[None, :], qkv, qkv, qkv)


def attend_back_body(seg_col, seg_row, q_ref, k_ref, v_ref, do_ref, out_ref, bias_ref):
    tokens = q_ref.shape[0]
    step = pl.program_id(0)

    @pl.when(step == 0)
    def _():
        counts = build_bias(bias_ref, 0) & (seg_col[...] == seg_row[...])
        bias_ref[...] = jnp.where(counts, 0.0, -1e30)

    masks = lane_masks()
    scale = HDIM ** (-0.5)
    grad_k = [jnp.zeros((ROWS, 2 * HDIM), WIDE) for _ in range(tokens // ROWS)]
    grad_v = [jnp.zeros((ROWS, 2 * HDIM), WIDE) for _ in range(tokens // ROWS)]
    col = pl.multiple_of(step * 2 * HDIM, 2 * HDIM)
    for block, start in enumerate(range(0, tokens, ROWS)):
        keys = start + ROWS
        k = k_ref[:keys, :]
        v = v_ref[:keys, :]
        q = q_ref[start : start + ROWS, :]
        do = do_ref[start : start + ROWS, :]
        grad_q = jnp.zeros((ROWS, 2 * HDIM), WIDE)
        for mine in masks:
            q_own = q * mine
            do_own = do * mine
            scores = contract_cols(k, q_own) * scale + bias_ref[:keys, start : start + ROWS]
            expo = jnp.exp(scores - jnp.max(scores, 0, keepdims=True))
            total = jnp.sum(expo, 0, keepdims=True)
            probs = expo * (1.0 / total)
            grad_p = contract_cols(v, do_own)
            inner = jnp.sum(probs * grad_p, 0, keepdims=True)
            grad_s = (probs * (grad_p - inner)).astype(LOWER)
            grad_q = grad_q + contract_rows(grad_s, k * mine)
            into_v = plain(probs.astype(LOWER), do_own)
            into_k = plain(grad_s, q_own)
            for b in range(block + 1):
                grad_v[b] = grad_v[b] + into_v[b * ROWS : (b + 1) * ROWS]
                grad_k[b] = grad_k[b] + into_k[b * ROWS : (b + 1) * ROWS]
        out_ref[start : start + ROWS, pl.ds(col, 2 * HDIM)] = (grad_q * scale).astype(LOWER)
    for b in range(tokens // ROWS):
        rows = slice(b * ROWS, (b + 1) * ROWS)
        out_ref[rows, pl.ds(D + col, 2 * HDIM)] = (grad_k[b] * scale).astype(LOWER)
        out_ref[rows, pl.ds(2 * D + col, 2 * HDIM)] = grad_v[b].astype(LOWER)


def attend_back(qkv, grad_mixed, segment):
    tokens = qkv.shape[0]
    pairs = D // (2 * HDIM)
    return pl.pallas_call(
        attend_back_body,
        grid=(pairs,),
        in_specs=[
            pl.BlockSpec((tokens, 1), lambda j: (0, 0)),
            pl.BlockSpec((1, tokens), lambda j: (0, 0)),
        ]
        + head_specs(tokens, (0, pairs, 2 * pairs))
        + head_specs(tokens, (0,)),
        out_specs=pl.BlockSpec((tokens, 3 * D), lambda j: (0, 0)),
        out_shape=jax.ShapeDtypeStruct((tokens, 3 * D), LOWER),
        scratch_shapes=[pltpu.VMEM((tokens, tokens), WIDE)],
        compiler_params=pltpu.CompilerParams(vmem_limit_bytes=VMEM_BYTES),
        name="attend_back",
    )(segment[:, None], segment[None, :], qkv, qkv, qkv, grad_mixed)


def experts_forward(rows, w_in, w_out):
    gate_pre = plain(rows, w_in[0])
    up_pre = plain(rows, w_in[1])
    inner = (jax.nn.silu(gate_pre) * up_pre).astype(LOWER)
    part = plain(inner, w_out).astype(LOWER)
    return gate_pre, up_pre, inner, part


def experts_backward(grad_part, gate_pre, up_pre, w_in, w_out):
    grad_inner = contract_cols(grad_part, w_out)
    sig = jax.nn.sigmoid(gate_pre)
    grad_gate = (grad_inner * up_pre * sig * (1.0 + gate_pre * (1.0 - sig))).astype(LOWER)
    grad_up = (grad_inner * gate_pre * sig).astype(LOWER)
    grad_rows = (contract_cols(grad_gate, w_in[0]) + contract_cols(grad_up, w_in[1])).astype(LOWER)
    return grad_gate, grad_up, grad_rows


def cut(value, count):
    size = value.shape[0] // count
    return [value[i * size : (i + 1) * size] for i in range(count)]


def send_slots(buffer, n_dp, shards):
    half = n_dp // 2
    blocks = trade([b for b in cut(buffer, EXPERTS) for _ in range(shards)], n_dp)
    return jnp.concatenate(blocks[:half]), jnp.concatenate(blocks[half:])


def return_slots(near, far, n_dp, shards):
    half = n_dp // 2
    blocks = trade(cut(near, half) + cut(far, half), n_dp)
    return [jnp.concatenate(blocks[s::shards]) for s in range(shards)]


def pick_slots(picks, received):
    return sum(plain(picks, part) for part in received)


def layer_forward(hidden, lens, routes, dense_t, small_all, w_in, w_out, own, n_dp):
    shards = n_dp // EXPERTS
    gains, const_vec, router, const_gate = (
        small_all[:3].astype(WIDE),
        small_all[3:5].astype(WIDE),
        small_all[5:17].astype(LOWER),
        small_all[17:21].astype(LOWER),
    )
    tokens = hidden.shape[0]
    segment = segments(lens, tokens)
    normed, scale_one = norm_fwd(hidden, gains[0])
    normed_low = normed.astype(LOWER)
    qkv = contract_cols(normed_low, dense_t[: 3 * D]).astype(LOWER)
    mixed = attend(qkv, segment)
    first = hidden + contract_cols(mixed, dense_t[3 * D :])
    second, scale_two = norm_fwd(first, gains[1])
    second_low = second.astype(LOWER)
    route_p = jax.nn.softmax(contract_cols(second_low, router), -1)
    hits = routes[:, :, None] == jnp.arange(EXPERTS + NULLS, dtype=jnp.int32)[None, None, :]
    used = jnp.sum(hits.astype(WIDE), 1)
    weight = route_p * used
    earlier = jnp.tril(jnp.ones((tokens, tokens), LOWER), -1)
    rank = plain(earlier, used[:, :EXPERTS].astype(LOWER)).astype(jnp.int32)
    apart = jnp.arange(EXPERTS, dtype=jnp.int32) ^ (own // shards)
    place = apart[None] * CAP + rank
    place = jnp.where(rank < CAP, place, -1)
    real_hits = hits[:, :, :EXPERTS]
    slot = jnp.max(jnp.where(real_hits, place[:, None, :], -1), -1)
    w_slot = jnp.sum(jnp.where(real_hits, weight[:, None, :EXPERTS], 0.0), -1)
    all_slots = jnp.arange(EXPERTS * CAP, dtype=jnp.int32)
    picks = [(slot[:, k : k + 1] == all_slots[None]).astype(LOWER) for k in range(2)]
    both = picks[0] + picks[1]
    buffer = contract_rows(both, second_low).astype(LOWER)
    sent = send_slots(buffer, n_dp, shards)
    near, far = (experts_forward(rows, w_in, w_out) for rows in sent)
    returned = return_slots(near[3], far[3], n_dp, shards)
    outs = [pick_slots(picks[k], returned) for k in range(2)]
    moe = w_slot[:, 0:1] * outs[0] + w_slot[:, 1:2] * outs[1]
    const_p = jax.nn.softmax(contract_cols(second_low, const_gate).reshape(tokens, 2, 2), -1)
    const_out = const_p[:, :, 0:1] * second[:, None, :] + const_p[:, :, 1:2] * const_vec[None]
    moe = moe + weight[:, EXPERTS + 1 : EXPERTS + 2] * second
    moe = (
        moe
        + weight[:, EXPERTS + 2 : EXPERTS + 3] * const_out[:, 0]
        + weight[:, EXPERTS + 3 :] * const_out[:, 1]
    )
    third = first + moe
    saved = dict(
        gains=gains,
        const_vec=const_vec,
        router=router,
        const_gate=const_gate,
        segment=segment,
        scale_one=scale_one,
        normed_low=normed_low,
        qkv=qkv,
        mixed=mixed,
        first=first,
        second=second,
        scale_two=scale_two,
        second_low=second_low,
        route_p=route_p,
        hits=hits,
        used=used,
        weight=weight,
        w_slot=w_slot,
        picks=picks,
        both=both,
        rows=sent,
        near=near,
        far=far,
        outs=outs,
        const_p=const_p,
        const_out=const_out,
    )
    return (third, saved)


def vocab_tile(rows):
    return min(1024, (1 << 20) // rows)


def scores_body(aim_ref, rows_ref, table_ref, expo_ref, tops_ref, stats_ref, *, step_rows):
    tile = table_ref.shape[0]
    j = pl.program_id(0)

    @pl.when(j == 0)
    def _():
        stats_ref[0:1, :] = jnp.full((1, stats_ref.shape[1]), -1e30, WIDE)
        stats_ref[1:8, :] = jnp.zeros((7, stats_ref.shape[1]), WIDE)

    table = table_ref[...]
    for start in range(0, rows_ref.shape[0], step_rows):
        cols = slice(start, start + step_rows)
        logits = contract_cols(table, rows_ref[cols, :])
        top = jnp.max(logits, 0, keepdims=True)
        expo = jnp.exp(logits - top)
        expo_ref[:, cols] = expo.astype(LOWER)
        total = jnp.sum(expo, 0, keepdims=True)
        place = lax.broadcasted_iota(jnp.int32, logits.shape, 0)
        hit = place == aim_ref[:, cols] - j * tile
        aimed = jnp.sum(jnp.where(hit, logits, 0.0), 0, keepdims=True)
        tops_ref[0, :, cols] = top
        old = stats_ref[0:1, cols]
        high = jnp.maximum(old, top)
        stats_ref[1:2, cols] = stats_ref[1:2, cols] * jnp.exp(old - high) + total * jnp.exp(
            top - high
        )
        stats_ref[0:1, cols] = high
        stats_ref[2:3, cols] = stats_ref[2:3, cols] + aimed


def vocab_scores(rows, table, aim):
    count, vocab = rows.shape[0], table.shape[0]
    tile = vocab_tile(count)
    steps = vocab // tile
    return pl.pallas_call(
        functools.partial(scores_body, step_rows=ROWS),
        grid=(steps,),
        in_specs=[
            pl.BlockSpec((1, count), lambda j: (0, 0)),
            pl.BlockSpec((count, D), lambda j: (0, 0)),
            pl.BlockSpec((tile, D), lambda j: (j, 0)),
        ],
        out_specs=[
            pl.BlockSpec((tile, count), lambda j: (j, 0)),
            pl.BlockSpec((1, 1, count), lambda j: (j, 0, 0)),
            pl.BlockSpec((8, count), lambda j: (0, 0)),
        ],
        out_shape=[
            jax.ShapeDtypeStruct((vocab, count), LOWER),
            jax.ShapeDtypeStruct((steps, 1, count), WIDE),
            jax.ShapeDtypeStruct((8, count), WIDE),
        ],
        compiler_params=pltpu.CompilerParams(vmem_limit_bytes=VMEM_BYTES),
        name="vocab_scores",
    )(aim, rows, table)


def dlogits_body(aim_ref, scale_ref, expo_ref, table_ref, grad_ref, out_ref, *, step_rows, unit):
    tile = table_ref.shape[0]
    j = pl.program_id(0)

    @pl.when(j == 0)
    def _():
        out_ref[...] = jnp.zeros(out_ref.shape, WIDE)

    table = table_ref[...]
    for start in range(0, expo_ref.shape[1], step_rows):
        cols = slice(start, start + step_rows)
        expo = expo_ref[:, cols].astype(WIDE)
        place = lax.broadcasted_iota(jnp.int32, expo.shape, 0)
        hit = place == aim_ref[:, cols] - j * tile
        grad = (expo * scale_ref[0, :, cols] - jnp.where(hit, unit, 0.0)).astype(LOWER)
        grad_ref[:, cols] = grad
        out_ref[cols, :] += contract_rows(grad, table)


def vocab_grad_rows(expo, table, aim, scale, unit):
    vocab, count = expo.shape
    tile = vocab_tile(count)
    steps = vocab // tile
    return pl.pallas_call(
        functools.partial(dlogits_body, step_rows=ROWS, unit=unit),
        grid=(steps,),
        in_specs=[
            pl.BlockSpec((1, count), lambda j: (0, 0)),
            pl.BlockSpec((1, 1, count), lambda j: (j, 0, 0)),
            pl.BlockSpec((tile, count), lambda j: (j, 0)),
            pl.BlockSpec((tile, D), lambda j: (j, 0)),
        ],
        out_specs=[
            pl.BlockSpec((tile, count), lambda j: (j, 0)),
            pl.BlockSpec((count, D), lambda j: (0, 0)),
        ],
        out_shape=[
            jax.ShapeDtypeStruct((vocab, count), LOWER),
            jax.ShapeDtypeStruct((count, D), WIDE),
        ],
        compiler_params=pltpu.CompilerParams(vmem_limit_bytes=VMEM_BYTES),
        name="vocab_grad_rows",
    )(aim, scale, expo, table)


def vocab_grad_table_body(grad_ref, rows_ref, out_ref):
    out_ref[...] = plain(grad_ref[...], rows_ref[...]).astype(LOWER)


def vocab_grad_table(grad, rows):
    vocab, count = grad.shape
    tile = 2 * vocab_tile(count)
    return pl.pallas_call(
        vocab_grad_table_body,
        grid=(vocab // tile,),
        in_specs=[
            pl.BlockSpec((tile, count), lambda j: (j, 0)),
            pl.BlockSpec((count, D), lambda j: (0, 0)),
        ],
        out_specs=pl.BlockSpec((tile, D), lambda j: (j, 0)),
        out_shape=jax.ShapeDtypeStruct((vocab, D), LOWER),
        compiler_params=pltpu.CompilerParams(vmem_limit_bytes=VMEM_BYTES),
        name="vocab_grad_table",
    )(grad, rows)


def head_step(third, positions, targets, table_all, gain, own, n_dp):
    final, scale_three = norm_fwd(third, gain)
    tokens = third.shape[0]
    count = positions.shape[0]
    pick = positions[:, None] == jnp.arange(tokens, dtype=jnp.int32)[None, :]
    chosen = plain(pick.astype(LOWER), final.astype(LOWER)).astype(LOWER)
    near, far = gather_flips(chosen, n_dp)
    gathered = jnp.concatenate(near + far)
    aim = by_distance(targets, own).reshape(1, -1) - own * table_all.shape[0]
    expo, tops, stats = vocab_scores(gathered, table_all, aim)
    stats = by_distance(stats.reshape(8, n_dp, count).swapaxes(0, 1), own)
    stats = swap(jnp.broadcast_to(stats[None], (n_dp,) + stats.shape), "dp")
    high = jnp.max(stats[:, :, 0], 0)
    sums = jnp.sum(stats[:, :, 1] * jnp.exp(stats[:, :, 0] - high[None]), 0)
    lse = high + jnp.log(sums)
    lse = by_distance(lse, own)
    loss_part = jnp.sum(lse[0] - by_distance(jnp.sum(stats[:, :, 2], 0), own)[0]) / count
    lse = lse.reshape(1, 1, -1)
    scale = jnp.exp(tops - lse) / count
    grad_logits, grad_rows = vocab_grad_rows(expo, table_all, aim, scale, 1.0 / count)
    grad_rows = grad_rows.astype(LOWER)
    grad_chosen = sum_flips(cut(grad_rows, n_dp), n_dp)
    grad_table = vocab_grad_table(grad_logits, gathered)
    grad_chosen, grad_table = lax.optimization_barrier((grad_chosen, grad_table))
    grad_final = rows_high(pick.astype(WIDE), grad_chosen)
    grad_third, grad_gain = norm_back(third, scale_three, gain, grad_final)
    return (loss_part, grad_third, grad_gain, grad_table)


def layer_backward(hidden, grad_third, saved, dense_t, w_in, w_out, n_dp):
    shards = n_dp // EXPERTS
    gains, const_vec = saved["gains"], saved["const_vec"]
    router, const_gate = saved["router"], saved["const_gate"]
    tokens = hidden.shape[0]
    weight = saved["weight"]
    route_p = saved["route_p"]
    second_wide = saved["second_low"].astype(WIDE)
    w_slot, picks = saved["w_slot"], saved["picks"]
    grad_out = contract_rows(picks[0], (w_slot[:, 0:1] * grad_third).astype(LOWER))
    grad_out = grad_out + contract_rows(picks[1], (w_slot[:, 1:2] * grad_third).astype(LOWER))
    sent = send_slots(grad_out.astype(LOWER), n_dp, shards)
    near, far = saved["near"], saved["far"]
    near_back = experts_backward(sent[0], near[0], near[1], w_in, w_out)
    far_back = experts_backward(sent[1], far[0], far[1], w_in, w_out)
    came_back = return_slots(near_back[2], far_back[2], n_dp, shards)
    rows = jnp.concatenate(saved["rows"])
    grad_w_out = contract_rows(
        jnp.concatenate([near[2], far[2]]), jnp.concatenate(sent)
    ).astype(LOWER)
    grad_w_in = jnp.stack(
        [
            contract_rows(rows, jnp.concatenate([near_back[k], far_back[k]])).astype(LOWER)
            for k in range(2)
        ]
    )
    dots = [jnp.sum(saved["outs"][k] * grad_third, -1, keepdims=True) for k in range(2)]
    hits = saved["hits"].astype(WIDE)
    grad_real = (dots[0] * hits[:, 0] + dots[1] * hits[:, 1])[:, :EXPERTS]
    grad_copy = jnp.sum(grad_third * saved["second"], -1, keepdims=True)
    grad_const = jnp.sum(grad_third[:, None, :] * saved["const_out"], -1)
    grad_weight = jnp.concatenate(
        [grad_real, jnp.zeros((tokens, 1), WIDE), grad_copy, grad_const], 1
    )
    grad_p = grad_weight * saved["used"]
    grad_logit = route_p * (grad_p - jnp.sum(route_p * grad_p, -1, keepdims=True))
    const_p = saved["const_p"]
    w_const = weight[:, EXPERTS + 2 :]
    along_vec = jnp.dot(grad_third, const_vec.T, precision=HIGH)
    grad_alpha = w_const[:, :, None] * jnp.stack(
        [jnp.broadcast_to(grad_copy, along_vec.shape), along_vec], -1
    )
    grad_clog = (const_p * (grad_alpha - jnp.sum(const_p * grad_alpha, -1, keepdims=True))).reshape(
        tokens, 4
    )
    grad_cvec = rows_high(w_const * const_p[:, :, 1], grad_third)
    logit_all = jnp.concatenate([grad_logit, grad_clog], 1)
    grad_gates = rows_high(logit_all, second_wide)
    gates_all = jnp.concatenate([router, const_gate], 0).astype(WIDE)
    grad_second = jnp.dot(logit_all, gates_all, precision=HIGH)
    carry = weight[:, EXPERTS + 1 : EXPERTS + 2] + jnp.sum(
        w_const * const_p[:, :, 0], -1, keepdims=True
    )
    grad_second = grad_second + carry * grad_third
    grad_second = grad_second + pick_slots(saved["both"], came_back)
    grad_first_norm, grad_gain_two = norm_back(
        saved["first"], saved["scale_two"], gains[1], grad_second
    )
    grad_first = grad_third + grad_first_norm
    grad_attn = grad_first.astype(LOWER)
    grad_mixed = plain(grad_attn, dense_t[3 * D :]).astype(LOWER)
    grad_qkv = attend_back(saved["qkv"], grad_mixed, saved["segment"])
    grad_normed = plain(grad_qkv, dense_t[: 3 * D])
    unused, grad_gain_one = norm_back(hidden, saved["scale_one"], gains[0], grad_normed)
    left = (grad_qkv, grad_attn)
    return (left, grad_gain_one, grad_gain_two, grad_cvec, grad_gates, grad_w_in, grad_w_out)


def fold(value):
    rows, cols = value.shape
    if rows % 8 or cols % LANES:
        return jnp.pad(jnp.sum(value * value)[None], (0, LANES - 1))
    squares = jnp.sum((value * value).reshape(rows // 8, 8, cols), 0)
    return jnp.sum(squares.reshape(8, cols // LANES, LANES), (0, 1))


def group_squares(arrays, device):
    dense, small, ein, eout, tab = arrays
    width = dense.shape[1]
    front = (device * width + jnp.arange(width, dtype=jnp.int32) < 3 * D).astype(WIDE)
    lanes = (0, LANES - width)
    dense_sq = jnp.sum(dense * dense, 0)
    return [
        jnp.pad(dense_sq * front, lanes),
        jnp.pad(dense_sq * (1.0 - front), lanes),
        jnp.pad(jnp.sum(small[:5] * small[:5], 0), (0, LANES - small.shape[1])),
        jnp.pad(jnp.sum(small[5:] * small[5:], 0), (0, LANES - small.shape[1])),
        fold(ein.reshape(-1, ein.shape[-1])),
        fold(eout),
        fold(tab),
    ]


def moments(weight, first, second, grad):
    first = 0.5 * first + 0.5 * grad
    second = 0.5 * second + 0.5 * grad * grad
    corr = 1.0 - 0.5**STEP
    update = first / corr / (jnp.sqrt(second / corr) + EPS) + 0.01 * weight
    return (first, second, update)


def local(
    x_in,
    seq_lens,
    routes,
    positions,
    targets,
    dense_w,
    small_w,
    expert_in,
    expert_out,
    table,
    dense_m,
    small_m,
    expin_m,
    expout_m,
    table_m,
    dense_v,
    small_v,
    expin_v,
    expout_v,
    table_v,
):
    n_dp, n_rep = lax.axis_size("dp"), lax.axis_size("rep")
    devices = n_dp * n_rep
    own = lax.axis_index("dp")
    device = own * n_rep + lax.axis_index("rep")
    masters = (dense_w, small_w, expert_in, expert_out, table)
    width, thin = dense_w.shape[1], small_w.shape[1]
    place = jnp.stack([own, lax.axis_index("rep")]).astype(jnp.int32)
    flips = n_rep == 4 and width % 16 == 0 and thin % 8 == 0
    if flips:
        dense_t, small_all = gather_weights(dense_w, small_w, place, n_dp)
    else:
        dense_t = lax.all_gather(dense_w.T.astype(LOWER), BOTH, axis=0, tiled=True)
        small_t = jnp.pad(small_w.T.astype(LOWER), ((0, 0), (0, LANES - small_w.shape[0])))
        small_all = share(small_t, BOTH, devices).reshape(-1, LANES).T
    w_in, w_out, table_all = (
        lax.all_gather(expert_in.astype(LOWER), "rep", axis=1, tiled=True),
        lax.all_gather(expert_out.astype(LOWER), "rep", axis=0, tiled=True),
        lax.all_gather(table.astype(LOWER), "rep", axis=0, tiled=True),
    )
    hidden = x_in.astype(WIDE)
    third, saved = layer_forward(
        hidden, seq_lens[0], routes, dense_t, small_all, w_in, w_out, own, n_dp
    )
    loss_part, grad_third, grad_gain_final, grad_table = head_step(
        third, positions, targets[0], table_all, saved["gains"][2], own, n_dp
    )
    table_g = lax.psum_scatter(grad_table, "rep", scatter_dimension=0, tiled=True)
    left, gain_one, gain_two, grad_cvec, grad_gates, grad_w_in, grad_w_out = layer_backward(
        hidden, grad_third, saved, dense_t, w_in, w_out, n_dp
    )
    ein_g, eout_g = (
        lax.psum_scatter(grad_w_in, "rep", scatter_dimension=1, tiled=True),
        lax.psum_scatter(grad_w_out, "rep", scatter_dimension=0, tiled=True),
    )
    small_grad = jnp.concatenate(
        [gain_one[None], gain_two[None], grad_gain_final[None], grad_cvec, grad_gates], 0
    )
    normed, mixed = saved["normed_low"], saved["mixed"]
    if flips:
        turned = jnp.pad(small_grad, ((0, LANES - small_grad.shape[0]), (0, 0))).T
        mine, other = dense_grads(place, *left, normed, mixed, turned, n_dp, width)
        block = sum_weights(mine, other, n_dp)
        small_g = block[width:].reshape(8, -1, LANES)[:, : thin // 8].swapaxes(0, 1)
        small_g = small_g.reshape(thin, LANES)[:, : small_w.shape[0]].T
    else:
        dense_grad = jnp.concatenate(
            [contract_rows(left[0], normed), contract_rows(left[1], mixed)]
        )
        small_blocks = small_grad.reshape(-1, devices, thin).swapaxes(0, 1).reshape(devices, -1)
        extra = -(-small_blocks.shape[1] // (8 * D)) * 8 * D
        small_blocks = jnp.pad(small_blocks, ((0, 0), (0, extra - small_blocks.shape[1])))
        blocks = jnp.concatenate(
            [dense_grad.reshape(devices, width, D), small_blocks.reshape(devices, -1, D)], 1
        )
        block = scatter_sum(blocks.reshape((n_dp, n_rep) + blocks.shape[1:]), n_dp, n_rep)
        small_g = block[width:].reshape(-1)[: small_w.size].reshape(small_w.shape)
    dense_g = block[:width].T
    grads = (dense_g, small_g, ein_g.astype(WIDE), eout_g.astype(WIDE), table_g.astype(WIDE))
    firsts = (dense_m, small_m, expin_m, expout_m, table_m)
    seconds = (dense_v, small_v, expin_v, expout_v, table_v)
    results = [moments(w, m, v, g) for w, m, v, g in zip(masters, firsts, seconds, grads)]
    update_parts = group_squares(tuple((r[2] for r in results)), device)
    loss_row = jnp.pad(loss_part[None], (0, LANES - 1))
    parts = jnp.stack(group_squares(masters, device) + update_parts + [loss_row, loss_row * 0.0])
    sums = jnp.sum(share(parts, BOTH, devices), (0, 2))
    loss = sums[14]
    weight_norm = jnp.sqrt(sums[:7])
    update_norm = jnp.sqrt(sums[7:14])
    trust = weight_norm / update_norm
    column = device * width + jnp.arange(width, dtype=jnp.int32)
    dense_scale = jnp.where(column < 3 * D, trust[0], trust[1])[None, :]
    small_scale = jnp.where(jnp.arange(21, dtype=jnp.int32) < 5, trust[2], trust[3])[:, None]
    scales = (dense_scale, small_scale, trust[4], trust[5], trust[6])
    outs = [loss, jnp.stack([weight_norm, update_norm, trust])]
    for w, r, factor in zip(masters, results, scales):
        fresh = w - 0.2 * factor * r[2]
        outs += [r[0], r[1], fresh, fresh.astype(LOWER)]
    return tuple(outs)


def solution(mesh):
    in_specs = (
        P(("dp", "rep"), None),
        P(("dp", "rep"), None),
        P(("dp", "rep"), None),
        P(("dp", "rep")),
        P("rep", None, None),
        P(None, ("dp", "rep")),
        P(None, ("dp", "rep")),
        P(None, "rep", "dp"),
        P(("dp", "rep"), None),
        P(("dp", "rep"), None),
        P(None, ("dp", "rep")),
        P(None, ("dp", "rep")),
        P(None, "rep", "dp"),
        P(("dp", "rep"), None),
        P(("dp", "rep"), None),
        P(None, ("dp", "rep")),
        P(None, ("dp", "rep")),
        P(None, "rep", "dp"),
        P(("dp", "rep"), None),
        P(("dp", "rep"), None),
    )
    out_specs = (
        P(),
        P(),
        P(None, ("dp", "rep")),
        P(None, ("dp", "rep")),
        P(None, ("dp", "rep")),
        P(None, ("dp", "rep")),
        P(None, ("dp", "rep")),
        P(None, ("dp", "rep")),
        P(None, ("dp", "rep")),
        P(None, ("dp", "rep")),
        P(None, "rep", "dp"),
        P(None, "rep", "dp"),
        P(None, "rep", "dp"),
        P(None, "rep", "dp"),
        P(("dp", "rep"), None),
        P(("dp", "rep"), None),
        P(("dp", "rep"), None),
        P(("dp", "rep"), None),
        P(("dp", "rep"), None),
        P(("dp", "rep"), None),
        P(("dp", "rep"), None),
        P(("dp", "rep"), None),
    )
    return jax.shard_map(local, mesh=mesh, in_specs=in_specs, out_specs=out_specs, check_vma=False)
```

```python
import functools

import jax
import jax.numpy as jnp
from jax import lax
from jax.experimental import pallas as pl
from jax.experimental.pallas import tpu as pltpu
from jax.sharding import PartitionSpec as P

D = 768
HDIM = 64
EXPERTS = 8
NULLS = 4
STEP = 5
CAP = 96


EPS = 1e-06
HIGH = lax.Precision.HIGHEST
LOWER = jnp.bfloat16
WIDE = jnp.float32
BOTH = ("dp", "rep")
LANES = 128
MOST_FLIPS = 8
ROWS = 256
VMEM_BYTES = 48 << 20


def params(name, products=0, moved=0, exps=0):
    return dict(
        compiler_params=pltpu.CompilerParams(vmem_limit_bytes=VMEM_BYTES),
        cost_estimate=pl.CostEstimate(
            flops=2 * products, bytes_accessed=moved, transcendentals=exps
        ),
        name=name,
    )


def contract_rows(left, right):
    return lax.dot_general(left, right, (((0,), (0,)), ((), ())), preferred_element_type=WIDE)


def contract_cols(left, right):
    return lax.dot_general(left, right, (((1,), (1,)), ((), ())), preferred_element_type=WIDE)


def plain(left, right):
    return jnp.dot(left, right, preferred_element_type=WIDE)


def rows_high(left, right):
    return lax.dot_general(left, right, (((0,), (0,)), ((), ())), precision=HIGH)


def swap(value, axis):
    return lax.all_to_all(value, axis, split_axis=0, concat_axis=0, tiled=True)


def share(value, axis, count):
    return swap(jnp.broadcast_to(value[None], (count,) + value.shape), axis)


def flip(value, axis, mask, size):
    return lax.ppermute(value, axis, [(i, i ^ mask) for i in range(size)])


def by_distance(value, own):
    shape = value.shape
    mask = 1
    while mask < shape[0]:
        pairs = value.reshape((shape[0] // (2 * mask), 2, mask) + shape[1:])
        value = jnp.where((own & mask) != 0, jnp.flip(pairs, 1), pairs).reshape(shape)
        mask *= 2
    return value


def trade(blocks, n_dp):
    if n_dp > MOST_FLIPS:
        own = lax.axis_index("dp")
        return list(by_distance(swap(by_distance(jnp.stack(blocks), own), "dp"), own))
    half = n_dp // 2
    far = [flip(blocks[m], "dp", m, n_dp) for m in range(half, n_dp)]
    return blocks[:1] + [flip(blocks[m], "dp", m, n_dp) for m in range(1, half)] + far


def gather_flips(block, n_dp):
    half = n_dp // 2
    if n_dp > MOST_FLIPS:
        pieces = list(by_distance(lax.all_gather(block, "dp"), lax.axis_index("dp")))
        return pieces[:half], pieces[half:]
    cross = flip(block, "dp", half, n_dp)
    near = [block] + [flip(block, "dp", m, n_dp) for m in range(1, half)]
    far = [cross] + [flip(cross, "dp", m, n_dp) for m in range(1, half)]
    return near, far


def sum_flips(parts, n_dp):
    half = n_dp // 2
    if n_dp > MOST_FLIPS:
        pieces = by_distance(jnp.stack(parts).astype(LOWER), lax.axis_index("dp"))
        return jnp.sum(swap(pieces, "dp").astype(WIDE), 0)
    aims = [flip(parts[half + m].astype(LOWER), "dp", m, n_dp) for m in range(1, half)]
    across = sum([a.astype(WIDE) for a in aims], parts[half].astype(WIDE)).astype(LOWER)
    cross = flip(across, "dp", half, n_dp)
    near = [flip(parts[m].astype(LOWER), "dp", m, n_dp) for m in range(1, half)]
    total = sum([a.astype(WIDE) for a in near], parts[0].astype(WIDE))
    return total + cross.astype(WIDE)


def halve(buffer, axis, mask, size):
    own = (lax.axis_index(axis) & mask) // mask
    halves = buffer.reshape((buffer.shape[0] // 2, 2) + buffer.shape[1:])
    keep = lax.dynamic_index_in_dim(halves, own, 1, keepdims=False)
    give = lax.dynamic_index_in_dim(halves, 1 - own, 1, keepdims=False).astype(LOWER)
    take = lax.ppermute(give, axis, [(i, i ^ mask) for i in range(size)])
    return keep + take.astype(WIDE)


def scatter_sum(blocks, n_dp, n_rep):
    value = blocks.swapaxes(0, 1)
    mask = 1
    while mask < n_rep:
        value = halve(value, "rep", mask, n_rep)
        mask *= 2
    value = value[0]
    mask = 1
    while mask < n_dp:
        value = halve(value, "dp", mask, n_dp)
        mask *= 2
    return value[0]


def pack_body(dense_ref, small_ref, out_ref):
    width = dense_ref.shape[1]
    rows, thin = small_ref.shape
    out_ref[:width, :] = dense_ref[...].T.astype(LOWER)
    out_ref[width:, :] = jnp.zeros((8, D), LOWER)
    turned = small_ref[...].T.astype(LOWER)
    for g in range(thin // 8):
        out_ref[width:, g * LANES : g * LANES + rows] = turned[g * 8 : g * 8 + 8, :]


def pack(dense_w, small_w):
    return pl.pallas_call(
        pack_body,
        out_shape=jax.ShapeDtypeStruct((dense_w.shape[1] + 8, D), LOWER),
        **params("pack", 0, 6 * dense_w.size),
    )(dense_w, small_w)


def assemble_body(place_ref, *refs, n_dp, width, thin):
    pieces = refs[: 2 * n_dp]
    qkv_ref, out_ref, small_ref, raw_ref, turned_ref, dense_sem, small_sem = refs[2 * n_dp :]
    own, rep = place_ref[0], place_ref[1]
    front = qkv_ref.shape[0]
    small_waits, dense_waits = [], []
    for m in range(n_dp):
        for pair in range(2):
            for core in range(2):
                piece = pieces[core * n_dp + m]
                device = (own ^ m) * 4 + (rep ^ (2 * pair + core))
                top = pair * (width + 8)
                number = m * 4 + pair * 2 + core
                small = pltpu.make_async_copy(
                    piece.at[pl.ds(top + width, 8), :], raw_ref.at[device], small_sem.at[number]
                )
                small.start()
                rows = piece.at[pl.ds(top, width), :]
                into_qkv = pltpu.make_async_copy(
                    rows, qkv_ref.at[jnp.minimum(device, front - 1)], dense_sem.at[number]
                )
                into_out = pltpu.make_async_copy(
                    rows, out_ref.at[jnp.maximum(device - front, 0)], dense_sem.at[number]
                )
                pl.when(device < front)(into_qkv.start)
                pl.when(device >= front)(into_out.start)
                small_waits.append(small)
                dense_waits.append(into_qkv)
    for copy in small_waits:
        copy.wait()
    for device in range(4 * n_dp):
        for g in range(thin // 8):
            start = device * thin + g * 8
            tile = raw_ref[device, :, g * LANES : (g + 1) * LANES]
            turned_ref[start : start + 8, :] = tile.astype(WIDE)
    small_ref[...] = turned_ref[...].T[: small_ref.shape[0], :]
    for copy in dense_waits:
        copy.wait()


def assemble(pieces, place, n_dp, width, thin):
    return pl.pallas_call(
        functools.partial(assemble_body, n_dp=n_dp, width=width, thin=thin),
        in_specs=[pl.BlockSpec(memory_space=pltpu.SMEM)]
        + [pl.BlockSpec(memory_space=pl.ANY)] * len(pieces),
        out_specs=[
            pl.BlockSpec(memory_space=pl.ANY),
            pl.BlockSpec(memory_space=pl.ANY),
            pl.BlockSpec(memory_space=pltpu.VMEM),
        ],
        out_shape=[
            jax.ShapeDtypeStruct((3 * n_dp, width, D), LOWER),
            jax.ShapeDtypeStruct((n_dp, width, D), LOWER),
            jax.ShapeDtypeStruct((24, D), WIDE),
        ],
        scratch_shapes=[
            pltpu.VMEM((4 * n_dp, 8, D), LOWER),
            pltpu.VMEM((4 * n_dp * thin, LANES), WIDE),
            pltpu.SemaphoreType.DMA((4 * n_dp,)),
            pltpu.SemaphoreType.DMA((4 * n_dp,)),
        ],
        **params("assemble", 0, 32 * n_dp * width * D),
    )(place, *pieces)


def gather_weights(block, place, n_dp, width, thin):
    both = jnp.concatenate([block, flip(block, "rep", 2, 4)])
    near, far = gather_flips(both, n_dp)
    mine = near + far
    theirs = [flip(piece, "rep", 1, 4) for piece in mine]
    qkv, out, small = assemble(mine + theirs, place, n_dp, width, thin)
    return qkv.reshape(-1, D), out.reshape(-1, D), small


def dense_grad_body(
    place_ref, qkv_ref, attn_ref, normed_ref, mixed_ref, small_ref, mine_ref, other_ref, sum_ref
):
    j = pl.program_id(0)
    width, thin = mine_ref.shape[2] - 8, small_ref.shape[0] // (4 * pl.num_programs(0))
    front = 3 * D // (4 * width)

    @pl.when(j < front)
    def _():
        sum_ref[...] = contract_rows(qkv_ref[...], normed_ref[...])

    @pl.when(j >= front)
    def _():
        sum_ref[...] = contract_rows(attn_ref[...], mixed_ref[...])

    rep = place_ref[1]
    for pair in range(2):
        for core, out_ref in enumerate((mine_ref, other_ref)):
            r = rep ^ (2 * pair + core)
            rows = pl.multiple_of(r * width, 8)
            out_ref[0, pair, :width, :] = sum_ref[pl.ds(rows, width), :].astype(out_ref.dtype)
            out_ref[0, pair, width:, :] = jnp.zeros((8, D), out_ref.dtype)
            for g in range(thin // 8):
                start = pl.multiple_of((j * 4 + r) * thin + g * 8, 8)
                tile = small_ref[pl.ds(start, 8), :].astype(out_ref.dtype)
                out_ref[0, pair, width:, g * LANES : (g + 1) * LANES] = tile


def dense_grads(place, grad_qkv, grad_attn, normed, mixed, small_turned, n_dp, width):
    tokens = grad_qkv.shape[0]
    wide = 4 * width
    front = 3 * D // wide
    block = (1, 2, width + 8, D)
    whole = lambda shape: pl.BlockSpec(shape, lambda j, place: (0, 0))
    out_spec = pl.BlockSpec(block, lambda j, place: (j ^ place[0], 0, 0, 0))
    return pl.pallas_call(
        dense_grad_body,
        grid_spec=pltpu.PrefetchScalarGridSpec(
            num_scalar_prefetch=1,
            grid=(n_dp,),
            in_specs=[
                pl.BlockSpec((tokens, wide), lambda j, place: (0, jnp.minimum(j, front - 1))),
                pl.BlockSpec((tokens, wide), lambda j, place: (0, jnp.maximum(j - front, 0))),
                whole((tokens, D)),
                whole((tokens, D)),
                whole(small_turned.shape),
            ],
            out_specs=[out_spec, out_spec],
            scratch_shapes=[pltpu.VMEM((wide, D), WIDE)],
        ),
        out_shape=[
            jax.ShapeDtypeStruct((n_dp,) + block[1:], WIDE),
            jax.ShapeDtypeStruct((n_dp,) + block[1:], LOWER),
        ],
        **params("dense_grads", tokens * 4 * D * D, 12 * tokens * D + 24 * D * D),
    )(place, grad_qkv, grad_attn, normed, mixed, small_turned)


def sum_weights(mine, other, n_dp, jobs):
    both = mine + flip(other, "rep", 1, 4).astype(WIDE)
    parts = [both[m] for m in range(n_dp)]
    done = []

    def beside(value, job):
        value, result = lax.optimization_barrier((value, job(done)))
        done.append(result)
        return value

    if n_dp > MOST_FLIPS:
        pair = beside(beside(sum_flips(parts, n_dp), jobs[0]), jobs[1])
    else:
        half = n_dp // 2
        aims = [flip(parts[half + m].astype(LOWER), "dp", m, n_dp) for m in range(1, half)]
        near = [flip(parts[m].astype(LOWER), "dp", m, n_dp) for m in range(1, half)]
        aims = beside(aims, jobs[0])
        cross = flip(add_up([parts[half]] + aims).astype(LOWER), "dp", half, n_dp)
        cross = beside(cross, jobs[1])
        pair = add_up([parts[0]] + near + [cross])
    far = beside(flip(pair[1].astype(LOWER), "rep", 2, 4), jobs[2])
    return pair[0] + far.astype(WIDE), done


def norm_fwd(hidden, gain):
    scale = lax.rsqrt(jnp.mean(hidden * hidden, -1, keepdims=True) + EPS)
    return (hidden * scale * gain, scale)


def norm_back(hidden, scale, gain, grad_out):
    normed = hidden * scale
    grad_gain = jnp.sum(grad_out * normed, 0)
    inner = grad_out * gain
    grad_in = scale * (inner - normed * jnp.mean(inner * normed, -1, keepdims=True))
    return (grad_in, grad_gain)


def segments(lens, tokens):
    place = jnp.arange(tokens, dtype=jnp.int32)
    ends = [jnp.sum(lens[: i + 1]) for i in range(lens.shape[0])]
    return sum((place >= end).astype(jnp.int32) for end in ends)


def build_bias(bias_ref, key_dim):
    shape = bias_ref.shape
    query = lax.broadcasted_iota(jnp.int32, shape, 1 - key_dim)
    key = lax.broadcasted_iota(jnp.int32, shape, key_dim)
    return key <= query


def lane_masks():
    lane = lax.broadcasted_iota(jnp.int32, (1, 2 * HDIM), 1)
    low = (lane < HDIM).astype(WIDE)
    return (low.astype(LOWER), (1.0 - low).astype(LOWER))


def attend_body(seg_col, seg_row, q_ref, k_ref, v_ref, out_ref, bias_ref):
    tokens = q_ref.shape[0]

    @pl.when(pl.program_id(0) == 0)
    def _():
        counts = build_bias(bias_ref, 1) & (seg_col[...] == seg_row[...])
        bias_ref[...] = jnp.where(counts, 0.0, -1e30)

    masks = lane_masks()
    for start in range(0, tokens, ROWS):
        keys = start + ROWS
        k = k_ref[:keys, :]
        v = v_ref[:keys, :]
        q = q_ref[start : start + ROWS, :]
        acc = jnp.zeros((ROWS, 2 * HDIM), WIDE)
        for mine in masks:
            scores = contract_cols(q * mine, k) * HDIM ** (-0.5)
            scores = scores + bias_ref[start : start + ROWS, :keys]
            expo = jnp.exp(scores - jnp.max(scores, -1, keepdims=True))
            total = jnp.sum(expo, -1, keepdims=True)
            probs = (expo * (1.0 / total)).astype(LOWER)
            acc = acc + plain(probs, v * mine)
        out_ref[start : start + ROWS, :] = acc.astype(LOWER)


def head_specs(tokens, first):
    return [
        pl.BlockSpec((tokens, 2 * HDIM), lambda j, base=base: (0, base + j)) for base in first
    ]


def attend(qkv, segment):
    tokens = qkv.shape[0]
    pairs = D // (2 * HDIM)
    return pl.pallas_call(
        attend_body,
        grid=(pairs,),
        in_specs=[
            pl.BlockSpec((tokens, 1), lambda j: (0, 0)),
            pl.BlockSpec((1, tokens), lambda j: (0, 0)),
        ]
        + head_specs(tokens, (0, pairs, 2 * pairs)),
        out_specs=pl.BlockSpec((tokens, 2 * HDIM), lambda j: (0, j)),
        out_shape=jax.ShapeDtypeStruct((tokens, D), LOWER),
        scratch_shapes=[pltpu.VMEM((tokens, tokens), WIDE)],
        **params("attend", 2 * tokens * tokens * D, 8 * tokens * D, tokens * tokens * D // HDIM),
    )(segment[:, None], segment[None, :], qkv, qkv, qkv)


def attend_back_body(seg_col, seg_row, q_ref, k_ref, v_ref, do_ref, out_ref, bias_ref):
    tokens = q_ref.shape[0]
    step = pl.program_id(0)

    @pl.when(step == 0)
    def _():
        counts = build_bias(bias_ref, 0) & (seg_col[...] == seg_row[...])
        bias_ref[...] = jnp.where(counts, 0.0, -1e30)

    masks = lane_masks()
    scale = HDIM ** (-0.5)
    grad_k = [jnp.zeros((ROWS, 2 * HDIM), WIDE) for _ in range(tokens // ROWS)]
    grad_v = [jnp.zeros((ROWS, 2 * HDIM), WIDE) for _ in range(tokens // ROWS)]
    col = pl.multiple_of(step * 2 * HDIM, 2 * HDIM)
    for block, start in enumerate(range(0, tokens, ROWS)):
        keys = start + ROWS
        k = k_ref[:keys, :]
        v = v_ref[:keys, :]
        q = q_ref[start : start + ROWS, :]
        do = do_ref[start : start + ROWS, :]
        grad_q = jnp.zeros((ROWS, 2 * HDIM), WIDE)
        for mine in masks:
            q_own = q * mine
            do_own = do * mine
            scores = contract_cols(k, q_own) * scale + bias_ref[:keys, start : start + ROWS]
            expo = jnp.exp(scores - jnp.max(scores, 0, keepdims=True))
            total = jnp.sum(expo, 0, keepdims=True)
            probs = expo * (1.0 / total)
            grad_p = contract_cols(v, do_own)
            inner = jnp.sum(probs * grad_p, 0, keepdims=True)
            grad_s = (probs * (grad_p - inner)).astype(LOWER)
            grad_q = grad_q + contract_rows(grad_s, k * mine)
            into_v = plain(probs.astype(LOWER), do_own)
            into_k = plain(grad_s, q_own)
            for b in range(block + 1):
                grad_v[b] = grad_v[b] + into_v[b * ROWS : (b + 1) * ROWS]
                grad_k[b] = grad_k[b] + into_k[b * ROWS : (b + 1) * ROWS]
        out_ref[start : start + ROWS, pl.ds(col, 2 * HDIM)] = (grad_q * scale).astype(LOWER)
    for b in range(tokens // ROWS):
        rows = slice(b * ROWS, (b + 1) * ROWS)
        out_ref[rows, pl.ds(D + col, 2 * HDIM)] = (grad_k[b] * scale).astype(LOWER)
        out_ref[rows, pl.ds(2 * D + col, 2 * HDIM)] = grad_v[b].astype(LOWER)


def attend_back(qkv, grad_mixed, segment):
    tokens = qkv.shape[0]
    pairs = D // (2 * HDIM)
    return pl.pallas_call(
        attend_back_body,
        grid=(pairs,),
        in_specs=[
            pl.BlockSpec((tokens, 1), lambda j: (0, 0)),
            pl.BlockSpec((1, tokens), lambda j: (0, 0)),
        ]
        + head_specs(tokens, (0, pairs, 2 * pairs))
        + head_specs(tokens, (0,)),
        out_specs=pl.BlockSpec((tokens, 3 * D), lambda j: (0, 0)),
        out_shape=jax.ShapeDtypeStruct((tokens, 3 * D), LOWER),
        scratch_shapes=[pltpu.VMEM((tokens, tokens), WIDE)],
        **params("attend_back", 5 * tokens * tokens * D, 14 * tokens * D, tokens * tokens * D // HDIM),
    )(segment[:, None], segment[None, :], qkv, qkv, qkv, grad_mixed)


def full(shape):
    return pl.BlockSpec(shape, lambda *index: (0,) * len(shape))


def experts_forward_body(*refs):
    (*pieces, w_in_ref, w_out_ref, gate_ref, up_ref, inner_ref, rows_ref), rest = (
        refs[: len(refs) // 2 + 3],
        refs[len(refs) // 2 + 3 :],
    )
    *parts, acc_ref = rest
    j = pl.program_id(0)

    @pl.when(j == 0)
    def _():
        for i, piece in enumerate(pieces):
            rows_ref[i * CAP : (i + 1) * CAP, :] = piece[...]
        acc_ref[...] = jnp.zeros(acc_ref.shape, WIDE)

    rows = rows_ref[...]
    gate = plain(rows, w_in_ref[0])
    up = plain(rows, w_in_ref[1])
    inner = (jax.nn.silu(gate) * up).astype(LOWER)
    gate_ref[...] = gate
    up_ref[...] = up
    inner_ref[...] = inner
    acc_ref[...] += plain(inner, w_out_ref[...])

    @pl.when(j == pl.num_programs(0) - 1)
    def _():
        for i, part in enumerate(parts):
            part[...] = acc_ref[i * CAP : (i + 1) * CAP, :].astype(LOWER)


def experts_forward(pieces, w_in, w_out):
    rows, hidden = len(pieces) * CAP, w_out.shape[0]
    tile = min(hidden, 512)
    piece = full((CAP, D))
    band = pl.BlockSpec((rows, tile), lambda j: (0, j))
    gate, up, inner, joined, *parts = pl.pallas_call(
        experts_forward_body,
        grid=(hidden // tile,),
        in_specs=[piece] * len(pieces)
        + [
            pl.BlockSpec((2, D, tile), lambda j: (0, 0, j)),
            pl.BlockSpec((tile, D), lambda j: (j, 0)),
        ],
        out_specs=[band, band, band, full((rows, D))] + [piece] * len(pieces),
        out_shape=[
            jax.ShapeDtypeStruct((rows, hidden), WIDE),
            jax.ShapeDtypeStruct((rows, hidden), WIDE),
            jax.ShapeDtypeStruct((rows, hidden), LOWER),
            jax.ShapeDtypeStruct((rows, D), LOWER),
        ]
        + [jax.ShapeDtypeStruct((CAP, D), LOWER)] * len(pieces),
        scratch_shapes=[pltpu.VMEM((rows, D), WIDE)],
        **params("experts_forward", 3 * rows * hidden * D, 6 * hidden * D + 10 * rows * hidden),
    )(*pieces, w_in, w_out)
    return gate, up, inner, joined, parts


def experts_backward_body(*refs):
    count = (len(refs) - 7) // 2
    pieces, refs = refs[:count], refs[count:]
    gate_ref, up_ref, w_in_ref, w_out_ref, backs_ref, rows_ref, *parts, acc_ref = refs
    j = pl.program_id(0)

    @pl.when(j == 0)
    def _():
        for i, piece in enumerate(pieces):
            rows_ref[i * CAP : (i + 1) * CAP, :] = piece[...]
        acc_ref[...] = jnp.zeros(acc_ref.shape, WIDE)

    grad_inner = contract_cols(rows_ref[...], w_out_ref[...])
    gate, up = gate_ref[...], up_ref[...]
    sig = jax.nn.sigmoid(gate)
    grad_gate = (grad_inner * up * sig * (1.0 + gate * (1.0 - sig))).astype(LOWER)
    grad_up = (grad_inner * gate * sig).astype(LOWER)
    backs_ref[0] = grad_gate
    backs_ref[1] = grad_up
    acc_ref[...] += contract_cols(grad_gate, w_in_ref[0]) + contract_cols(grad_up, w_in_ref[1])

    @pl.when(j == pl.num_programs(0) - 1)
    def _():
        for i, part in enumerate(parts):
            part[...] = acc_ref[i * CAP : (i + 1) * CAP, :].astype(LOWER)


def experts_backward(pieces, gate, up, w_in, w_out):
    rows, hidden = gate.shape
    tile = min(hidden, 512)
    piece = full((CAP, D))
    band = pl.BlockSpec((rows, tile), lambda j: (0, j))
    backs, joined, *parts = pl.pallas_call(
        experts_backward_body,
        grid=(hidden // tile,),
        in_specs=[piece] * len(pieces)
        + [
            band,
            band,
            pl.BlockSpec((2, D, tile), lambda j: (0, 0, j)),
            pl.BlockSpec((tile, D), lambda j: (j, 0)),
        ],
        out_specs=[pl.BlockSpec((2, rows, tile), lambda j: (0, 0, j)), full((rows, D))]
        + [piece] * len(pieces),
        out_shape=[
            jax.ShapeDtypeStruct((2, rows, hidden), LOWER),
            jax.ShapeDtypeStruct((rows, D), LOWER),
        ]
        + [jax.ShapeDtypeStruct((CAP, D), LOWER)] * len(pieces),
        scratch_shapes=[pltpu.VMEM((rows, D), WIDE)],
        **params("experts_backward", 3 * rows * hidden * D, 6 * hidden * D + 12 * rows * hidden),
    )(*pieces, gate, up, w_in, w_out)
    return backs, joined, parts


def grads_in_body(
    place_ref, rows_a, rows_b, back_a, back_b, keep_ref, give_ref, sum_ref, turned_a, turned_b
):
    @pl.when((pl.program_id(0) == 0) & (pl.program_id(1) == 0))
    def _():
        turned_a[...] = rows_a[...].T
        turned_b[...] = rows_b[...].T

    sum_ref[...] = plain(turned_a[...], back_a[0]) + plain(turned_b[...], back_b[0])
    size = keep_ref.shape[2]
    for pair in range(2):
        for core, out_ref in enumerate((keep_ref, give_ref)):
            start = pl.multiple_of((place_ref[1] ^ (2 * pair + core)) * size, 8)
            out_ref[0, pair] = sum_ref[pl.ds(start, size), :].astype(LOWER)


def grads_in(place, rows_a, rows_b, back_a, back_b):
    rows, hidden = back_a.shape[1:]
    tile = 512
    size = D // 4
    back = pl.BlockSpec((1, rows, tile), lambda k, j, place: (k, 0, j))
    out = pl.BlockSpec((1, 2, size, tile), lambda k, j, place: (k, 0, 0, j))
    return pl.pallas_call(
        grads_in_body,
        grid_spec=pltpu.PrefetchScalarGridSpec(
            num_scalar_prefetch=1,
            grid=(2, hidden // tile),
            in_specs=[full((rows, D)), full((rows, D)), back, back],
            out_specs=[out, out],
            scratch_shapes=[pltpu.VMEM((D, tile), WIDE)] + [pltpu.VMEM((D, rows), LOWER)] * 2,
        ),
        out_shape=[jax.ShapeDtypeStruct((2, 2, size, hidden), LOWER)] * 2,
        **params("grads_in", 4 * rows * hidden * D, 4 * hidden * D + 8 * rows * hidden),
    )(place, rows_a, rows_b, back_a, back_b)


def grads_out_body(place_ref, inner_a, inner_b, back_a, back_b, out_ref):
    total = contract_rows(inner_a[...], back_a[...]) + contract_rows(inner_b[...], back_b[...])
    out_ref[0] = total.astype(LOWER)


def grads_out(place, core, inner_a, inner_b, back_a, back_b):
    rows, hidden = inner_a.shape
    size = hidden // 4
    band = pl.BlockSpec((rows, size), lambda x, place: (0, place[1] ^ (2 * x + core)))
    return pl.pallas_call(
        grads_out_body,
        grid_spec=pltpu.PrefetchScalarGridSpec(
            num_scalar_prefetch=1,
            grid=(2,),
            in_specs=[band, band, full((rows, D)), full((rows, D))],
            out_specs=pl.BlockSpec((1, size, D), lambda x, place: (x, 0, 0)),
        ),
        out_shape=jax.ShapeDtypeStruct((2, size, D), LOWER),
        **params("grads_out", rows * hidden * D, hidden * D + 2 * rows * hidden),
    )(place, inner_a, inner_b, back_a, back_b)


def sum_experts_out(place, near, far, near_back, far_back, came_back):
    if lax.axis_size("rep") != 4:
        grad = contract_rows(
            jnp.concatenate([near[2], far[2]]), jnp.concatenate([near_back[1], far_back[1]])
        ).astype(LOWER)
        return [lax.psum_scatter(grad, "rep", scatter_dimension=0, tiled=True)], came_back
    came_back, rows = lax.optimization_barrier((came_back, (near_back[1], far_back[1])))
    ends = (near[2], far[2]) + rows
    give, keep = grads_out(place, 1, *ends), grads_out(place, 0, *ends)
    came_back, give, keep = lax.optimization_barrier((came_back, give, keep))
    take = flip(give, "rep", 1, 4)
    return [keep[0], take[0], (keep[1].astype(WIDE) + take[1].astype(WIDE)).astype(LOWER)], came_back


def sum_experts_in(place, near, far, near_back, far_back, after):
    if lax.axis_size("rep") != 4:
        rows = jnp.concatenate([near[3], far[3]])
        backs = jnp.concatenate([near_back[0], far_back[0]], 1)
        grad = jnp.stack([contract_rows(rows, back).astype(LOWER) for back in backs])
        return [lax.psum_scatter(grad, "rep", scatter_dimension=1, tiled=True)], after
    after, backs = lax.optimization_barrier((after, (near_back[0], far_back[0])))
    keep, give = grads_in(place, near[3], far[3], *backs)
    take = flip(give, "rep", 1, 4)
    far = [(keep[k, 1].astype(WIDE) + take[k, 1].astype(WIDE)).astype(LOWER) for k in range(2)]
    return [keep[:, 0], take[:, 0], far], after


def add_up(parts):
    return sum([part.astype(WIDE) for part in parts[1:]], parts[0].astype(WIDE))


def cut(value, count):
    size = value.shape[0] // count
    return [value[i * size : (i + 1) * size] for i in range(count)]


def send_slots(buffer, n_dp, shards):
    half = n_dp // 2
    blocks = trade([b for b in cut(buffer, EXPERTS) for _ in range(shards)], n_dp)
    return blocks[:half], blocks[half:]


def return_slots(near, far, n_dp, shards):
    blocks = trade(list(near) + list(far), n_dp)
    return [jnp.concatenate(blocks[s::shards]) for s in range(shards)]


def pick_slots(picks, received):
    return sum(plain(picks, part) for part in received)


def layer_forward(hidden, lens, routes, w_qkv, w_attn, small_all, w_in, w_out, own, n_dp):
    shards = n_dp // EXPERTS
    gains, const_vec, router, const_gate = (
        small_all[:3].astype(WIDE),
        small_all[3:5].astype(WIDE),
        small_all[5:17].astype(LOWER),
        small_all[17:21].astype(LOWER),
    )
    tokens = hidden.shape[0]
    segment = segments(lens, tokens)
    normed, scale_one = norm_fwd(hidden, gains[0])
    normed_low = normed.astype(LOWER)
    qkv = contract_cols(normed_low, w_qkv).astype(LOWER)
    mixed = attend(qkv, segment)
    first = hidden + contract_cols(mixed, w_attn)
    second, scale_two = norm_fwd(first, gains[1])
    second_low = second.astype(LOWER)
    route_p = jax.nn.softmax(contract_cols(second_low, router), -1)
    hits = routes[:, :, None] == jnp.arange(EXPERTS + NULLS, dtype=jnp.int32)[None, None, :]
    used = jnp.sum(hits.astype(WIDE), 1)
    weight = route_p * used
    earlier = jnp.tril(jnp.ones((tokens, tokens), LOWER), -1)
    rank = plain(earlier, used[:, :EXPERTS].astype(LOWER)).astype(jnp.int32)
    apart = jnp.arange(EXPERTS, dtype=jnp.int32) ^ (own // shards)
    place = apart[None] * CAP + rank
    place = jnp.where(rank < CAP, place, -1)
    real_hits = hits[:, :, :EXPERTS]
    slot = jnp.max(jnp.where(real_hits, place[:, None, :], -1), -1)
    w_slot = jnp.sum(jnp.where(real_hits, weight[:, None, :EXPERTS], 0.0), -1)
    all_slots = jnp.arange(EXPERTS * CAP, dtype=jnp.int32)
    picks = [(slot[:, k : k + 1] == all_slots[None]).astype(LOWER) for k in range(2)]
    both = picks[0] + picks[1]
    buffer = contract_rows(both, second_low).astype(LOWER)
    sent = send_slots(buffer, n_dp, shards)
    near, far = (experts_forward(rows, w_in, w_out) for rows in sent)
    returned = return_slots(near[4], far[4], n_dp, shards)
    outs = [pick_slots(picks[k], returned) for k in range(2)]
    moe = w_slot[:, 0:1] * outs[0] + w_slot[:, 1:2] * outs[1]
    const_p = jax.nn.softmax(contract_cols(second_low, const_gate).reshape(tokens, 2, 2), -1)
    const_out = const_p[:, :, 0:1] * second[:, None, :] + const_p[:, :, 1:2] * const_vec[None]
    moe = moe + weight[:, EXPERTS + 1 : EXPERTS + 2] * second
    moe = (
        moe
        + weight[:, EXPERTS + 2 : EXPERTS + 3] * const_out[:, 0]
        + weight[:, EXPERTS + 3 :] * const_out[:, 1]
    )
    third = first + moe
    saved = dict(
        gains=gains,
        const_vec=const_vec,
        router=router,
        const_gate=const_gate,
        segment=segment,
        scale_one=scale_one,
        normed_low=normed_low,
        qkv=qkv,
        mixed=mixed,
        first=first,
        second=second,
        scale_two=scale_two,
        second_low=second_low,
        route_p=route_p,
        hits=hits,
        used=used,
        weight=weight,
        w_slot=w_slot,
        picks=picks,
        both=both,
        near=near,
        far=far,
        outs=outs,
        const_p=const_p,
        const_out=const_out,
    )
    return (third, saved)


def vocab_tile(rows):
    return min(1024, (1 << 20) // rows)


def scores_body(aim_ref, rows_ref, table_ref, expo_ref, tops_ref, stats_ref, *, step_rows):
    tile = table_ref.shape[0]
    j = pl.program_id(0)

    @pl.when(j == 0)
    def _():
        stats_ref[0:1, :] = jnp.full((1, stats_ref.shape[1]), -1e30, WIDE)
        stats_ref[1:8, :] = jnp.zeros((7, stats_ref.shape[1]), WIDE)

    table = table_ref[...]
    for start in range(0, rows_ref.shape[0], step_rows):
        cols = slice(start, start + step_rows)
        logits = contract_cols(table, rows_ref[cols, :])
        top = jnp.max(logits, 0, keepdims=True)
        expo = jnp.exp(logits - top)
        expo_ref[:, cols] = expo.astype(LOWER)
        total = jnp.sum(expo, 0, keepdims=True)
        place = lax.broadcasted_iota(jnp.int32, logits.shape, 0)
        hit = place == aim_ref[:, cols] - j * tile
        aimed = jnp.sum(jnp.where(hit, logits, 0.0), 0, keepdims=True)
        tops_ref[0, :, cols] = top
        old = stats_ref[0:1, cols]
        high = jnp.maximum(old, top)
        stats_ref[1:2, cols] = stats_ref[1:2, cols] * jnp.exp(old - high) + total * jnp.exp(
            top - high
        )
        stats_ref[0:1, cols] = high
        stats_ref[2:3, cols] = stats_ref[2:3, cols] + aimed


def vocab_scores(rows, table, aim):
    count, vocab = rows.shape[0], table.shape[0]
    tile = vocab_tile(count)
    steps = vocab // tile
    return pl.pallas_call(
        functools.partial(scores_body, step_rows=ROWS),
        grid=(steps,),
        in_specs=[
            pl.BlockSpec((1, count), lambda j: (0, 0)),
            pl.BlockSpec((count, D), lambda j: (0, 0)),
            pl.BlockSpec((tile, D), lambda j: (j, 0)),
        ],
        out_specs=[
            pl.BlockSpec((tile, count), lambda j: (j, 0)),
            pl.BlockSpec((1, 1, count), lambda j: (j, 0, 0)),
            pl.BlockSpec((8, count), lambda j: (0, 0)),
        ],
        out_shape=[
            jax.ShapeDtypeStruct((vocab, count), LOWER),
            jax.ShapeDtypeStruct((steps, 1, count), WIDE),
            jax.ShapeDtypeStruct((8, count), WIDE),
        ],
        **params("vocab_scores", count * vocab * D, 2 * vocab * (count + D), count * vocab),
    )(aim, rows, table)


def dlogits_body(aim_ref, scale_ref, expo_ref, table_ref, grad_ref, out_ref, *, step_rows, unit):
    tile = table_ref.shape[0]
    j = pl.program_id(0)

    @pl.when(j == 0)
    def _():
        out_ref[...] = jnp.zeros(out_ref.shape, WIDE)

    table = table_ref[...]
    for start in range(0, expo_ref.shape[1], step_rows):
        cols = slice(start, start + step_rows)
        expo = expo_ref[:, cols].astype(WIDE)
        place = lax.broadcasted_iota(jnp.int32, expo.shape, 0)
        hit = place == aim_ref[:, cols] - j * tile
        grad = (expo * scale_ref[0, :, cols] - jnp.where(hit, unit, 0.0)).astype(LOWER)
        grad_ref[:, cols] = grad
        out_ref[cols, :] += contract_rows(grad, table)


def vocab_grad_rows(expo, table, aim, scale, unit):
    vocab, count = expo.shape
    tile = vocab_tile(count)
    steps = vocab // tile
    return pl.pallas_call(
        functools.partial(dlogits_body, step_rows=ROWS, unit=unit),
        grid=(steps,),
        in_specs=[
            pl.BlockSpec((1, count), lambda j: (0, 0)),
            pl.BlockSpec((1, 1, count), lambda j: (j, 0, 0)),
            pl.BlockSpec((tile, count), lambda j: (j, 0)),
            pl.BlockSpec((tile, D), lambda j: (j, 0)),
        ],
        out_specs=[
            pl.BlockSpec((tile, count), lambda j: (j, 0)),
            pl.BlockSpec((count, D), lambda j: (0, 0)),
        ],
        out_shape=[
            jax.ShapeDtypeStruct((vocab, count), LOWER),
            jax.ShapeDtypeStruct((count, D), WIDE),
        ],
        **params("vocab_grad_rows", count * vocab * D, 2 * vocab * (2 * count + D)),
    )(aim, scale, expo, table)


def vocab_grad_table_body(grad_ref, rows_ref, out_ref):
    out_ref[...] = plain(grad_ref[...], rows_ref[...]).astype(LOWER)


def vocab_grad_table(grad, rows):
    vocab, count = grad.shape
    tile = 2 * vocab_tile(count)
    return pl.pallas_call(
        vocab_grad_table_body,
        grid=(vocab // tile,),
        in_specs=[
            pl.BlockSpec((tile, count), lambda j: (j, 0)),
            pl.BlockSpec((count, D), lambda j: (0, 0)),
        ],
        out_specs=pl.BlockSpec((tile, D), lambda j: (j, 0)),
        out_shape=jax.ShapeDtypeStruct((vocab, D), LOWER),
        **params("vocab_grad_table", count * vocab * D, 2 * vocab * (count + D)),
    )(grad, rows)


def head_step(third, positions, targets, table_all, gain, own, n_dp):
    final, scale_three = norm_fwd(third, gain)
    tokens = third.shape[0]
    count = positions.shape[0]
    pick = positions[:, None] == jnp.arange(tokens, dtype=jnp.int32)[None, :]
    chosen = plain(pick.astype(LOWER), final.astype(LOWER)).astype(LOWER)
    near, far = gather_flips(chosen, n_dp)
    gathered = jnp.concatenate(near + far)
    aim = by_distance(targets, own).reshape(1, -1) - own * table_all.shape[0]
    expo, tops, stats = vocab_scores(gathered, table_all, aim)
    stats = by_distance(stats.reshape(8, n_dp, count).swapaxes(0, 1), own)
    stats = swap(jnp.broadcast_to(stats[None], (n_dp,) + stats.shape), "dp")
    high = jnp.max(stats[:, :, 0], 0)
    sums = jnp.sum(stats[:, :, 1] * jnp.exp(stats[:, :, 0] - high[None]), 0)
    lse = high + jnp.log(sums)
    lse = by_distance(lse, own)
    loss_part = jnp.sum(lse[0] - by_distance(jnp.sum(stats[:, :, 2], 0), own)[0]) / count
    lse = lse.reshape(1, 1, -1)
    scale = jnp.exp(tops - lse) / count
    grad_logits, grad_rows = vocab_grad_rows(expo, table_all, aim, scale, 1.0 / count)
    grad_rows = grad_rows.astype(LOWER)
    grad_chosen = sum_flips(cut(grad_rows, n_dp), n_dp)
    grad_table = vocab_grad_table(grad_logits, gathered)
    grad_chosen, grad_table = lax.optimization_barrier((grad_chosen, grad_table))
    grad_final = rows_high(pick.astype(WIDE), grad_chosen)
    grad_third, grad_gain = norm_back(third, scale_three, gain, grad_final)
    return (loss_part, grad_third, grad_gain, grad_table)


def layer_backward(hidden, grad_third, saved, w_qkv, w_attn, w_in, w_out, n_dp, place):
    shards = n_dp // EXPERTS
    gains, const_vec = saved["gains"], saved["const_vec"]
    router, const_gate = saved["router"], saved["const_gate"]
    tokens = hidden.shape[0]
    weight = saved["weight"]
    route_p = saved["route_p"]
    second_wide = saved["second_low"].astype(WIDE)
    w_slot, picks = saved["w_slot"], saved["picks"]
    grad_out = contract_rows(picks[0], (w_slot[:, 0:1] * grad_third).astype(LOWER))
    grad_out = grad_out + contract_rows(picks[1], (w_slot[:, 1:2] * grad_third).astype(LOWER))
    sent = send_slots(grad_out.astype(LOWER), n_dp, shards)
    near, far = saved["near"], saved["far"]
    near_back = experts_backward(sent[0], near[0], near[1], w_in, w_out)
    far_back = experts_backward(sent[1], far[0], far[1], w_in, w_out)
    came_back = return_slots(near_back[2], far_back[2], n_dp, shards)
    ends = (place, near, far, near_back, far_back)
    eout_g, came_back = sum_experts_out(*ends, came_back)
    dots = [jnp.sum(saved["outs"][k] * grad_third, -1, keepdims=True) for k in range(2)]
    hits = saved["hits"].astype(WIDE)
    grad_real = (dots[0] * hits[:, 0] + dots[1] * hits[:, 1])[:, :EXPERTS]
    grad_copy = jnp.sum(grad_third * saved["second"], -1, keepdims=True)
    grad_const = jnp.sum(grad_third[:, None, :] * saved["const_out"], -1)
    grad_weight = jnp.concatenate(
        [grad_real, jnp.zeros((tokens, 1), WIDE), grad_copy, grad_const], 1
    )
    grad_p = grad_weight * saved["used"]
    grad_logit = route_p * (grad_p - jnp.sum(route_p * grad_p, -1, keepdims=True))
    const_p = saved["const_p"]
    w_const = weight[:, EXPERTS + 2 :]
    along_vec = jnp.dot(grad_third, const_vec.T, precision=HIGH)
    grad_alpha = w_const[:, :, None] * jnp.stack(
        [jnp.broadcast_to(grad_copy, along_vec.shape), along_vec], -1
    )
    grad_clog = (const_p * (grad_alpha - jnp.sum(const_p * grad_alpha, -1, keepdims=True))).reshape(
        tokens, 4
    )
    grad_cvec = rows_high(w_const * const_p[:, :, 1], grad_third)
    logit_all = jnp.concatenate([grad_logit, grad_clog], 1)
    grad_gates = rows_high(logit_all, second_wide)
    gates_all = jnp.concatenate([router, const_gate], 0).astype(WIDE)
    grad_second = jnp.dot(logit_all, gates_all, precision=HIGH)
    carry = weight[:, EXPERTS + 1 : EXPERTS + 2] + jnp.sum(
        w_const * const_p[:, :, 0], -1, keepdims=True
    )
    grad_second = grad_second + carry * grad_third
    grad_second = grad_second + pick_slots(saved["both"], came_back)
    grad_first_norm, grad_gain_two = norm_back(
        saved["first"], saved["scale_two"], gains[1], grad_second
    )
    grad_first = grad_third + grad_first_norm
    grad_attn = grad_first.astype(LOWER)
    grad_mixed = plain(grad_attn, w_attn).astype(LOWER)
    grad_qkv = attend_back(saved["qkv"], grad_mixed, saved["segment"])
    grad_qkv, eout_g = lax.optimization_barrier((grad_qkv, eout_g))
    grad_normed = plain(grad_qkv, w_qkv)
    unused, grad_gain_one = norm_back(hidden, saved["scale_one"], gains[0], grad_normed)
    left = (grad_qkv, grad_attn)
    return (left, grad_gain_one, grad_gain_two, grad_cvec, grad_gates, ends, eout_g)


def fold(value):
    rows, cols = value.shape
    if rows % 8 or cols % LANES:
        return jnp.pad(jnp.sum(value * value)[None], (0, LANES - 1))
    squares = jnp.sum((value * value).reshape(rows // 8, 8, cols), 0)
    return jnp.sum(squares.reshape(8, cols // LANES, LANES), (0, 1))


def own_squares(arrays, device):
    dense, small = arrays
    width = dense.shape[1]
    front = (device * width + jnp.arange(width, dtype=jnp.int32) < 3 * D).astype(WIDE)
    lanes = (0, LANES - width)
    dense_sq = jnp.sum(dense * dense, 0)
    return [
        jnp.pad(dense_sq * front, lanes),
        jnp.pad(dense_sq * (1.0 - front), lanes),
        jnp.pad(jnp.sum(small[:5] * small[:5], 0), (0, LANES - small.shape[1])),
        jnp.pad(jnp.sum(small[5:] * small[5:], 0), (0, LANES - small.shape[1])),
    ]


def update_of(weight, first, second):
    corr = 1.0 - 0.5**STEP
    return first / corr / (jnp.sqrt(second / corr) + EPS) + 0.01 * weight


def moments(weight, first, second, grad):
    first = 0.5 * first + 0.5 * grad
    second = 0.5 * second + 0.5 * grad * grad
    return (first, second, update_of(weight, first, second))


def shared_update(weight, first, second, parts):
    first, second, update = moments(weight, first, second, add_up(parts))
    lanes = weight.shape[-1]
    return (first, second, fold(weight.reshape(-1, lanes)), fold(update.reshape(-1, lanes)))


def local(
    x_in,
    seq_lens,
    routes,
    positions,
    targets,
    dense_w,
    small_w,
    expert_in,
    expert_out,
    table,
    dense_m,
    small_m,
    expin_m,
    expout_m,
    table_m,
    dense_v,
    small_v,
    expin_v,
    expout_v,
    table_v,
):
    n_dp, n_rep = lax.axis_size("dp"), lax.axis_size("rep")
    devices = n_dp * n_rep
    own = lax.axis_index("dp")
    device = own * n_rep + lax.axis_index("rep")
    masters = (dense_w, small_w, expert_in, expert_out, table)
    width, thin = dense_w.shape[1], small_w.shape[1]
    place = jnp.stack([own, lax.axis_index("rep")]).astype(jnp.int32)
    flips = n_rep == 4 and width % 16 == 0 and thin % 8 == 0
    shared = (expert_in, expert_out, table)
    if flips:
        block, shared = lax.optimization_barrier((pack(dense_w, small_w), shared))
        w_qkv, w_attn, small_all = gather_weights(block, place, n_dp, width, thin)
    else:
        dense_t = lax.all_gather(dense_w.T.astype(LOWER), BOTH, axis=0, tiled=True)
        small_t = jnp.pad(small_w.T.astype(LOWER), ((0, 0), (0, LANES - small_w.shape[0])))
        small_all = share(small_t, BOTH, devices).reshape(-1, LANES).T
        w_qkv, w_attn = dense_t[: 3 * D], dense_t[3 * D :]
    w_in, w_out, table_all = (
        lax.all_gather(value.astype(LOWER), "rep", axis=axis, tiled=True)
        for value, axis in zip(shared, (1, 0, 0))
    )
    hidden = x_in.astype(WIDE)
    third, saved = layer_forward(
        hidden, seq_lens[0], routes, w_qkv, w_attn, small_all, w_in, w_out, own, n_dp
    )
    loss_part, grad_third, grad_gain_final, grad_table = head_step(
        third, positions, targets[0], table_all, saved["gains"][2], own, n_dp
    )
    table_g = lax.psum_scatter(grad_table, "rep", scatter_dimension=0, tiled=True)
    left, gain_one, gain_two, grad_cvec, grad_gates, ends, eout_g = layer_backward(
        hidden, grad_third, saved, w_qkv, w_attn, w_in, w_out, n_dp, place
    )
    small_grad = jnp.concatenate(
        [gain_one[None], gain_two[None], grad_gain_final[None], grad_cvec, grad_gates], 0
    )
    loss_row = jnp.pad(loss_part[None], (0, LANES - 1))

    def crossed(value):
        return flip(value, "rep", 2, 4) if n_rep == 4 else value

    def table_job(done):
        return shared_update(table, table_m, table_v, [table_g]), crossed(eout_g[-1])

    def out_job(done):
        made = shared_update(expert_out, expout_m, expout_v, eout_g[:-1] + [done[0][1]])
        if n_rep != 4:
            return made, None
        return made, crossed(ein_g[2][0])

    def in_job(done):
        parts = ein_g
        if n_rep == 4:
            parts = ein_g[:2] + [jnp.stack([done[1][1], crossed(ein_g[2][1])])]
        return shared_update(expert_in, expin_m, expin_v, parts), None

    jobs = (table_job, out_job, in_job)
    normed, mixed = saved["normed_low"], saved["mixed"]
    if flips:
        turned = jnp.pad(small_grad, ((0, LANES - small_grad.shape[0]), (0, 0))).T
        mine, other = dense_grads(place, *left, normed, mixed, turned, n_dp, width)
        ein_g, other = sum_experts_in(*ends, other)
        block, done = sum_weights(mine, other, n_dp, jobs)
        small_g = block[width:].reshape(8, -1, LANES)[:, : thin // 8].swapaxes(0, 1)
        small_g = small_g.reshape(thin, LANES)[:, : small_w.shape[0]].T
    else:
        dense_grad = jnp.concatenate(
            [contract_rows(left[0], normed), contract_rows(left[1], mixed)]
        )
        small_blocks = small_grad.reshape(-1, devices, thin).swapaxes(0, 1).reshape(devices, -1)
        extra = -(-small_blocks.shape[1] // (8 * D)) * 8 * D
        small_blocks = jnp.pad(small_blocks, ((0, 0), (0, extra - small_blocks.shape[1])))
        blocks = jnp.concatenate(
            [dense_grad.reshape(devices, width, D), small_blocks.reshape(devices, -1, D)], 1
        )
        block = scatter_sum(blocks.reshape((n_dp, n_rep) + blocks.shape[1:]), n_dp, n_rep)
        small_g = block[width:].reshape(-1)[: small_w.size].reshape(small_w.shape)
        ein_g, block = sum_experts_in(*ends, block)
        done = []
        for job in jobs:
            done.append(job(done))
    dense_g = block[:width].T
    own_results = [
        moments(w, m, v, g)
        for w, m, v, g in ((dense_w, dense_m, dense_v, dense_g), (small_w, small_m, small_v, small_g))
    ]
    made = [done[2][0], done[1][0], done[0][0]]
    rows = own_squares((dense_w, small_w), device) + [one[2] for one in made]
    rows = rows + own_squares([r[2] for r in own_results], device) + [one[3] for one in made]
    rows = jnp.stack(rows + [loss_row, loss_row * 0.0])
    sums = jnp.sum(share(rows, BOTH, devices), (0, 2))
    shared_results = [(m, v, update_of(w, m, v)) for w, (m, v, *_) in zip(masters[2:], made)]
    results = own_results + shared_results
    loss = sums[14]
    weight_sq, update_sq = sums[:7], sums[7:14]
    weight_norm = jnp.sqrt(weight_sq)
    update_norm = jnp.sqrt(update_sq)
    trust = weight_norm / update_norm
    column = device * width + jnp.arange(width, dtype=jnp.int32)
    dense_scale = jnp.where(column < 3 * D, trust[0], trust[1])[None, :]
    small_scale = jnp.where(jnp.arange(21, dtype=jnp.int32) < 5, trust[2], trust[3])[:, None]
    scales = (dense_scale, small_scale, trust[4], trust[5], trust[6])
    outs = [loss, jnp.stack([weight_norm, update_norm, trust])]
    for w, r, factor in zip(masters, results, scales):
        fresh = w - 0.2 * factor * r[2]
        outs += [r[0], r[1], fresh, fresh.astype(LOWER)]
    return tuple(outs)


def solution(mesh):
    in_specs = (
        P(("dp", "rep"), None),
        P(("dp", "rep"), None),
        P(("dp", "rep"), None),
        P(("dp", "rep")),
        P("rep", None, None),
        P(None, ("dp", "rep")),
        P(None, ("dp", "rep")),
        P(None, "rep", "dp"),
        P(("dp", "rep"), None),
        P(("dp", "rep"), None),
        P(None, ("dp", "rep")),
        P(None, ("dp", "rep")),
        P(None, "rep", "dp"),
        P(("dp", "rep"), None),
        P(("dp", "rep"), None),
        P(None, ("dp", "rep")),
        P(None, ("dp", "rep")),
        P(None, "rep", "dp"),
        P(("dp", "rep"), None),
        P(("dp", "rep"), None),
    )
    out_specs = (
        P(),
        P(),
        P(None, ("dp", "rep")),
        P(None, ("dp", "rep")),
        P(None, ("dp", "rep")),
        P(None, ("dp", "rep")),
        P(None, ("dp", "rep")),
        P(None, ("dp", "rep")),
        P(None, ("dp", "rep")),
        P(None, ("dp", "rep")),
        P(None, "rep", "dp"),
        P(None, "rep", "dp"),
        P(None, "rep", "dp"),
        P(None, "rep", "dp"),
        P(("dp", "rep"), None),
        P(("dp", "rep"), None),
        P(("dp", "rep"), None),
        P(("dp", "rep"), None),
        P(("dp", "rep"), None),
        P(("dp", "rep"), None),
        P(("dp", "rep"), None),
        P(("dp", "rep"), None),
    )
    return jax.shard_map(local, mesh=mesh, in_specs=in_specs, out_specs=out_specs, check_vma=False)
```

```python
import functools

import jax
import jax.numpy as jnp
from jax import lax
from jax.experimental import pallas as pl
from jax.experimental.pallas import tpu as pltpu
from jax.sharding import PartitionSpec as P

D = 768
HDIM = 64
EXPERTS = 8
NULLS = 4
STEP = 5
CAP = 96


EPS = 1e-06
HIGH = lax.Precision.HIGHEST
LOWER = jnp.bfloat16
WIDE = jnp.float32
BOTH = ("dp", "rep")
LANES = 128
MOST_FLIPS = 8
ROWS = 256
BAND = 256
VMEM_BYTES = 48 << 20


def params(name, products=0, moved=0, exps=0, room=None):
    return dict(
        compiler_params=pltpu.CompilerParams(vmem_limit_bytes=room or VMEM_BYTES),
        cost_estimate=pl.CostEstimate(
            flops=2 * products, bytes_accessed=moved, transcendentals=exps
        ),
        name=name,
    )


def contract_rows(left, right):
    return lax.dot_general(left, right, (((0,), (0,)), ((), ())), preferred_element_type=WIDE)


def contract_cols(left, right):
    return lax.dot_general(left, right, (((1,), (1,)), ((), ())), preferred_element_type=WIDE)


def plain(left, right):
    return jnp.dot(left, right, preferred_element_type=WIDE)


def rows_high(left, right):
    return lax.dot_general(left, right, (((0,), (0,)), ((), ())), precision=HIGH)


def swap(value, axis):
    return lax.all_to_all(value, axis, split_axis=0, concat_axis=0, tiled=True)


def share(value, axis, count):
    return swap(jnp.broadcast_to(value[None], (count,) + value.shape), axis)


def flip(value, axis, mask, size):
    return lax.ppermute(value, axis, [(i, i ^ mask) for i in range(size)])


def by_distance(value, own):
    shape = value.shape
    mask = 1
    while mask < shape[0]:
        pairs = value.reshape((shape[0] // (2 * mask), 2, mask) + shape[1:])
        value = jnp.where((own & mask) != 0, jnp.flip(pairs, 1), pairs).reshape(shape)
        mask *= 2
    return value


def trade(blocks, n_dp):
    if n_dp > MOST_FLIPS:
        own = lax.axis_index("dp")
        return list(by_distance(swap(by_distance(jnp.stack(blocks), own), "dp"), own))
    half = n_dp // 2
    far = [flip(blocks[m], "dp", m, n_dp) for m in range(half, n_dp)]
    return blocks[:1] + [flip(blocks[m], "dp", m, n_dp) for m in range(1, half)] + far


def gather_flips(block, n_dp):
    half = n_dp // 2
    if n_dp > MOST_FLIPS:
        pieces = list(by_distance(lax.all_gather(block, "dp"), lax.axis_index("dp")))
        return pieces[:half], pieces[half:]
    cross = flip(block, "dp", half, n_dp)
    near = [block] + [flip(block, "dp", m, n_dp) for m in range(1, half)]
    far = [cross] + [flip(cross, "dp", m, n_dp) for m in range(1, half)]
    return near, far


def sum_flips(parts, n_dp):
    half = n_dp // 2
    if n_dp > MOST_FLIPS:
        pieces = by_distance(jnp.stack(parts).astype(LOWER), lax.axis_index("dp"))
        return [jnp.sum(swap(pieces, "dp").astype(WIDE), 0)]
    aims = [flip(parts[half + m].astype(LOWER), "dp", m, n_dp) for m in range(1, half)]
    across = sum([a.astype(WIDE) for a in aims], parts[half].astype(WIDE)).astype(LOWER)
    cross = flip(across, "dp", half, n_dp)
    near = [flip(parts[m].astype(LOWER), "dp", m, n_dp) for m in range(1, half)]
    return [parts[0]] + near + [cross]


def halve(buffer, axis, mask, size):
    own = (lax.axis_index(axis) & mask) // mask
    halves = buffer.reshape((buffer.shape[0] // 2, 2) + buffer.shape[1:])
    keep = lax.dynamic_index_in_dim(halves, own, 1, keepdims=False)
    give = lax.dynamic_index_in_dim(halves, 1 - own, 1, keepdims=False).astype(LOWER)
    take = lax.ppermute(give, axis, [(i, i ^ mask) for i in range(size)])
    return keep + take.astype(WIDE)


def scatter_sum(blocks, n_dp, n_rep):
    value = blocks.swapaxes(0, 1)
    mask = 1
    while mask < n_rep:
        value = halve(value, "rep", mask, n_rep)
        mask *= 2
    value = value[0]
    mask = 1
    while mask < n_dp:
        value = halve(value, "dp", mask, n_dp)
        mask *= 2
    return value[0]


def pack_body(dense_ref, small_ref, out_ref):
    width = dense_ref.shape[1]
    rows, thin = small_ref.shape
    out_ref[:width, :] = dense_ref[...].T.astype(LOWER)
    out_ref[width:, :] = jnp.zeros((8, D), LOWER)
    turned = small_ref[...].T.astype(LOWER)
    for g in range(thin // 8):
        out_ref[width:, g * LANES : g * LANES + rows] = turned[g * 8 : g * 8 + 8, :]


def pack(dense_w, small_w):
    return pl.pallas_call(
        pack_body,
        out_shape=jax.ShapeDtypeStruct((dense_w.shape[1] + 8, D), LOWER),
        **params("pack", 0, 6 * dense_w.size),
    )(dense_w, small_w)


def assemble_body(place_ref, *refs, n_dp, width, thin):
    pieces = refs[: 2 * n_dp]
    qkv_ref, out_ref, small_ref, raw_ref, turned_ref, dense_sem, small_sem = refs[2 * n_dp :]
    own, rep = place_ref[0], place_ref[1]
    front = qkv_ref.shape[0]
    small_waits, dense_waits = [], []
    for m in range(n_dp):
        for pair in range(2):
            for core in range(2):
                piece = pieces[core * n_dp + m]
                device = (own ^ m) * 4 + (rep ^ (2 * pair + core))
                top = pair * (width + 8)
                number = m * 4 + pair * 2 + core
                small = pltpu.make_async_copy(
                    piece.at[pl.ds(top + width, 8), :], raw_ref.at[device], small_sem.at[number]
                )
                small.start()
                rows = piece.at[pl.ds(top, width), :]
                into_qkv = pltpu.make_async_copy(
                    rows, qkv_ref.at[jnp.minimum(device, front - 1)], dense_sem.at[number]
                )
                into_out = pltpu.make_async_copy(
                    rows, out_ref.at[jnp.maximum(device - front, 0)], dense_sem.at[number]
                )
                pl.when(device < front)(into_qkv.start)
                pl.when(device >= front)(into_out.start)
                small_waits.append(small)
                dense_waits.append(into_qkv)
    for copy in small_waits:
        copy.wait()
    for device in range(4 * n_dp):
        for g in range(thin // 8):
            start = device * thin + g * 8
            tile = raw_ref[device, :, g * LANES : (g + 1) * LANES]
            turned_ref[start : start + 8, :] = tile.astype(WIDE)
    small_ref[...] = turned_ref[...].T[: small_ref.shape[0], :]
    for copy in dense_waits:
        copy.wait()


def assemble(pieces, place, n_dp, width, thin):
    return pl.pallas_call(
        functools.partial(assemble_body, n_dp=n_dp, width=width, thin=thin),
        in_specs=[pl.BlockSpec(memory_space=pltpu.SMEM)]
        + [pl.BlockSpec(memory_space=pl.ANY)] * len(pieces),
        out_specs=[
            pl.BlockSpec(memory_space=pl.ANY),
            pl.BlockSpec(memory_space=pl.ANY),
            pl.BlockSpec(memory_space=pltpu.VMEM),
        ],
        out_shape=[
            jax.ShapeDtypeStruct((3 * n_dp, width, D), LOWER),
            jax.ShapeDtypeStruct((n_dp, width, D), LOWER),
            jax.ShapeDtypeStruct((24, D), WIDE),
        ],
        scratch_shapes=[
            pltpu.VMEM((4 * n_dp, 8, D), LOWER),
            pltpu.VMEM((4 * n_dp * thin, LANES), WIDE),
            pltpu.SemaphoreType.DMA((4 * n_dp,)),
            pltpu.SemaphoreType.DMA((4 * n_dp,)),
        ],
        **params("assemble", 0, 32 * n_dp * width * D, room=48 << 20),
    )(place, *pieces)


def gather_weights(block, place, n_dp, width, thin):
    both = jnp.concatenate([block, flip(block, "rep", 2, 4)])
    near, far = gather_flips(both, n_dp)
    mine = near + far
    theirs = [flip(piece, "rep", 1, 4) for piece in mine]
    qkv, out, small = assemble(mine + theirs, place, n_dp, width, thin)
    return qkv.reshape(-1, D), out.reshape(-1, D), small


def dense_grad_body(
    place_ref, qkv_ref, attn_ref, normed_ref, mixed_ref, small_ref, mine_ref, other_ref, sum_ref
):
    j = pl.program_id(0)
    width, thin = mine_ref.shape[2] - 8, small_ref.shape[0] // (4 * pl.num_programs(0))
    front = 3 * D // (4 * width)

    @pl.when(j < front)
    def _():
        sum_ref[...] = contract_rows(qkv_ref[...], normed_ref[...])

    @pl.when(j >= front)
    def _():
        sum_ref[...] = contract_rows(attn_ref[...], mixed_ref[...])

    rep = place_ref[1]
    for pair in range(2):
        for core, out_ref in enumerate((mine_ref, other_ref)):
            r = rep ^ (2 * pair + core)
            rows = pl.multiple_of(r * width, 8)
            out_ref[0, pair, :width, :] = sum_ref[pl.ds(rows, width), :].astype(out_ref.dtype)
            out_ref[0, pair, width:, :] = jnp.zeros((8, D), out_ref.dtype)
            for g in range(thin // 8):
                start = pl.multiple_of((j * 4 + r) * thin + g * 8, 8)
                tile = small_ref[pl.ds(start, 8), :].astype(out_ref.dtype)
                out_ref[0, pair, width:, g * LANES : (g + 1) * LANES] = tile


def dense_grads(place, grad_qkv, grad_attn, normed, mixed, small_turned, n_dp, width):
    tokens = grad_qkv.shape[0]
    wide = 4 * width
    front = 3 * D // wide
    block = (1, 2, width + 8, D)
    whole = lambda shape: pl.BlockSpec(shape, lambda j, place: (0, 0))
    out_spec = pl.BlockSpec(block, lambda j, place: (j ^ place[0], 0, 0, 0))
    return pl.pallas_call(
        dense_grad_body,
        grid_spec=pltpu.PrefetchScalarGridSpec(
            num_scalar_prefetch=1,
            grid=(n_dp,),
            in_specs=[
                pl.BlockSpec((tokens, wide), lambda j, place: (0, jnp.minimum(j, front - 1))),
                pl.BlockSpec((tokens, wide), lambda j, place: (0, jnp.maximum(j - front, 0))),
                whole((tokens, D)),
                whole((tokens, D)),
                whole(small_turned.shape),
            ],
            out_specs=[out_spec, out_spec],
            scratch_shapes=[pltpu.VMEM((wide, D), WIDE)],
        ),
        out_shape=[jax.ShapeDtypeStruct((n_dp,) + block[1:], LOWER)] * 2,
        **params("dense_grads", tokens * 4 * D * D, 12 * tokens * D + 24 * D * D),
    )(place, grad_qkv, grad_attn, normed, mixed, small_turned)


def sum_weights(mine, other, n_dp, jobs):
    both = flip(other, "rep", 1, 4)
    parts = [mine[m].astype(WIDE) + both[m].astype(WIDE) for m in range(n_dp)]
    done = []

    def beside(value, job):
        value, result = lax.optimization_barrier((value, job(done)))
        done.append(result)
        return value

    if n_dp > MOST_FLIPS:
        pair = beside(beside(add_up(sum_flips(parts, n_dp)), jobs[0]), jobs[1])
    else:
        half = n_dp // 2
        aims = [flip(parts[half + m].astype(LOWER), "dp", m, n_dp) for m in range(1, half)]
        near = [flip(parts[m].astype(LOWER), "dp", m, n_dp) for m in range(1, half)]
        aims, near = beside((aims, near), jobs[0])
        cross = flip(add_up([parts[half]] + aims).astype(LOWER), "dp", half, n_dp)
        cross = beside(cross, jobs[1])
        pair = add_up([parts[0]] + near + [cross])
    far = beside(flip(pair[1].astype(LOWER), "rep", 2, 4), jobs[2])
    return pair[0] + far.astype(WIDE), done


def norm_fwd(hidden, gain):
    scale = lax.rsqrt(jnp.mean(hidden * hidden, -1, keepdims=True) + EPS)
    return (hidden * scale * gain, scale)


def norm_back(hidden, scale, gain, grad_out):
    normed = hidden * scale
    grad_gain = jnp.sum(grad_out * normed, 0)
    inner = grad_out * gain
    grad_in = scale * (inner - normed * jnp.mean(inner * normed, -1, keepdims=True))
    return (grad_in, grad_gain)


def segments(lens, tokens):
    place = jnp.arange(tokens, dtype=jnp.int32)
    ends = [jnp.sum(lens[: i + 1]) for i in range(lens.shape[0])]
    return sum((place >= end).astype(jnp.int32) for end in ends)


def build_bias(bias_ref, key_dim):
    shape = bias_ref.shape
    query = lax.broadcasted_iota(jnp.int32, shape, 1 - key_dim)
    key = lax.broadcasted_iota(jnp.int32, shape, key_dim)
    return key <= query


def lane_masks():
    lane = lax.broadcasted_iota(jnp.int32, (1, 2 * HDIM), 1)
    low = (lane < HDIM).astype(WIDE)
    return (low.astype(LOWER), (1.0 - low).astype(LOWER))


def attend_body(seg_col, seg_row, q_ref, k_ref, v_ref, out_ref, bias_ref):
    tokens = q_ref.shape[0]

    @pl.when(pl.program_id(0) == 0)
    def _():
        counts = build_bias(bias_ref, 1) & (seg_col[...] == seg_row[...])
        bias_ref[...] = jnp.where(counts, 0.0, -1e30)

    masks = lane_masks()
    for start in range(0, tokens, BAND):
        keys = start + BAND
        k = k_ref[:keys, :]
        v = v_ref[:keys, :]
        q = q_ref[start : start + BAND, :]
        acc = jnp.zeros((BAND, 2 * HDIM), WIDE)
        for mine in masks:
            scores = contract_cols(q * mine, k) * HDIM ** (-0.5)
            scores = scores + bias_ref[start : start + BAND, :keys]
            expo = jnp.exp(scores - jnp.max(scores, -1, keepdims=True))
            total = jnp.sum(expo, -1, keepdims=True)
            probs = (expo * (1.0 / total)).astype(LOWER)
            acc = acc + plain(probs, v * mine)
        out_ref[start : start + BAND, :] = acc.astype(LOWER)


def head_specs(tokens, first):
    return [
        pl.BlockSpec((tokens, 2 * HDIM), lambda j, base=base: (0, base + j)) for base in first
    ]


def attend(qkv, segment):
    tokens = qkv.shape[0]
    pairs = D // (2 * HDIM)
    return pl.pallas_call(
        attend_body,
        grid=(pairs,),
        in_specs=[
            pl.BlockSpec((tokens, 1), lambda j: (0, 0)),
            pl.BlockSpec((1, tokens), lambda j: (0, 0)),
        ]
        + head_specs(tokens, (0, pairs, 2 * pairs)),
        out_specs=pl.BlockSpec((tokens, 2 * HDIM), lambda j: (0, j)),
        out_shape=jax.ShapeDtypeStruct((tokens, D), LOWER),
        scratch_shapes=[pltpu.VMEM((tokens, tokens), WIDE)],
        **params("attend", 2 * tokens * tokens * D, 8 * tokens * D, tokens * tokens * D // HDIM),
    )(segment[:, None], segment[None, :], qkv, qkv, qkv)


def attend_back_body(seg_col, seg_row, q_ref, k_ref, v_ref, do_ref, out_ref, bias_ref):
    tokens = q_ref.shape[0]
    step = pl.program_id(0)

    @pl.when(step == 0)
    def _():
        counts = build_bias(bias_ref, 0) & (seg_col[...] == seg_row[...])
        bias_ref[...] = jnp.where(counts, 0.0, -1e30)

    masks = lane_masks()
    scale = HDIM ** (-0.5)
    grad_k = [jnp.zeros((BAND, 2 * HDIM), WIDE) for _ in range(tokens // BAND)]
    grad_v = [jnp.zeros((BAND, 2 * HDIM), WIDE) for _ in range(tokens // BAND)]
    col = pl.multiple_of(step * 2 * HDIM, 2 * HDIM)
    for block, start in enumerate(range(0, tokens, BAND)):
        keys = start + BAND
        k = k_ref[:keys, :]
        v = v_ref[:keys, :]
        q = q_ref[start : start + BAND, :]
        do = do_ref[start : start + BAND, :]
        grad_q = jnp.zeros((BAND, 2 * HDIM), WIDE)
        for mine in masks:
            q_own = q * mine
            do_own = do * mine
            scores = contract_cols(k, q_own) * scale + bias_ref[:keys, start : start + BAND]
            expo = jnp.exp(scores - jnp.max(scores, 0, keepdims=True))
            total = jnp.sum(expo, 0, keepdims=True)
            probs = expo * (1.0 / total)
            grad_p = contract_cols(v, do_own)
            inner = jnp.sum(probs * grad_p, 0, keepdims=True)
            grad_s = (probs * (grad_p - inner)).astype(LOWER)
            grad_q = grad_q + contract_rows(grad_s, k * mine)
            into_v = plain(probs.astype(LOWER), do_own)
            into_k = plain(grad_s, q_own)
            for b in range(block + 1):
                grad_v[b] = grad_v[b] + into_v[b * BAND : (b + 1) * BAND]
                grad_k[b] = grad_k[b] + into_k[b * BAND : (b + 1) * BAND]
        out_ref[start : start + BAND, pl.ds(col, 2 * HDIM)] = (grad_q * scale).astype(LOWER)
    for b in range(tokens // BAND):
        rows = slice(b * BAND, (b + 1) * BAND)
        out_ref[rows, pl.ds(D + col, 2 * HDIM)] = (grad_k[b] * scale).astype(LOWER)
        out_ref[rows, pl.ds(2 * D + col, 2 * HDIM)] = grad_v[b].astype(LOWER)


def attend_back(qkv, grad_mixed, segment):
    tokens = qkv.shape[0]
    pairs = D // (2 * HDIM)
    return pl.pallas_call(
        attend_back_body,
        grid=(pairs,),
        in_specs=[
            pl.BlockSpec((tokens, 1), lambda j: (0, 0)),
            pl.BlockSpec((1, tokens), lambda j: (0, 0)),
        ]
        + head_specs(tokens, (0, pairs, 2 * pairs))
        + head_specs(tokens, (0,)),
        out_specs=pl.BlockSpec((tokens, 3 * D), lambda j: (0, 0)),
        out_shape=jax.ShapeDtypeStruct((tokens, 3 * D), LOWER),
        scratch_shapes=[pltpu.VMEM((tokens, tokens), WIDE)],
        **params("attend_back", 5 * tokens * tokens * D, 14 * tokens * D, tokens * tokens * D // HDIM),
    )(segment[:, None], segment[None, :], qkv, qkv, qkv, grad_mixed)


def full(shape):
    return pl.BlockSpec(shape, lambda *index: (0,) * len(shape))


def experts_forward_body(*refs):
    (*pieces, w_in_ref, w_out_ref, gate_ref, up_ref, inner_ref, rows_ref), rest = (
        refs[: len(refs) // 2 + 3],
        refs[len(refs) // 2 + 3 :],
    )
    *parts, acc_ref = rest
    j = pl.program_id(0)

    @pl.when(j == 0)
    def _():
        for i, piece in enumerate(pieces):
            rows_ref[i * CAP : (i + 1) * CAP, :] = piece[...]
        acc_ref[...] = jnp.zeros(acc_ref.shape, WIDE)

    rows = rows_ref[...]
    gate = plain(rows, w_in_ref[0])
    up = plain(rows, w_in_ref[1])
    inner = (jax.nn.silu(gate) * up).astype(LOWER)
    gate_ref[...] = gate
    up_ref[...] = up
    inner_ref[...] = inner
    acc_ref[...] += plain(inner, w_out_ref[...])

    @pl.when(j == pl.num_programs(0) - 1)
    def _():
        for i, part in enumerate(parts):
            part[...] = acc_ref[i * CAP : (i + 1) * CAP, :].astype(LOWER)


def experts_forward(pieces, w_in, w_out):
    rows, hidden = len(pieces) * CAP, w_out.shape[0]
    tile = min(hidden, 512)
    piece = full((CAP, D))
    band = pl.BlockSpec((rows, tile), lambda j: (0, j))
    gate, up, inner, joined, *parts = pl.pallas_call(
        experts_forward_body,
        grid=(hidden // tile,),
        in_specs=[piece] * len(pieces)
        + [
            pl.BlockSpec((2, D, tile), lambda j: (0, 0, j)),
            pl.BlockSpec((tile, D), lambda j: (j, 0)),
        ],
        out_specs=[band, band, band, full((rows, D))] + [piece] * len(pieces),
        out_shape=[
            jax.ShapeDtypeStruct((rows, hidden), WIDE),
            jax.ShapeDtypeStruct((rows, hidden), WIDE),
            jax.ShapeDtypeStruct((rows, hidden), LOWER),
            jax.ShapeDtypeStruct((rows, D), LOWER),
        ]
        + [jax.ShapeDtypeStruct((CAP, D), LOWER)] * len(pieces),
        scratch_shapes=[pltpu.VMEM((rows, D), WIDE)],
        **params("experts_forward", 3 * rows * hidden * D, 6 * hidden * D + 10 * rows * hidden),
    )(*pieces, w_in, w_out)
    return gate, up, inner, joined, parts


def experts_backward_body(*refs):
    count = (len(refs) - 7) // 2
    pieces, refs = refs[:count], refs[count:]
    gate_ref, up_ref, w_in_ref, w_out_ref, backs_ref, rows_ref, *parts, acc_ref = refs
    j = pl.program_id(0)

    @pl.when(j == 0)
    def _():
        for i, piece in enumerate(pieces):
            rows_ref[i * CAP : (i + 1) * CAP, :] = piece[...]
        acc_ref[...] = jnp.zeros(acc_ref.shape, WIDE)

    grad_inner = contract_cols(rows_ref[...], w_out_ref[...])
    gate, up = gate_ref[...], up_ref[...]
    sig = jax.nn.sigmoid(gate)
    grad_gate = (grad_inner * up * sig * (1.0 + gate * (1.0 - sig))).astype(LOWER)
    grad_up = (grad_inner * gate * sig).astype(LOWER)
    backs_ref[0] = grad_gate
    backs_ref[1] = grad_up
    acc_ref[...] += contract_cols(grad_gate, w_in_ref[0]) + contract_cols(grad_up, w_in_ref[1])

    @pl.when(j == pl.num_programs(0) - 1)
    def _():
        for i, part in enumerate(parts):
            part[...] = acc_ref[i * CAP : (i + 1) * CAP, :].astype(LOWER)


def experts_backward(pieces, gate, up, w_in, w_out):
    rows, hidden = gate.shape
    tile = min(hidden, 512)
    piece = full((CAP, D))
    band = pl.BlockSpec((rows, tile), lambda j: (0, j))
    backs, joined, *parts = pl.pallas_call(
        experts_backward_body,
        grid=(hidden // tile,),
        in_specs=[piece] * len(pieces)
        + [
            band,
            band,
            pl.BlockSpec((2, D, tile), lambda j: (0, 0, j)),
            pl.BlockSpec((tile, D), lambda j: (j, 0)),
        ],
        out_specs=[pl.BlockSpec((2, rows, tile), lambda j: (0, 0, j)), full((rows, D))]
        + [piece] * len(pieces),
        out_shape=[
            jax.ShapeDtypeStruct((2, rows, hidden), LOWER),
            jax.ShapeDtypeStruct((rows, D), LOWER),
        ]
        + [jax.ShapeDtypeStruct((CAP, D), LOWER)] * len(pieces),
        scratch_shapes=[pltpu.VMEM((rows, D), WIDE)],
        **params("experts_backward", 3 * rows * hidden * D, 6 * hidden * D + 12 * rows * hidden),
    )(*pieces, gate, up, w_in, w_out)
    return backs, joined, parts


def grads_in_body(
    place_ref, rows_a, rows_b, back_a, back_b, keep_ref, give_ref, sum_ref, turned_ref, back_ref
):
    rows = rows_a.shape[0]

    @pl.when((pl.program_id(0) == 0) & (pl.program_id(1) == 0))
    def _():
        turned_ref[:, :rows] = rows_a[...].T
        turned_ref[:, rows:] = rows_b[...].T

    back_ref[:rows, :] = back_a[0]
    back_ref[rows:, :] = back_b[0]
    sum_ref[...] = plain(turned_ref[...], back_ref[...])
    size = keep_ref.shape[2]
    for pair in range(2):
        for core, out_ref in enumerate((keep_ref, give_ref)):
            start = pl.multiple_of((place_ref[1] ^ (2 * pair + core)) * size, 8)
            out_ref[0, pair] = sum_ref[pl.ds(start, size), :].astype(LOWER)


def grads_in(place, rows_a, rows_b, back_a, back_b):
    rows, hidden = back_a.shape[1:]
    tile = 512
    size = D // 4
    back = pl.BlockSpec((1, rows, tile), lambda k, j, place: (k, 0, j))
    out = pl.BlockSpec((1, 2, size, tile), lambda k, j, place: (k, 0, 0, j))
    return pl.pallas_call(
        grads_in_body,
        grid_spec=pltpu.PrefetchScalarGridSpec(
            num_scalar_prefetch=1,
            grid=(2, hidden // tile),
            in_specs=[full((rows, D)), full((rows, D)), back, back],
            out_specs=[out, out],
            scratch_shapes=[
                pltpu.VMEM((D, tile), WIDE),
                pltpu.VMEM((D, 2 * rows), LOWER),
                pltpu.VMEM((2 * rows, tile), LOWER),
            ],
        ),
        out_shape=[jax.ShapeDtypeStruct((2, 2, size, hidden), LOWER)] * 2,
        **params("grads_in", 4 * rows * hidden * D, 4 * hidden * D + 8 * rows * hidden),
    )(place, rows_a, rows_b, back_a, back_b)


def grads_out_body(place_ref, inner_a, inner_b, back_a, back_b, out_ref):
    total = contract_rows(inner_a[...], back_a[...]) + contract_rows(inner_b[...], back_b[...])
    out_ref[0] = total.astype(LOWER)


def grads_out(place, core, inner_a, inner_b, back_a, back_b):
    rows, hidden = inner_a.shape
    size = hidden // 4
    band = pl.BlockSpec((rows, size), lambda x, place: (0, place[1] ^ (2 * x + core)))
    return pl.pallas_call(
        grads_out_body,
        grid_spec=pltpu.PrefetchScalarGridSpec(
            num_scalar_prefetch=1,
            grid=(2,),
            in_specs=[band, band, full((rows, D)), full((rows, D))],
            out_specs=pl.BlockSpec((1, size, D), lambda x, place: (x, 0, 0)),
        ),
        out_shape=jax.ShapeDtypeStruct((2, size, D), LOWER),
        **params("grads_out", rows * hidden * D, hidden * D + 2 * rows * hidden),
    )(place, inner_a, inner_b, back_a, back_b)


def sum_experts_out(place, near, far, near_back, far_back, came_back):
    if lax.axis_size("rep") != 4:
        grad = contract_rows(
            jnp.concatenate([near[2], far[2]]), jnp.concatenate([near_back[1], far_back[1]])
        ).astype(LOWER)
        return [lax.psum_scatter(grad, "rep", scatter_dimension=0, tiled=True)], came_back
    half = len(came_back) // 2
    arrived, rows = lax.optimization_barrier((came_back[:half], (near_back[1], far_back[1])))
    came_back = arrived + came_back[half:]
    ends = (near[2], far[2]) + rows
    give, keep = grads_out(place, 1, *ends), grads_out(place, 0, *ends)
    came_back, give, keep = lax.optimization_barrier((came_back, give, keep))
    take = flip(give, "rep", 1, 4)
    return [keep[0], take[0], (keep[1].astype(WIDE) + take[1].astype(WIDE)).astype(LOWER)], came_back


def sum_experts_in(place, near, far, near_back, far_back, after, eout_g):
    if lax.axis_size("rep") != 4:
        rows = jnp.concatenate([near[3], far[3]])
        backs = jnp.concatenate([near_back[0], far_back[0]], 1)
        grad = jnp.stack([contract_rows(rows, back).astype(LOWER) for back in backs])
        return [lax.psum_scatter(grad, "rep", scatter_dimension=1, tiled=True)], after, eout_g
    after, backs = lax.optimization_barrier((after, (near_back[0], far_back[0])))
    keep, give = grads_in(place, near[3], far[3], *backs)
    crossed = flip(eout_g[2], "rep", 2, 4)
    give, crossed = lax.optimization_barrier((give, crossed))
    take = flip(give, "rep", 1, 4)
    far = [(keep[k, 1].astype(WIDE) + take[k, 1].astype(WIDE)).astype(LOWER) for k in range(2)]
    return [keep[:, 0], take[:, 0], far], after, eout_g[:2] + [crossed]


def add_up(parts):
    return sum([part.astype(WIDE) for part in parts[1:]], parts[0].astype(WIDE))


def cut(value, count):
    size = value.shape[0] // count
    return [value[i * size : (i + 1) * size] for i in range(count)]


def send_slots(buffer, n_dp, shards):
    half = n_dp // 2
    blocks = trade([b for b in buffer for _ in range(shards)], n_dp)
    return blocks[:half], blocks[half:]


def return_slots(near, far, n_dp, shards):
    blocks = trade(list(near) + list(far), n_dp)
    return [jnp.concatenate(blocks[s::shards]) for s in range(shards)]


def pick_slots(picks, received):
    return sum(plain(picks, part) for part in received)


def layer_forward(hidden, lens, routes, w_qkv, w_attn, small_all, w_in, w_out, own, n_dp):
    shards = n_dp // EXPERTS
    gains, const_vec, router, const_gate = (
        small_all[:3].astype(WIDE),
        small_all[3:5].astype(WIDE),
        small_all[5:17].astype(LOWER),
        small_all[17:21].astype(LOWER),
    )
    tokens = hidden.shape[0]
    segment = segments(lens, tokens)
    normed, scale_one = norm_fwd(hidden, gains[0])
    normed_low = normed.astype(LOWER)
    qkv = contract_cols(normed_low, w_qkv).astype(LOWER)
    mixed = attend(qkv, segment)
    first = hidden + contract_cols(mixed, w_attn)
    second, scale_two = norm_fwd(first, gains[1])
    second_low = second.astype(LOWER)
    route_p = jax.nn.softmax(contract_cols(second_low, router), -1)
    hits = routes[:, :, None] == jnp.arange(EXPERTS + NULLS, dtype=jnp.int32)[None, None, :]
    used = jnp.sum(hits.astype(WIDE), 1)
    weight = route_p * used
    earlier = jnp.tril(jnp.ones((tokens, tokens), LOWER), -1)
    rank = plain(earlier, used[:, :EXPERTS].astype(LOWER)).astype(jnp.int32)
    apart = jnp.arange(EXPERTS, dtype=jnp.int32) ^ (own // shards)
    place = apart[None] * CAP + rank
    place = jnp.where(rank < CAP, place, -1)
    real_hits = hits[:, :, :EXPERTS]
    slot = jnp.max(jnp.where(real_hits, place[:, None, :], -1), -1)
    w_slot = jnp.sum(jnp.where(real_hits, weight[:, None, :EXPERTS], 0.0), -1)
    all_slots = jnp.arange(EXPERTS * CAP, dtype=jnp.int32)
    picks = [(slot[:, k : k + 1] == all_slots[None]).astype(LOWER) for k in range(2)]
    both = picks[0] + picks[1]
    buffer = contract_rows(both, second_low).astype(LOWER)
    sent = send_slots(cut(buffer, EXPERTS), n_dp, shards)
    near, far = (experts_forward(rows, w_in, w_out) for rows in sent)
    returned = return_slots(near[4], far[4], n_dp, shards)
    outs = [pick_slots(picks[k], returned) for k in range(2)]
    moe = w_slot[:, 0:1] * outs[0] + w_slot[:, 1:2] * outs[1]
    const_p = jax.nn.softmax(contract_cols(second_low, const_gate).reshape(tokens, 2, 2), -1)
    const_out = const_p[:, :, 0:1] * second[:, None, :] + const_p[:, :, 1:2] * const_vec[None]
    moe = moe + weight[:, EXPERTS + 1 : EXPERTS + 2] * second
    moe = (
        moe
        + weight[:, EXPERTS + 2 : EXPERTS + 3] * const_out[:, 0]
        + weight[:, EXPERTS + 3 :] * const_out[:, 1]
    )
    third = first + moe
    saved = dict(
        gains=gains,
        const_vec=const_vec,
        router=router,
        const_gate=const_gate,
        segment=segment,
        scale_one=scale_one,
        normed_low=normed_low,
        qkv=qkv,
        mixed=mixed,
        first=first,
        second=second,
        scale_two=scale_two,
        second_low=second_low,
        route_p=route_p,
        hits=hits,
        used=used,
        weight=weight,
        w_slot=w_slot,
        slot=slot,
        picks=picks,
        both=both,
        near=near,
        far=far,
        outs=outs,
        const_p=const_p,
        const_out=const_out,
    )
    return (third, saved)


def vocab_tile(rows):
    return min(1024, (1 << 20) // rows)


def scores_body(aim_ref, rows_ref, table_ref, expo_ref, tops_ref, stats_ref, *, step_rows):
    tile = table_ref.shape[0]
    j = pl.program_id(0)

    @pl.when(j == 0)
    def _():
        stats_ref[0:1, :] = jnp.full((1, stats_ref.shape[1]), -1e30, WIDE)
        stats_ref[1:8, :] = jnp.zeros((7, stats_ref.shape[1]), WIDE)

    table = table_ref[...]
    for start in range(0, rows_ref.shape[0], step_rows):
        cols = slice(start, start + step_rows)
        logits = contract_cols(table, rows_ref[cols, :])
        top = jnp.max(logits, 0, keepdims=True)
        expo = jnp.exp(logits - top)
        expo_ref[:, cols] = expo.astype(LOWER)
        total = jnp.sum(expo, 0, keepdims=True)
        place = lax.broadcasted_iota(jnp.int32, logits.shape, 0)
        hit = place == aim_ref[:, cols] - j * tile
        aimed = jnp.sum(jnp.where(hit, logits, 0.0), 0, keepdims=True)
        tops_ref[0, :, cols] = top
        old = stats_ref[0:1, cols]
        high = jnp.maximum(old, top)
        stats_ref[1:2, cols] = stats_ref[1:2, cols] * jnp.exp(old - high) + total * jnp.exp(
            top - high
        )
        stats_ref[0:1, cols] = high
        stats_ref[2:3, cols] = stats_ref[2:3, cols] + aimed


def vocab_scores(rows, table, aim):
    count, vocab = rows.shape[0], table.shape[0]
    tile = vocab_tile(count)
    steps = vocab // tile
    return pl.pallas_call(
        functools.partial(scores_body, step_rows=ROWS),
        grid=(steps,),
        in_specs=[
            pl.BlockSpec((1, count), lambda j: (0, 0)),
            pl.BlockSpec((count, D), lambda j: (0, 0)),
            pl.BlockSpec((tile, D), lambda j: (j, 0)),
        ],
        out_specs=[
            pl.BlockSpec((tile, count), lambda j: (j, 0)),
            pl.BlockSpec((1, 1, count), lambda j: (j, 0, 0)),
            pl.BlockSpec((8, count), lambda j: (0, 0)),
        ],
        out_shape=[
            jax.ShapeDtypeStruct((vocab, count), LOWER),
            jax.ShapeDtypeStruct((steps, 1, count), WIDE),
            jax.ShapeDtypeStruct((8, count), WIDE),
        ],
        **params("vocab_scores", count * vocab * D, 2 * vocab * (count + D), count * vocab),
    )(aim, rows, table)


def dlogits_body(aim_ref, scale_ref, expo_ref, table_ref, grad_ref, out_ref, *, step_rows, unit):
    tile = table_ref.shape[0]
    j = pl.program_id(0)

    @pl.when(j == 0)
    def _():
        out_ref[...] = jnp.zeros(out_ref.shape, WIDE)

    table = table_ref[...]
    for start in range(0, expo_ref.shape[1], step_rows):
        cols = slice(start, start + step_rows)
        expo = expo_ref[:, cols].astype(WIDE)
        place = lax.broadcasted_iota(jnp.int32, expo.shape, 0)
        hit = place == aim_ref[:, cols] - j * tile
        grad = (expo * scale_ref[0, :, cols] - jnp.where(hit, unit, 0.0)).astype(LOWER)
        grad_ref[:, cols] = grad
        out_ref[cols, :] += contract_rows(grad, table)


def vocab_grad_rows(expo, table, aim, scale, unit):
    vocab, count = expo.shape
    tile = vocab_tile(count)
    steps = vocab // tile
    return pl.pallas_call(
        functools.partial(dlogits_body, step_rows=ROWS, unit=unit),
        grid=(steps,),
        in_specs=[
            pl.BlockSpec((1, count), lambda j: (0, 0)),
            pl.BlockSpec((1, 1, count), lambda j: (j, 0, 0)),
            pl.BlockSpec((tile, count), lambda j: (j, 0)),
            pl.BlockSpec((tile, D), lambda j: (j, 0)),
        ],
        out_specs=[
            pl.BlockSpec((tile, count), lambda j: (j, 0)),
            pl.BlockSpec((count, D), lambda j: (0, 0)),
        ],
        out_shape=[
            jax.ShapeDtypeStruct((vocab, count), LOWER),
            jax.ShapeDtypeStruct((count, D), WIDE),
        ],
        **params("vocab_grad_rows", count * vocab * D, 2 * vocab * (2 * count + D)),
    )(aim, scale, expo, table)


def vocab_grad_table_body(grad_ref, rows_ref, out_ref):
    out_ref[...] = plain(grad_ref[...], rows_ref[...]).astype(LOWER)


def vocab_grad_table(grad, rows):
    vocab, count = grad.shape
    tile = 2 * vocab_tile(count)
    return pl.pallas_call(
        vocab_grad_table_body,
        grid=(vocab // tile,),
        in_specs=[
            pl.BlockSpec((tile, count), lambda j: (j, 0)),
            pl.BlockSpec((count, D), lambda j: (0, 0)),
        ],
        out_specs=pl.BlockSpec((tile, D), lambda j: (j, 0)),
        out_shape=jax.ShapeDtypeStruct((vocab, D), LOWER),
        **params("vocab_grad_table", count * vocab * D, 2 * vocab * (count + D)),
    )(grad, rows)


def head_step(third, positions, targets, table_all, gain, own, n_dp):
    final, unused = norm_fwd(third, gain)
    tokens = third.shape[0]
    count = positions.shape[0]
    pick = positions[:, None] == jnp.arange(tokens, dtype=jnp.int32)[None, :]
    chosen = plain(pick.astype(LOWER), final.astype(LOWER)).astype(LOWER)
    near, far = gather_flips(chosen, n_dp)
    gathered = jnp.concatenate(near + far)
    aim = by_distance(targets, own).reshape(1, -1) - own * table_all.shape[0]
    expo, tops, stats = vocab_scores(gathered, table_all, aim)
    stats = by_distance(stats.reshape(8, n_dp, count).swapaxes(0, 1), own)
    stats = swap(jnp.broadcast_to(stats[None], (n_dp,) + stats.shape), "dp")
    high = jnp.max(stats[:, :, 0], 0)
    sums = jnp.sum(stats[:, :, 1] * jnp.exp(stats[:, :, 0] - high[None]), 0)
    lse = high + jnp.log(sums)
    lse = by_distance(lse, own)
    loss_part = jnp.sum(lse[0] - by_distance(jnp.sum(stats[:, :, 2], 0), own)[0]) / count
    lse = lse.reshape(1, 1, -1)
    scale = jnp.exp(tops - lse) / count
    grad_logits, grad_rows = vocab_grad_rows(expo, table_all, aim, scale, 1.0 / count)
    grad_rows = grad_rows.astype(LOWER)
    grad_chosen = sum_flips(cut(grad_rows, n_dp), n_dp)
    grad_table = vocab_grad_table(grad_logits, gathered)
    grad_chosen, grad_table = lax.optimization_barrier((grad_chosen, grad_table))
    return (loss_part, grad_chosen, grad_table)


def head_back_body(*refs, count):
    terms, refs = refs[:count], refs[count:]
    spot_ref, slot_ref, third_ref, gain_ref, w_ref, grad_ref, gain_grad_ref, *blocks = refs
    tokens = third_ref.shape[0]
    total = terms[0][...].astype(WIDE)
    for term in terms[1:]:
        total = total + term[...].astype(WIDE)
    spots = spot_ref[...] == lax.broadcasted_iota(jnp.int32, (tokens, total.shape[0]), 0)
    spots = spots.astype(WIDE).astype(LOWER)
    grad = jnp.zeros(third_ref.shape, WIDE)
    for _ in range(3):
        piece = total.astype(LOWER)
        total = total - piece.astype(WIDE)
        grad = grad + plain(spots, piece)
    third = third_ref[...]
    scale = lax.rsqrt(jnp.mean(third * third, -1, keepdims=True) + EPS)
    normed = third * scale
    gain_grad_ref[...] = jnp.sum(grad * normed, 0, keepdims=True)
    inner = grad * gain_ref[...]
    grad = scale * (inner - normed * jnp.mean(inner * normed, -1, keepdims=True))
    grad_ref[...] = grad
    out = jnp.zeros((EXPERTS * CAP, D), WIDE)
    places = lax.broadcasted_iota(jnp.int32, (EXPERTS * CAP, tokens), 0)
    for k in range(2):
        picks = (slot_ref[k : k + 1, :] == places).astype(WIDE).astype(LOWER)
        out = out + plain(picks, (w_ref[:, k : k + 1] * grad).astype(LOWER))
    for e, block in enumerate(blocks):
        block[...] = out[e * CAP : (e + 1) * CAP, :].astype(LOWER)


def head_back(terms, positions, slot, third, gain, w_slot):
    tokens = third.shape[0]
    grad_third, grad_gain, *blocks = pl.pallas_call(
        functools.partial(head_back_body, count=len(terms)),
        out_shape=[
            jax.ShapeDtypeStruct((tokens, D), WIDE),
            jax.ShapeDtypeStruct((1, D), WIDE),
        ]
        + [jax.ShapeDtypeStruct((CAP, D), LOWER)] * EXPERTS,
        **params("head_back", 2 * tokens * EXPERTS * CAP * D, 12 * tokens * D),
    )(*terms, positions[None, :], slot.T, third, gain[None, :], w_slot)
    return grad_third, grad_gain[0], blocks


def layer_backward(hidden, grad_third, saved, w_qkv, w_attn, w_in, w_out, n_dp, place, blocks):
    shards = n_dp // EXPERTS
    gains, const_vec = saved["gains"], saved["const_vec"]
    router, const_gate = saved["router"], saved["const_gate"]
    tokens = hidden.shape[0]
    weight = saved["weight"]
    route_p = saved["route_p"]
    second_wide = saved["second_low"].astype(WIDE)
    sent = send_slots(blocks, n_dp, shards)
    near, far = saved["near"], saved["far"]
    near_back = experts_backward(sent[0], near[0], near[1], w_in, w_out)
    far_back = experts_backward(sent[1], far[0], far[1], w_in, w_out)
    blocks = trade(list(near_back[2]) + list(far_back[2]), n_dp)
    ends = (place, near, far, near_back, far_back)
    eout_g, blocks = sum_experts_out(*ends, blocks)
    came_back = [jnp.concatenate(blocks[s::shards]) for s in range(shards)]
    dots = [jnp.sum(saved["outs"][k] * grad_third, -1, keepdims=True) for k in range(2)]
    hits = saved["hits"].astype(WIDE)
    grad_real = (dots[0] * hits[:, 0] + dots[1] * hits[:, 1])[:, :EXPERTS]
    grad_copy = jnp.sum(grad_third * saved["second"], -1, keepdims=True)
    grad_const = jnp.sum(grad_third[:, None, :] * saved["const_out"], -1)
    grad_weight = jnp.concatenate(
        [grad_real, jnp.zeros((tokens, 1), WIDE), grad_copy, grad_const], 1
    )
    grad_p = grad_weight * saved["used"]
    grad_logit = route_p * (grad_p - jnp.sum(route_p * grad_p, -1, keepdims=True))
    const_p = saved["const_p"]
    w_const = weight[:, EXPERTS + 2 :]
    along_vec = jnp.dot(grad_third, const_vec.T, precision=HIGH)
    grad_alpha = w_const[:, :, None] * jnp.stack(
        [jnp.broadcast_to(grad_copy, along_vec.shape), along_vec], -1
    )
    grad_clog = (const_p * (grad_alpha - jnp.sum(const_p * grad_alpha, -1, keepdims=True))).reshape(
        tokens, 4
    )
    grad_cvec = rows_high(w_const * const_p[:, :, 1], grad_third)
    logit_all = jnp.concatenate([grad_logit, grad_clog], 1)
    grad_gates = rows_high(logit_all, second_wide)
    gates_all = jnp.concatenate([router, const_gate], 0).astype(WIDE)
    grad_second = jnp.dot(logit_all, gates_all, precision=HIGH)
    carry = weight[:, EXPERTS + 1 : EXPERTS + 2] + jnp.sum(
        w_const * const_p[:, :, 0], -1, keepdims=True
    )
    grad_second = grad_second + carry * grad_third
    grad_second = grad_second + pick_slots(saved["both"], came_back)
    grad_first_norm, grad_gain_two = norm_back(
        saved["first"], saved["scale_two"], gains[1], grad_second
    )
    grad_first = grad_third + grad_first_norm
    grad_attn = grad_first.astype(LOWER)
    grad_mixed = plain(grad_attn, w_attn).astype(LOWER)
    grad_qkv = attend_back(saved["qkv"], grad_mixed, saved["segment"])
    grad_qkv, eout_g = lax.optimization_barrier((grad_qkv, eout_g))
    grad_normed = plain(grad_qkv, w_qkv)
    unused, grad_gain_one = norm_back(hidden, saved["scale_one"], gains[0], grad_normed)
    left = (grad_qkv, grad_attn)
    return (left, grad_gain_one, grad_gain_two, grad_cvec, grad_gates, ends, eout_g)


def fold(value):
    rows, cols = value.shape
    if rows % 8 or cols % LANES:
        return jnp.pad(jnp.sum(value * value)[None], (0, LANES - 1))
    squares = jnp.sum((value * value).reshape(rows // 8, 8, cols), 0)
    return jnp.sum(squares.reshape(8, cols // LANES, LANES), (0, 1))


def own_squares(arrays, device):
    dense, small = arrays
    width = dense.shape[1]
    front = (device * width + jnp.arange(width, dtype=jnp.int32) < 3 * D).astype(WIDE)
    lanes = (0, LANES - width)
    dense_sq = jnp.sum(dense * dense, 0)
    return [
        jnp.pad(dense_sq * front, lanes),
        jnp.pad(dense_sq * (1.0 - front), lanes),
        jnp.pad(jnp.sum(small[:5] * small[:5], 0), (0, LANES - small.shape[1])),
        jnp.pad(jnp.sum(small[5:] * small[5:], 0), (0, LANES - small.shape[1])),
    ]


def update_of(weight, first, second):
    corr = 1.0 - 0.5**STEP
    return first / corr / (jnp.sqrt(second / corr) + EPS) + 0.01 * weight


def moments(weight, first, second, grad):
    first = 0.5 * first + 0.5 * grad
    second = 0.5 * second + 0.5 * grad * grad
    return (first, second, update_of(weight, first, second))


def shared_update(weight, first, second, parts):
    first, second, update = moments(weight, first, second, add_up(parts))
    lanes = weight.shape[-1]
    return (first, second, fold(weight.reshape(-1, lanes)), fold(update.reshape(-1, lanes)))


def local(
    x_in,
    seq_lens,
    routes,
    positions,
    targets,
    dense_w,
    small_w,
    expert_in,
    expert_out,
    table,
    dense_m,
    small_m,
    expin_m,
    expout_m,
    table_m,
    dense_v,
    small_v,
    expin_v,
    expout_v,
    table_v,
):
    n_dp, n_rep = lax.axis_size("dp"), lax.axis_size("rep")
    devices = n_dp * n_rep
    own = lax.axis_index("dp")
    device = own * n_rep + lax.axis_index("rep")
    masters = (dense_w, small_w, expert_in, expert_out, table)
    width, thin = dense_w.shape[1], small_w.shape[1]
    place = jnp.stack([own, lax.axis_index("rep")]).astype(jnp.int32)
    flips = n_rep == 4 and width % 16 == 0 and thin % 8 == 0
    shared = (expert_in, expert_out, table)
    if flips:
        block, shared = lax.optimization_barrier((pack(dense_w, small_w), shared))
        w_qkv, w_attn, small_all = gather_weights(block, place, n_dp, width, thin)
    else:
        dense_t = lax.all_gather(dense_w.T.astype(LOWER), BOTH, axis=0, tiled=True)
        small_t = jnp.pad(small_w.T.astype(LOWER), ((0, 0), (0, LANES - small_w.shape[0])))
        small_all = share(small_t, BOTH, devices).reshape(-1, LANES).T
        w_qkv, w_attn = dense_t[: 3 * D], dense_t[3 * D :]
    w_in, w_out, table_all = (
        lax.all_gather(value.astype(LOWER), "rep", axis=axis, tiled=True)
        for value, axis in zip(shared, (1, 0, 0))
    )
    hidden = x_in.astype(WIDE)
    third, saved = layer_forward(
        hidden, seq_lens[0], routes, w_qkv, w_attn, small_all, w_in, w_out, own, n_dp
    )
    loss_part, terms, grad_table = head_step(
        third, positions, targets[0], table_all, saved["gains"][2], own, n_dp
    )
    grad_third, grad_gain_final, blocks = head_back(
        terms, positions, saved["slot"], third, saved["gains"][2], saved["w_slot"]
    )
    table_g = lax.psum_scatter(grad_table, "rep", scatter_dimension=0, tiled=True)
    left, gain_one, gain_two, grad_cvec, grad_gates, ends, eout_g = layer_backward(
        hidden, grad_third, saved, w_qkv, w_attn, w_in, w_out, n_dp, place, blocks
    )
    small_grad = jnp.concatenate(
        [gain_one[None], gain_two[None], grad_gain_final[None], grad_cvec, grad_gates], 0
    )
    loss_row = jnp.pad(loss_part[None], (0, LANES - 1))

    def crossed(value):
        return flip(value, "rep", 2, 4) if n_rep == 4 else value

    def table_job(done):
        made = shared_update(table, table_m, table_v, [table_g])
        return made, (crossed(ein_g[2][0]) if n_rep == 4 else None)

    def out_job(done):
        made = shared_update(expert_out, expout_m, expout_v, eout_g)
        return made, (crossed(ein_g[2][1]) if n_rep == 4 else None)

    def in_job(done):
        parts = ein_g
        if n_rep == 4:
            parts = ein_g[:2] + [jnp.stack([done[0][1], done[1][1]])]
        return shared_update(expert_in, expin_m, expin_v, parts), None

    jobs = (table_job, out_job, in_job)
    normed, mixed = saved["normed_low"], saved["mixed"]
    if flips:
        turned = jnp.pad(small_grad, ((0, LANES - small_grad.shape[0]), (0, 0))).T
        mine, other = dense_grads(place, *left, normed, mixed, turned, n_dp, width)
        ein_g, other, eout_g = sum_experts_in(*ends, other, eout_g)
        block, done = sum_weights(mine, other, n_dp, jobs)
        small_g = block[width:].reshape(8, -1, LANES)[:, : thin // 8].swapaxes(0, 1)
        small_g = small_g.reshape(thin, LANES)[:, : small_w.shape[0]].T
    else:
        dense_grad = jnp.concatenate(
            [contract_rows(left[0], normed), contract_rows(left[1], mixed)]
        )
        small_blocks = small_grad.reshape(-1, devices, thin).swapaxes(0, 1).reshape(devices, -1)
        extra = -(-small_blocks.shape[1] // (8 * D)) * 8 * D
        small_blocks = jnp.pad(small_blocks, ((0, 0), (0, extra - small_blocks.shape[1])))
        blocks = jnp.concatenate(
            [dense_grad.reshape(devices, width, D), small_blocks.reshape(devices, -1, D)], 1
        )
        block = scatter_sum(blocks.reshape((n_dp, n_rep) + blocks.shape[1:]), n_dp, n_rep)
        small_g = block[width:].reshape(-1)[: small_w.size].reshape(small_w.shape)
        ein_g, block, eout_g = sum_experts_in(*ends, block, eout_g)
        done = []
        for job in jobs:
            done.append(job(done))
    dense_g = block[:width].T
    own_results = [
        moments(w, m, v, g)
        for w, m, v, g in ((dense_w, dense_m, dense_v, dense_g), (small_w, small_m, small_v, small_g))
    ]
    made = [done[2][0], done[1][0], done[0][0]]
    rows = own_squares((dense_w, small_w), device) + [one[2] for one in made]
    rows = rows + own_squares([r[2] for r in own_results], device) + [one[3] for one in made]
    rows = jnp.stack(rows + [loss_row, loss_row * 0.0])
    sums = jnp.sum(share(rows, BOTH, devices), (0, 2))
    shared_results = [(m, v, update_of(w, m, v)) for w, (m, v, *_) in zip(masters[2:], made)]
    results = own_results + shared_results
    loss = sums[14]
    weight_sq, update_sq = sums[:7], sums[7:14]
    weight_norm = jnp.sqrt(weight_sq)
    update_norm = jnp.sqrt(update_sq)
    trust = weight_norm / update_norm
    column = device * width + jnp.arange(width, dtype=jnp.int32)
    dense_scale = jnp.where(column < 3 * D, trust[0], trust[1])[None, :]
    small_scale = jnp.where(jnp.arange(21, dtype=jnp.int32) < 5, trust[2], trust[3])[:, None]
    scales = (dense_scale, small_scale, trust[4], trust[5], trust[6])
    outs = [loss, jnp.stack([weight_norm, update_norm, trust])]
    for w, r, factor in zip(masters, results, scales):
        fresh = w - 0.2 * factor * r[2]
        outs += [r[0], r[1], fresh, fresh.astype(LOWER)]
    return tuple(outs)


def solution(mesh):
    in_specs = (
        P(("dp", "rep"), None),
        P(("dp", "rep"), None),
        P(("dp", "rep"), None),
        P(("dp", "rep")),
        P("rep", None, None),
        P(None, ("dp", "rep")),
        P(None, ("dp", "rep")),
        P(None, "rep", "dp"),
        P(("dp", "rep"), None),
        P(("dp", "rep"), None),
        P(None, ("dp", "rep")),
        P(None, ("dp", "rep")),
        P(None, "rep", "dp"),
        P(("dp", "rep"), None),
        P(("dp", "rep"), None),
        P(None, ("dp", "rep")),
        P(None, ("dp", "rep")),
        P(None, "rep", "dp"),
        P(("dp", "rep"), None),
        P(("dp", "rep"), None),
    )
    out_specs = (
        P(),
        P(),
        P(None, ("dp", "rep")),
        P(None, ("dp", "rep")),
        P(None, ("dp", "rep")),
        P(None, ("dp", "rep")),
        P(None, ("dp", "rep")),
        P(None, ("dp", "rep")),
        P(None, ("dp", "rep")),
        P(None, ("dp", "rep")),
        P(None, "rep", "dp"),
        P(None, "rep", "dp"),
        P(None, "rep", "dp"),
        P(None, "rep", "dp"),
        P(("dp", "rep"), None),
        P(("dp", "rep"), None),
        P(("dp", "rep"), None),
        P(("dp", "rep"), None),
        P(("dp", "rep"), None),
        P(("dp", "rep"), None),
        P(("dp", "rep"), None),
        P(("dp", "rep"), None),
    )
    return jax.shard_map(local, mesh=mesh, in_specs=in_specs, out_specs=out_specs, check_vma=False)
```

```python
import functools

import jax
import jax.numpy as jnp
from jax import lax
from jax.experimental import pallas as pl
from jax.experimental.pallas import tpu as pltpu
from jax.sharding import PartitionSpec as P

D = 768
HDIM = 64
EXPERTS = 8
NULLS = 4
STEP = 5
CAP = 96


EPS = 1e-06
HIGH = lax.Precision.HIGHEST
LOWER = jnp.bfloat16
WIDE = jnp.float32
BOTH = ("dp", "rep")
LANES = 128
MOST_FLIPS = 8
ROWS = 256
BAND = 256
VMEM_BYTES = 48 << 20


def params(name, products=0, moved=0, exps=0, room=None):
    return dict(
        compiler_params=pltpu.CompilerParams(vmem_limit_bytes=room or VMEM_BYTES),
        cost_estimate=pl.CostEstimate(
            flops=2 * products, bytes_accessed=moved, transcendentals=exps
        ),
        name=name,
    )


def contract_rows(left, right):
    return lax.dot_general(left, right, (((0,), (0,)), ((), ())), preferred_element_type=WIDE)


def contract_cols(left, right):
    return lax.dot_general(left, right, (((1,), (1,)), ((), ())), preferred_element_type=WIDE)


def plain(left, right):
    return jnp.dot(left, right, preferred_element_type=WIDE)


def rows_high(left, right):
    return lax.dot_general(left, right, (((0,), (0,)), ((), ())), precision=HIGH)


def swap(value, axis):
    return lax.all_to_all(value, axis, split_axis=0, concat_axis=0, tiled=True)


def share(value, axis, count):
    return swap(jnp.broadcast_to(value[None], (count,) + value.shape), axis)


def flip(value, axis, mask, size):
    return lax.ppermute(value, axis, [(i, i ^ mask) for i in range(size)])


def by_distance(value, own):
    shape = value.shape
    mask = 1
    while mask < shape[0]:
        pairs = value.reshape((shape[0] // (2 * mask), 2, mask) + shape[1:])
        value = jnp.where((own & mask) != 0, jnp.flip(pairs, 1), pairs).reshape(shape)
        mask *= 2
    return value


def trade(blocks, n_dp):
    if n_dp > MOST_FLIPS:
        own = lax.axis_index("dp")
        return list(by_distance(swap(by_distance(jnp.stack(blocks), own), "dp"), own))
    half = n_dp // 2
    far = [flip(blocks[m], "dp", m, n_dp) for m in range(half, n_dp)]
    return blocks[:1] + [flip(blocks[m], "dp", m, n_dp) for m in range(1, half)] + far


def gather_flips(block, n_dp):
    half = n_dp // 2
    if n_dp > MOST_FLIPS:
        pieces = list(by_distance(lax.all_gather(block, "dp"), lax.axis_index("dp")))
        return pieces[:half], pieces[half:]
    cross = flip(block, "dp", half, n_dp)
    near = [block] + [flip(block, "dp", m, n_dp) for m in range(1, half)]
    far = [cross] + [flip(cross, "dp", m, n_dp) for m in range(1, half)]
    return near, far


def sum_flips(parts, n_dp):
    half = n_dp // 2
    if n_dp > MOST_FLIPS:
        pieces = by_distance(jnp.stack(parts).astype(LOWER), lax.axis_index("dp"))
        return [jnp.sum(swap(pieces, "dp").astype(WIDE), 0)]
    aims = [flip(parts[half + m].astype(LOWER), "dp", m, n_dp) for m in range(1, half)]
    across = sum([a.astype(WIDE) for a in aims], parts[half].astype(WIDE)).astype(LOWER)
    cross = flip(across, "dp", half, n_dp)
    near = [flip(parts[m].astype(LOWER), "dp", m, n_dp) for m in range(1, half)]
    return [parts[0]] + near + [cross]


def halve(buffer, axis, mask, size):
    own = (lax.axis_index(axis) & mask) // mask
    halves = buffer.reshape((buffer.shape[0] // 2, 2) + buffer.shape[1:])
    keep = lax.dynamic_index_in_dim(halves, own, 1, keepdims=False)
    give = lax.dynamic_index_in_dim(halves, 1 - own, 1, keepdims=False).astype(LOWER)
    take = lax.ppermute(give, axis, [(i, i ^ mask) for i in range(size)])
    return keep + take.astype(WIDE)


def scatter_sum(blocks, n_dp, n_rep):
    value = blocks.swapaxes(0, 1)
    mask = 1
    while mask < n_rep:
        value = halve(value, "rep", mask, n_rep)
        mask *= 2
    value = value[0]
    mask = 1
    while mask < n_dp:
        value = halve(value, "dp", mask, n_dp)
        mask *= 2
    return value[0]


def pack_body(dense_ref, small_ref, out_ref):
    width = dense_ref.shape[1]
    rows, thin = small_ref.shape
    out_ref[:width, :] = dense_ref[...].T.astype(LOWER)
    out_ref[width:, :] = jnp.zeros((8, D), LOWER)
    turned = small_ref[...].T.astype(LOWER)
    for g in range(thin // 8):
        out_ref[width:, g * LANES : g * LANES + rows] = turned[g * 8 : g * 8 + 8, :]


def pack(dense_w, small_w):
    return pl.pallas_call(
        pack_body,
        out_shape=jax.ShapeDtypeStruct((dense_w.shape[1] + 8, D), LOWER),
        **params("pack", 0, 6 * dense_w.size),
    )(dense_w, small_w)


def assemble_body(place_ref, *refs, n_dp, width, thin):
    pieces = refs[: 2 * n_dp]
    qkv_ref, out_ref, small_ref, raw_ref, turned_ref, dense_sem, small_sem = refs[2 * n_dp :]
    own, rep = place_ref[0], place_ref[1]
    front = qkv_ref.shape[0]
    small_waits, dense_waits = [], []
    for m in range(n_dp):
        for pair in range(2):
            for core in range(2):
                piece = pieces[core * n_dp + m]
                device = (own ^ m) * 4 + (rep ^ (2 * pair + core))
                top = pair * (width + 8)
                number = m * 4 + pair * 2 + core
                small = pltpu.make_async_copy(
                    piece.at[pl.ds(top + width, 8), :], raw_ref.at[device], small_sem.at[number]
                )
                small.start()
                rows = piece.at[pl.ds(top, width), :]
                into_qkv = pltpu.make_async_copy(
                    rows, qkv_ref.at[jnp.minimum(device, front - 1)], dense_sem.at[number]
                )
                into_out = pltpu.make_async_copy(
                    rows, out_ref.at[jnp.maximum(device - front, 0)], dense_sem.at[number]
                )
                pl.when(device < front)(into_qkv.start)
                pl.when(device >= front)(into_out.start)
                small_waits.append(small)
                dense_waits.append(into_qkv)
    for copy in small_waits:
        copy.wait()
    for device in range(4 * n_dp):
        for g in range(thin // 8):
            start = device * thin + g * 8
            tile = raw_ref[device, :, g * LANES : (g + 1) * LANES]
            turned_ref[start : start + 8, :] = tile.astype(WIDE)
    small_ref[...] = turned_ref[...].T[: small_ref.shape[0], :]
    for copy in dense_waits:
        copy.wait()


def assemble(pieces, place, n_dp, width, thin):
    return pl.pallas_call(
        functools.partial(assemble_body, n_dp=n_dp, width=width, thin=thin),
        in_specs=[pl.BlockSpec(memory_space=pltpu.SMEM)]
        + [pl.BlockSpec(memory_space=pl.ANY)] * len(pieces),
        out_specs=[
            pl.BlockSpec(memory_space=pl.ANY),
            pl.BlockSpec(memory_space=pl.ANY),
            pl.BlockSpec(memory_space=pltpu.VMEM),
        ],
        out_shape=[
            jax.ShapeDtypeStruct((3 * n_dp, width, D), LOWER),
            jax.ShapeDtypeStruct((n_dp, width, D), LOWER),
            jax.ShapeDtypeStruct((24, D), WIDE),
        ],
        scratch_shapes=[
            pltpu.VMEM((4 * n_dp, 8, D), LOWER),
            pltpu.VMEM((4 * n_dp * thin, LANES), WIDE),
            pltpu.SemaphoreType.DMA((4 * n_dp,)),
            pltpu.SemaphoreType.DMA((4 * n_dp,)),
        ],
        **params("assemble", 0, 32 * n_dp * width * D, room=48 << 20),
    )(place, *pieces)


def gather_weights(block, place, n_dp, width, thin):
    both = jnp.concatenate([block, flip(block, "rep", 2, 4)])
    near, far = gather_flips(both, n_dp)
    mine = near + far
    theirs = [flip(piece, "rep", 1, 4) for piece in mine]
    qkv, out, small = assemble(mine + theirs, place, n_dp, width, thin)
    return qkv.reshape(-1, D), out.reshape(-1, D), small


def dense_grad_body(
    place_ref, qkv_ref, attn_ref, normed_ref, mixed_ref, small_ref, mine_ref, other_ref, sum_ref
):
    j = pl.program_id(0)
    width, thin = mine_ref.shape[2] - 8, small_ref.shape[0] // (4 * pl.num_programs(0))
    front = 3 * D // (4 * width)

    @pl.when(j < front)
    def _():
        sum_ref[...] = contract_rows(qkv_ref[...], normed_ref[...])

    @pl.when(j >= front)
    def _():
        sum_ref[...] = contract_rows(attn_ref[...], mixed_ref[...])

    rep = place_ref[1]
    for pair in range(2):
        for core, out_ref in enumerate((mine_ref, other_ref)):
            r = rep ^ (2 * pair + core)
            rows = pl.multiple_of(r * width, 8)
            out_ref[0, pair, :width, :] = sum_ref[pl.ds(rows, width), :].astype(out_ref.dtype)
            out_ref[0, pair, width:, :] = jnp.zeros((8, D), out_ref.dtype)
            for g in range(thin // 8):
                start = pl.multiple_of((j * 4 + r) * thin + g * 8, 8)
                tile = small_ref[pl.ds(start, 8), :].astype(out_ref.dtype)
                out_ref[0, pair, width:, g * LANES : (g + 1) * LANES] = tile


def dense_grads(place, grad_qkv, grad_attn, normed, mixed, small_turned, n_dp, width):
    tokens = grad_qkv.shape[0]
    wide = 4 * width
    front = 3 * D // wide
    block = (1, 2, width + 8, D)
    whole = lambda shape: pl.BlockSpec(shape, lambda j, place: (0, 0))
    out_spec = pl.BlockSpec(block, lambda j, place: (j ^ place[0], 0, 0, 0))
    return pl.pallas_call(
        dense_grad_body,
        grid_spec=pltpu.PrefetchScalarGridSpec(
            num_scalar_prefetch=1,
            grid=(n_dp,),
            in_specs=[
                pl.BlockSpec((tokens, wide), lambda j, place: (0, jnp.minimum(j, front - 1))),
                pl.BlockSpec((tokens, wide), lambda j, place: (0, jnp.maximum(j - front, 0))),
                whole((tokens, D)),
                whole((tokens, D)),
                whole(small_turned.shape),
            ],
            out_specs=[out_spec, out_spec],
            scratch_shapes=[pltpu.VMEM((wide, D), WIDE)],
        ),
        out_shape=[jax.ShapeDtypeStruct((n_dp,) + block[1:], LOWER)] * 2,
        **params("dense_grads", tokens * 4 * D * D, 12 * tokens * D + 24 * D * D),
    )(place, grad_qkv, grad_attn, normed, mixed, small_turned)


def sum_weights(mine, other, n_dp, jobs):
    both = flip(other, "rep", 1, 4)
    parts = [mine[m].astype(WIDE) + both[m].astype(WIDE) for m in range(n_dp)]
    done = []

    def beside(value, job):
        value, result = lax.optimization_barrier((value, job(done)))
        done.append(result)
        return value

    if n_dp > MOST_FLIPS:
        pair = beside(beside(add_up(sum_flips(parts, n_dp)), jobs[0]), jobs[1])
    else:
        half = n_dp // 2
        aims = [flip(parts[half + m].astype(LOWER), "dp", m, n_dp) for m in range(1, half)]
        near = [flip(parts[m].astype(LOWER), "dp", m, n_dp) for m in range(1, half)]
        aims, near = beside((aims, near), jobs[0])
        cross = flip(add_up([parts[half]] + aims).astype(LOWER), "dp", half, n_dp)
        cross = beside(cross, jobs[1])
        pair = add_up([parts[0]] + near + [cross])
    far = beside(flip(pair[1].astype(LOWER), "rep", 2, 4), jobs[2])
    return pair[0] + far.astype(WIDE), done


def norm_fwd(hidden, gain):
    scale = lax.rsqrt(jnp.mean(hidden * hidden, -1, keepdims=True) + EPS)
    return (hidden * scale * gain, scale)


def norm_back(hidden, scale, gain, grad_out):
    normed = hidden * scale
    grad_gain = jnp.sum(grad_out * normed, 0)
    inner = grad_out * gain
    grad_in = scale * (inner - normed * jnp.mean(inner * normed, -1, keepdims=True))
    return (grad_in, grad_gain)


def segments(lens, tokens):
    place = jnp.arange(tokens, dtype=jnp.int32)
    ends = [jnp.sum(lens[: i + 1]) for i in range(lens.shape[0])]
    return sum((place >= end).astype(jnp.int32) for end in ends)


def build_bias(bias_ref, key_dim):
    shape = bias_ref.shape
    query = lax.broadcasted_iota(jnp.int32, shape, 1 - key_dim)
    key = lax.broadcasted_iota(jnp.int32, shape, key_dim)
    return key <= query


def lane_masks():
    lane = lax.broadcasted_iota(jnp.int32, (1, 2 * HDIM), 1)
    low = (lane < HDIM).astype(WIDE)
    return (low.astype(LOWER), (1.0 - low).astype(LOWER))


def attend_body(seg_col, seg_row, q_ref, k_ref, v_ref, out_ref, bias_ref):
    tokens = q_ref.shape[0]

    @pl.when(pl.program_id(0) == 0)
    def _():
        counts = build_bias(bias_ref, 1) & (seg_col[...] == seg_row[...])
        bias_ref[...] = jnp.where(counts, 0.0, -1e30)

    masks = lane_masks()
    for start in range(0, tokens, BAND):
        keys = start + BAND
        k = k_ref[:keys, :]
        v = v_ref[:keys, :]
        q = q_ref[start : start + BAND, :]
        acc = jnp.zeros((BAND, 2 * HDIM), WIDE)
        for mine in masks:
            scores = contract_cols(q * mine, k) * HDIM ** (-0.5)
            scores = scores + bias_ref[start : start + BAND, :keys]
            expo = jnp.exp(scores - jnp.max(scores, -1, keepdims=True))
            total = jnp.sum(expo, -1, keepdims=True)
            probs = (expo * (1.0 / total)).astype(LOWER)
            acc = acc + plain(probs, v * mine)
        out_ref[start : start + BAND, :] = acc.astype(LOWER)


def head_specs(tokens, first):
    return [
        pl.BlockSpec((tokens, 2 * HDIM), lambda j, base=base: (0, base + j)) for base in first
    ]


def attend(qkv, segment):
    tokens = qkv.shape[0]
    pairs = D // (2 * HDIM)
    return pl.pallas_call(
        attend_body,
        grid=(pairs,),
        in_specs=[
            pl.BlockSpec((tokens, 1), lambda j: (0, 0)),
            pl.BlockSpec((1, tokens), lambda j: (0, 0)),
        ]
        + head_specs(tokens, (0, pairs, 2 * pairs)),
        out_specs=pl.BlockSpec((tokens, 2 * HDIM), lambda j: (0, j)),
        out_shape=jax.ShapeDtypeStruct((tokens, D), LOWER),
        scratch_shapes=[pltpu.VMEM((tokens, tokens), WIDE)],
        **params("attend", 2 * tokens * tokens * D, 8 * tokens * D, tokens * tokens * D // HDIM),
    )(segment[:, None], segment[None, :], qkv, qkv, qkv)


def attend_back_body(seg_col, seg_row, q_ref, k_ref, v_ref, do_ref, out_ref, bias_ref):
    tokens = q_ref.shape[0]
    step = pl.program_id(0)

    @pl.when(step == 0)
    def _():
        counts = build_bias(bias_ref, 0) & (seg_col[...] == seg_row[...])
        bias_ref[...] = jnp.where(counts, 0.0, -1e30)

    masks = lane_masks()
    scale = HDIM ** (-0.5)
    grad_k = [jnp.zeros((BAND, 2 * HDIM), WIDE) for _ in range(tokens // BAND)]
    grad_v = [jnp.zeros((BAND, 2 * HDIM), WIDE) for _ in range(tokens // BAND)]
    col = pl.multiple_of(step * 2 * HDIM, 2 * HDIM)
    for block, start in enumerate(range(0, tokens, BAND)):
        keys = start + BAND
        k = k_ref[:keys, :]
        v = v_ref[:keys, :]
        q = q_ref[start : start + BAND, :]
        do = do_ref[start : start + BAND, :]
        grad_q = jnp.zeros((BAND, 2 * HDIM), WIDE)
        for mine in masks:
            q_own = q * mine
            do_own = do * mine
            scores = contract_cols(k, q_own) * scale + bias_ref[:keys, start : start + BAND]
            expo = jnp.exp(scores - jnp.max(scores, 0, keepdims=True))
            total = jnp.sum(expo, 0, keepdims=True)
            probs = expo * (1.0 / total)
            grad_p = contract_cols(v, do_own)
            inner = jnp.sum(probs * grad_p, 0, keepdims=True)
            grad_s = (probs * (grad_p - inner)).astype(LOWER)
            grad_q = grad_q + contract_rows(grad_s, k * mine)
            into_v = plain(probs.astype(LOWER), do_own)
            into_k = plain(grad_s, q_own)
            for b in range(block + 1):
                grad_v[b] = grad_v[b] + into_v[b * BAND : (b + 1) * BAND]
                grad_k[b] = grad_k[b] + into_k[b * BAND : (b + 1) * BAND]
        out_ref[start : start + BAND, pl.ds(col, 2 * HDIM)] = (grad_q * scale).astype(LOWER)
    for b in range(tokens // BAND):
        rows = slice(b * BAND, (b + 1) * BAND)
        out_ref[rows, pl.ds(D + col, 2 * HDIM)] = (grad_k[b] * scale).astype(LOWER)
        out_ref[rows, pl.ds(2 * D + col, 2 * HDIM)] = grad_v[b].astype(LOWER)


def attend_back(qkv, grad_mixed, segment):
    tokens = qkv.shape[0]
    pairs = D // (2 * HDIM)
    return pl.pallas_call(
        attend_back_body,
        grid=(pairs,),
        in_specs=[
            pl.BlockSpec((tokens, 1), lambda j: (0, 0)),
            pl.BlockSpec((1, tokens), lambda j: (0, 0)),
        ]
        + head_specs(tokens, (0, pairs, 2 * pairs))
        + head_specs(tokens, (0,)),
        out_specs=pl.BlockSpec((tokens, 3 * D), lambda j: (0, 0)),
        out_shape=jax.ShapeDtypeStruct((tokens, 3 * D), LOWER),
        scratch_shapes=[pltpu.VMEM((tokens, tokens), WIDE)],
        **params("attend_back", 5 * tokens * tokens * D, 14 * tokens * D, tokens * tokens * D // HDIM),
    )(segment[:, None], segment[None, :], qkv, qkv, qkv, grad_mixed)


def full(shape):
    return pl.BlockSpec(shape, lambda *index: (0,) * len(shape))


def experts_forward_body(*refs):
    (*pieces, w_in_ref, w_out_ref, gate_ref, up_ref, inner_ref, rows_ref), rest = (
        refs[: len(refs) // 2 + 3],
        refs[len(refs) // 2 + 3 :],
    )
    *parts, acc_ref = rest
    j = pl.program_id(0)

    @pl.when(j == 0)
    def _():
        for i, piece in enumerate(pieces):
            rows_ref[i * CAP : (i + 1) * CAP, :] = piece[...]
        acc_ref[...] = jnp.zeros(acc_ref.shape, WIDE)

    rows = rows_ref[...]
    gate = plain(rows, w_in_ref[0])
    up = plain(rows, w_in_ref[1])
    inner = (jax.nn.silu(gate) * up).astype(LOWER)
    gate_ref[...] = gate
    up_ref[...] = up
    inner_ref[...] = inner
    acc_ref[...] += plain(inner, w_out_ref[...])

    @pl.when(j == pl.num_programs(0) - 1)
    def _():
        for i, part in enumerate(parts):
            part[...] = acc_ref[i * CAP : (i + 1) * CAP, :].astype(LOWER)


def experts_forward(pieces, w_in, w_out):
    rows, hidden = len(pieces) * CAP, w_out.shape[0]
    tile = min(hidden, 1024)
    piece = full((CAP, D))
    band = pl.BlockSpec((rows, tile), lambda j: (0, j))
    gate, up, inner, joined, *parts = pl.pallas_call(
        experts_forward_body,
        grid=(hidden // tile,),
        in_specs=[piece] * len(pieces)
        + [
            pl.BlockSpec((2, D, tile), lambda j: (0, 0, j)),
            pl.BlockSpec((tile, D), lambda j: (j, 0)),
        ],
        out_specs=[band, band, band, full((rows, D))] + [piece] * len(pieces),
        out_shape=[
            jax.ShapeDtypeStruct((rows, hidden), WIDE),
            jax.ShapeDtypeStruct((rows, hidden), WIDE),
            jax.ShapeDtypeStruct((rows, hidden), LOWER),
            jax.ShapeDtypeStruct((rows, D), LOWER),
        ]
        + [jax.ShapeDtypeStruct((CAP, D), LOWER)] * len(pieces),
        scratch_shapes=[pltpu.VMEM((rows, D), WIDE)],
        **params("experts_forward", 3 * rows * hidden * D, 6 * hidden * D + 10 * rows * hidden),
    )(*pieces, w_in, w_out)
    return gate, up, inner, joined, parts


def experts_backward_body(*refs):
    count = (len(refs) - 7) // 2
    pieces, refs = refs[:count], refs[count:]
    gate_ref, up_ref, w_in_ref, w_out_ref, backs_ref, rows_ref, *parts, acc_ref = refs
    j = pl.program_id(0)

    @pl.when(j == 0)
    def _():
        for i, piece in enumerate(pieces):
            rows_ref[i * CAP : (i + 1) * CAP, :] = piece[...]
        acc_ref[...] = jnp.zeros(acc_ref.shape, WIDE)

    grad_inner = contract_cols(rows_ref[...], w_out_ref[...])
    gate, up = gate_ref[...], up_ref[...]
    sig = jax.nn.sigmoid(gate)
    grad_gate = (grad_inner * up * sig * (1.0 + gate * (1.0 - sig))).astype(LOWER)
    grad_up = (grad_inner * gate * sig).astype(LOWER)
    backs_ref[0] = grad_gate
    backs_ref[1] = grad_up
    acc_ref[...] += contract_cols(grad_gate, w_in_ref[0]) + contract_cols(grad_up, w_in_ref[1])

    @pl.when(j == pl.num_programs(0) - 1)
    def _():
        for i, part in enumerate(parts):
            part[...] = acc_ref[i * CAP : (i + 1) * CAP, :].astype(LOWER)


def experts_backward(pieces, gate, up, w_in, w_out):
    rows, hidden = gate.shape
    tile = min(hidden, 1024)
    piece = full((CAP, D))
    band = pl.BlockSpec((rows, tile), lambda j: (0, j))
    backs, joined, *parts = pl.pallas_call(
        experts_backward_body,
        grid=(hidden // tile,),
        in_specs=[piece] * len(pieces)
        + [
            band,
            band,
            pl.BlockSpec((2, D, tile), lambda j: (0, 0, j)),
            pl.BlockSpec((tile, D), lambda j: (j, 0)),
        ],
        out_specs=[pl.BlockSpec((2, rows, tile), lambda j: (0, 0, j)), full((rows, D))]
        + [piece] * len(pieces),
        out_shape=[
            jax.ShapeDtypeStruct((2, rows, hidden), LOWER),
            jax.ShapeDtypeStruct((rows, D), LOWER),
        ]
        + [jax.ShapeDtypeStruct((CAP, D), LOWER)] * len(pieces),
        scratch_shapes=[pltpu.VMEM((rows, D), WIDE)],
        **params("experts_backward", 3 * rows * hidden * D, 6 * hidden * D + 12 * rows * hidden),
    )(*pieces, gate, up, w_in, w_out)
    return backs, joined, parts


def grads_in_body(
    place_ref, rows_a, rows_b, back_a, back_b, keep_ref, give_ref, sum_ref, turned_ref, back_ref
):
    rows = rows_a.shape[0]

    @pl.when((pl.program_id(0) == 0) & (pl.program_id(1) == 0))
    def _():
        turned_ref[:, :rows] = rows_a[...].T
        turned_ref[:, rows:] = rows_b[...].T

    back_ref[:rows, :] = back_a[0]
    back_ref[rows:, :] = back_b[0]
    sum_ref[...] = plain(turned_ref[...], back_ref[...])
    size = keep_ref.shape[2]
    for pair in range(2):
        for core, out_ref in enumerate((keep_ref, give_ref)):
            start = pl.multiple_of((place_ref[1] ^ (2 * pair + core)) * size, 8)
            out_ref[0, pair] = sum_ref[pl.ds(start, size), :].astype(LOWER)


def grads_in(place, rows_a, rows_b, back_a, back_b):
    rows, hidden = back_a.shape[1:]
    tile = 1024
    size = D // 4
    back = pl.BlockSpec((1, rows, tile), lambda k, j, place: (k, 0, j))
    out = pl.BlockSpec((1, 2, size, tile), lambda k, j, place: (k, 0, 0, j))
    return pl.pallas_call(
        grads_in_body,
        grid_spec=pltpu.PrefetchScalarGridSpec(
            num_scalar_prefetch=1,
            grid=(2, hidden // tile),
            in_specs=[full((rows, D)), full((rows, D)), back, back],
            out_specs=[out, out],
            scratch_shapes=[
                pltpu.VMEM((D, tile), WIDE),
                pltpu.VMEM((D, 2 * rows), LOWER),
                pltpu.VMEM((2 * rows, tile), LOWER),
            ],
        ),
        out_shape=[jax.ShapeDtypeStruct((2, 2, size, hidden), LOWER)] * 2,
        **params("grads_in", 4 * rows * hidden * D, 4 * hidden * D + 8 * rows * hidden),
    )(place, rows_a, rows_b, back_a, back_b)


def grads_out_body(place_ref, inner_a, inner_b, back_a, back_b, out_ref):
    total = contract_rows(inner_a[...], back_a[...]) + contract_rows(inner_b[...], back_b[...])
    out_ref[0] = total.astype(LOWER)


def grads_out(place, core, inner_a, inner_b, back_a, back_b):
    rows, hidden = inner_a.shape
    size = hidden // 4
    band = pl.BlockSpec((rows, size), lambda x, place: (0, place[1] ^ (2 * x + core)))
    return pl.pallas_call(
        grads_out_body,
        grid_spec=pltpu.PrefetchScalarGridSpec(
            num_scalar_prefetch=1,
            grid=(2,),
            in_specs=[band, band, full((rows, D)), full((rows, D))],
            out_specs=pl.BlockSpec((1, size, D), lambda x, place: (x, 0, 0)),
        ),
        out_shape=jax.ShapeDtypeStruct((2, size, D), LOWER),
        **params("grads_out", rows * hidden * D, hidden * D + 2 * rows * hidden),
    )(place, inner_a, inner_b, back_a, back_b)


def sum_experts_out(place, near, far, near_back, far_back, came_back):
    if lax.axis_size("rep") != 4:
        grad = contract_rows(
            jnp.concatenate([near[2], far[2]]), jnp.concatenate([near_back[1], far_back[1]])
        ).astype(LOWER)
        return [lax.psum_scatter(grad, "rep", scatter_dimension=0, tiled=True)], came_back
    half = len(came_back) // 2
    arrived, rows = lax.optimization_barrier((came_back[:half], (near_back[1], far_back[1])))
    came_back = arrived + came_back[half:]
    ends = (near[2], far[2]) + rows
    give, keep = grads_out(place, 1, *ends), grads_out(place, 0, *ends)
    came_back, give, keep = lax.optimization_barrier((came_back, give, keep))
    take = flip(give, "rep", 1, 4)
    return [keep[0], take[0], (keep[1].astype(WIDE) + take[1].astype(WIDE)).astype(LOWER)], came_back


def sum_experts_in(place, near, far, near_back, far_back, after, eout_g):
    if lax.axis_size("rep") != 4:
        rows = jnp.concatenate([near[3], far[3]])
        backs = jnp.concatenate([near_back[0], far_back[0]], 1)
        grad = jnp.stack([contract_rows(rows, back).astype(LOWER) for back in backs])
        return [lax.psum_scatter(grad, "rep", scatter_dimension=1, tiled=True)], after, eout_g
    after, backs = lax.optimization_barrier((after, (near_back[0], far_back[0])))
    keep, give = grads_in(place, near[3], far[3], *backs)
    crossed = flip(eout_g[2], "rep", 2, 4)
    give, crossed = lax.optimization_barrier((give, crossed))
    take = flip(give, "rep", 1, 4)
    far = [(keep[k, 1].astype(WIDE) + take[k, 1].astype(WIDE)).astype(LOWER) for k in range(2)]
    return [keep[:, 0], take[:, 0], far], after, eout_g[:2] + [crossed]


def add_up(parts):
    return sum([part.astype(WIDE) for part in parts[1:]], parts[0].astype(WIDE))


def cut(value, count):
    size = value.shape[0] // count
    return [value[i * size : (i + 1) * size] for i in range(count)]


def send_slots(buffer, n_dp, shards):
    half = n_dp // 2
    blocks = trade([b for b in buffer for _ in range(shards)], n_dp)
    return blocks[:half], blocks[half:]


def return_slots(near, far, n_dp, shards):
    blocks = trade(list(near) + list(far), n_dp)
    return [jnp.concatenate(blocks[s::shards]) for s in range(shards)]


def pick_slots(picks, received):
    return sum(plain(picks, part) for part in received)


def layer_forward(hidden, lens, routes, w_qkv, w_attn, small_all, w_in, w_out, own, n_dp):
    shards = n_dp // EXPERTS
    gains, const_vec, router, const_gate = (
        small_all[:3].astype(WIDE),
        small_all[3:5].astype(WIDE),
        small_all[5:17].astype(LOWER),
        small_all[17:21].astype(LOWER),
    )
    tokens = hidden.shape[0]
    segment = segments(lens, tokens)
    normed, scale_one = norm_fwd(hidden, gains[0])
    normed_low = normed.astype(LOWER)
    qkv = contract_cols(normed_low, w_qkv).astype(LOWER)
    mixed = attend(qkv, segment)
    first = hidden + contract_cols(mixed, w_attn)
    second, scale_two = norm_fwd(first, gains[1])
    second_low = second.astype(LOWER)
    route_p = jax.nn.softmax(contract_cols(second_low, router), -1)
    hits = routes[:, :, None] == jnp.arange(EXPERTS + NULLS, dtype=jnp.int32)[None, None, :]
    used = jnp.sum(hits.astype(WIDE), 1)
    weight = route_p * used
    earlier = jnp.tril(jnp.ones((tokens, tokens), LOWER), -1)
    rank = plain(earlier, used[:, :EXPERTS].astype(LOWER)).astype(jnp.int32)
    apart = jnp.arange(EXPERTS, dtype=jnp.int32) ^ (own // shards)
    place = apart[None] * CAP + rank
    place = jnp.where(rank < CAP, place, -1)
    real_hits = hits[:, :, :EXPERTS]
    slot = jnp.max(jnp.where(real_hits, place[:, None, :], -1), -1)
    w_slot = jnp.sum(jnp.where(real_hits, weight[:, None, :EXPERTS], 0.0), -1)
    all_slots = jnp.arange(EXPERTS * CAP, dtype=jnp.int32)
    picks = [(slot[:, k : k + 1] == all_slots[None]).astype(LOWER) for k in range(2)]
    both = picks[0] + picks[1]
    buffer = contract_rows(both, second_low).astype(LOWER)
    sent = send_slots(cut(buffer, EXPERTS), n_dp, shards)
    near, far = (experts_forward(rows, w_in, w_out) for rows in sent)
    returned = return_slots(near[4], far[4], n_dp, shards)
    outs = [pick_slots(picks[k], returned) for k in range(2)]
    moe = w_slot[:, 0:1] * outs[0] + w_slot[:, 1:2] * outs[1]
    const_p = jax.nn.softmax(contract_cols(second_low, const_gate).reshape(tokens, 2, 2), -1)
    const_out = const_p[:, :, 0:1] * second[:, None, :] + const_p[:, :, 1:2] * const_vec[None]
    moe = moe + weight[:, EXPERTS + 1 : EXPERTS + 2] * second
    moe = (
        moe
        + weight[:, EXPERTS + 2 : EXPERTS + 3] * const_out[:, 0]
        + weight[:, EXPERTS + 3 :] * const_out[:, 1]
    )
    third = first + moe
    saved = dict(
        gains=gains,
        const_vec=const_vec,
        router=router,
        const_gate=const_gate,
        segment=segment,
        scale_one=scale_one,
        normed_low=normed_low,
        qkv=qkv,
        mixed=mixed,
        first=first,
        second=second,
        scale_two=scale_two,
        second_low=second_low,
        route_p=route_p,
        hits=hits,
        used=used,
        weight=weight,
        w_slot=w_slot,
        slot=slot,
        picks=picks,
        both=both,
        near=near,
        far=far,
        outs=outs,
        const_p=const_p,
        const_out=const_out,
    )
    return (third, saved)


def vocab_tile(rows):
    return min(1024, (1 << 20) // rows)


def scores_body(aim_ref, rows_ref, table_ref, expo_ref, tops_ref, stats_ref, *, step_rows):
    tile = table_ref.shape[0]
    j = pl.program_id(0)

    @pl.when(j == 0)
    def _():
        stats_ref[0:1, :] = jnp.full((1, stats_ref.shape[1]), -1e30, WIDE)
        stats_ref[1:8, :] = jnp.zeros((7, stats_ref.shape[1]), WIDE)

    table = table_ref[...]
    for start in range(0, rows_ref.shape[0], step_rows):
        cols = slice(start, start + step_rows)
        logits = contract_cols(table, rows_ref[cols, :])
        top = jnp.max(logits, 0, keepdims=True)
        expo = jnp.exp(logits - top)
        expo_ref[:, cols] = expo.astype(LOWER)
        total = jnp.sum(expo, 0, keepdims=True)
        place = lax.broadcasted_iota(jnp.int32, logits.shape, 0)
        hit = place == aim_ref[:, cols] - j * tile
        aimed = jnp.sum(jnp.where(hit, logits, 0.0), 0, keepdims=True)
        tops_ref[0, :, cols] = top
        old = stats_ref[0:1, cols]
        high = jnp.maximum(old, top)
        stats_ref[1:2, cols] = stats_ref[1:2, cols] * jnp.exp(old - high) + total * jnp.exp(
            top - high
        )
        stats_ref[0:1, cols] = high
        stats_ref[2:3, cols] = stats_ref[2:3, cols] + aimed


def vocab_scores(rows, table, aim):
    count, vocab = rows.shape[0], table.shape[0]
    tile = vocab_tile(count)
    steps = vocab // tile
    return pl.pallas_call(
        functools.partial(scores_body, step_rows=ROWS),
        grid=(steps,),
        in_specs=[
            pl.BlockSpec((1, count), lambda j: (0, 0)),
            pl.BlockSpec((count, D), lambda j: (0, 0)),
            pl.BlockSpec((tile, D), lambda j: (j, 0)),
        ],
        out_specs=[
            pl.BlockSpec((tile, count), lambda j: (j, 0)),
            pl.BlockSpec((1, 1, count), lambda j: (j, 0, 0)),
            pl.BlockSpec((8, count), lambda j: (0, 0)),
        ],
        out_shape=[
            jax.ShapeDtypeStruct((vocab, count), LOWER),
            jax.ShapeDtypeStruct((steps, 1, count), WIDE),
            jax.ShapeDtypeStruct((8, count), WIDE),
        ],
        **params("vocab_scores", count * vocab * D, 2 * vocab * (count + D), count * vocab),
    )(aim, rows, table)


def dlogits_body(aim_ref, scale_ref, expo_ref, table_ref, grad_ref, out_ref, *, step_rows, unit):
    tile = table_ref.shape[0]
    j = pl.program_id(0)

    @pl.when(j == 0)
    def _():
        out_ref[...] = jnp.zeros(out_ref.shape, WIDE)

    table = table_ref[...]
    for start in range(0, expo_ref.shape[1], step_rows):
        cols = slice(start, start + step_rows)
        expo = expo_ref[:, cols].astype(WIDE)
        place = lax.broadcasted_iota(jnp.int32, expo.shape, 0)
        hit = place == aim_ref[:, cols] - j * tile
        grad = (expo * scale_ref[0, :, cols] - jnp.where(hit, unit, 0.0)).astype(LOWER)
        grad_ref[:, cols] = grad
        out_ref[cols, :] += contract_rows(grad, table)


def vocab_grad_rows(expo, table, aim, scale, unit):
    vocab, count = expo.shape
    tile = vocab_tile(count)
    steps = vocab // tile
    return pl.pallas_call(
        functools.partial(dlogits_body, step_rows=ROWS, unit=unit),
        grid=(steps,),
        in_specs=[
            pl.BlockSpec((1, count), lambda j: (0, 0)),
            pl.BlockSpec((1, 1, count), lambda j: (j, 0, 0)),
            pl.BlockSpec((tile, count), lambda j: (j, 0)),
            pl.BlockSpec((tile, D), lambda j: (j, 0)),
        ],
        out_specs=[
            pl.BlockSpec((tile, count), lambda j: (j, 0)),
            pl.BlockSpec((count, D), lambda j: (0, 0)),
        ],
        out_shape=[
            jax.ShapeDtypeStruct((vocab, count), LOWER),
            jax.ShapeDtypeStruct((count, D), WIDE),
        ],
        **params("vocab_grad_rows", count * vocab * D, 2 * vocab * (2 * count + D)),
    )(aim, scale, expo, table)


def vocab_grad_table_body(grad_ref, rows_ref, out_ref):
    out_ref[...] = plain(grad_ref[...], rows_ref[...]).astype(LOWER)


def vocab_grad_table(grad, rows):
    vocab, count = grad.shape
    tile = 2 * vocab_tile(count)
    return pl.pallas_call(
        vocab_grad_table_body,
        grid=(vocab // tile,),
        in_specs=[
            pl.BlockSpec((tile, count), lambda j: (j, 0)),
            pl.BlockSpec((count, D), lambda j: (0, 0)),
        ],
        out_specs=pl.BlockSpec((tile, D), lambda j: (j, 0)),
        out_shape=jax.ShapeDtypeStruct((vocab, D), LOWER),
        **params("vocab_grad_table", count * vocab * D, 2 * vocab * (count + D)),
    )(grad, rows)


def head_step(third, positions, targets, table_all, gain, own, n_dp):
    final, unused = norm_fwd(third, gain)
    tokens = third.shape[0]
    count = positions.shape[0]
    pick = positions[:, None] == jnp.arange(tokens, dtype=jnp.int32)[None, :]
    chosen = plain(pick.astype(LOWER), final.astype(LOWER)).astype(LOWER)
    near, far = gather_flips(chosen, n_dp)
    gathered = jnp.concatenate(near + far)
    aim = by_distance(targets, own).reshape(1, -1) - own * table_all.shape[0]
    expo, tops, stats = vocab_scores(gathered, table_all, aim)
    stats = by_distance(stats.reshape(8, n_dp, count).swapaxes(0, 1), own)
    stats = swap(jnp.broadcast_to(stats[None], (n_dp,) + stats.shape), "dp")
    high = jnp.max(stats[:, :, 0], 0)
    sums = jnp.sum(stats[:, :, 1] * jnp.exp(stats[:, :, 0] - high[None]), 0)
    lse = high + jnp.log(sums)
    lse = by_distance(lse, own)
    loss_part = jnp.sum(lse[0] - by_distance(jnp.sum(stats[:, :, 2], 0), own)[0]) / count
    lse = lse.reshape(1, 1, -1)
    scale = jnp.exp(tops - lse) / count
    grad_logits, grad_rows = vocab_grad_rows(expo, table_all, aim, scale, 1.0 / count)
    grad_rows = grad_rows.astype(LOWER)
    grad_chosen = sum_flips(cut(grad_rows, n_dp), n_dp)
    grad_table = vocab_grad_table(grad_logits, gathered)
    grad_chosen, grad_table = lax.optimization_barrier((grad_chosen, grad_table))
    return (loss_part, grad_chosen, grad_table)


def head_back_body(*refs, count):
    terms, refs = refs[:count], refs[count:]
    spot_ref, slot_ref, third_ref, gain_ref, w_ref, grad_ref, gain_grad_ref, *blocks = refs
    tokens = third_ref.shape[0]
    total = terms[0][...].astype(WIDE)
    for term in terms[1:]:
        total = total + term[...].astype(WIDE)
    spots = spot_ref[...] == lax.broadcasted_iota(jnp.int32, (tokens, total.shape[0]), 0)
    spots = spots.astype(WIDE).astype(LOWER)
    grad = jnp.zeros(third_ref.shape, WIDE)
    for _ in range(3):
        piece = total.astype(LOWER)
        total = total - piece.astype(WIDE)
        grad = grad + plain(spots, piece)
    third = third_ref[...]
    scale = lax.rsqrt(jnp.mean(third * third, -1, keepdims=True) + EPS)
    normed = third * scale
    gain_grad_ref[...] = jnp.sum(grad * normed, 0, keepdims=True)
    inner = grad * gain_ref[...]
    grad = scale * (inner - normed * jnp.mean(inner * normed, -1, keepdims=True))
    grad_ref[...] = grad
    out = jnp.zeros((EXPERTS * CAP, D), WIDE)
    places = lax.broadcasted_iota(jnp.int32, (EXPERTS * CAP, tokens), 0)
    for k in range(2):
        picks = (slot_ref[k : k + 1, :] == places).astype(WIDE).astype(LOWER)
        out = out + plain(picks, (w_ref[:, k : k + 1] * grad).astype(LOWER))
    for e, block in enumerate(blocks):
        block[...] = out[e * CAP : (e + 1) * CAP, :].astype(LOWER)


def head_back(terms, positions, slot, third, gain, w_slot):
    tokens = third.shape[0]
    grad_third, grad_gain, *blocks = pl.pallas_call(
        functools.partial(head_back_body, count=len(terms)),
        out_shape=[
            jax.ShapeDtypeStruct((tokens, D), WIDE),
            jax.ShapeDtypeStruct((1, D), WIDE),
        ]
        + [jax.ShapeDtypeStruct((CAP, D), LOWER)] * EXPERTS,
        **params("head_back", 2 * tokens * EXPERTS * CAP * D, 12 * tokens * D),
    )(*terms, positions[None, :], slot.T, third, gain[None, :], w_slot)
    return grad_third, grad_gain[0], blocks


def layer_backward(hidden, grad_third, saved, w_qkv, w_attn, w_in, w_out, n_dp, place, blocks):
    shards = n_dp // EXPERTS
    gains, const_vec = saved["gains"], saved["const_vec"]
    router, const_gate = saved["router"], saved["const_gate"]
    tokens = hidden.shape[0]
    weight = saved["weight"]
    route_p = saved["route_p"]
    second_wide = saved["second_low"].astype(WIDE)
    sent = send_slots(blocks, n_dp, shards)
    near, far = saved["near"], saved["far"]
    near_back = experts_backward(sent[0], near[0], near[1], w_in, w_out)
    far_back = experts_backward(sent[1], far[0], far[1], w_in, w_out)
    blocks = trade(list(near_back[2]) + list(far_back[2]), n_dp)
    ends = (place, near, far, near_back, far_back)
    eout_g, blocks = sum_experts_out(*ends, blocks)
    came_back = [jnp.concatenate(blocks[s::shards]) for s in range(shards)]
    dots = [jnp.sum(saved["outs"][k] * grad_third, -1, keepdims=True) for k in range(2)]
    hits = saved["hits"].astype(WIDE)
    grad_real = (dots[0] * hits[:, 0] + dots[1] * hits[:, 1])[:, :EXPERTS]
    grad_copy = jnp.sum(grad_third * saved["second"], -1, keepdims=True)
    grad_const = jnp.sum(grad_third[:, None, :] * saved["const_out"], -1)
    grad_weight = jnp.concatenate(
        [grad_real, jnp.zeros((tokens, 1), WIDE), grad_copy, grad_const], 1
    )
    grad_p = grad_weight * saved["used"]
    grad_logit = route_p * (grad_p - jnp.sum(route_p * grad_p, -1, keepdims=True))
    const_p = saved["const_p"]
    w_const = weight[:, EXPERTS + 2 :]
    along_vec = jnp.dot(grad_third, const_vec.T, precision=HIGH)
    grad_alpha = w_const[:, :, None] * jnp.stack(
        [jnp.broadcast_to(grad_copy, along_vec.shape), along_vec], -1
    )
    grad_clog = (const_p * (grad_alpha - jnp.sum(const_p * grad_alpha, -1, keepdims=True))).reshape(
        tokens, 4
    )
    grad_cvec = rows_high(w_const * const_p[:, :, 1], grad_third)
    logit_all = jnp.concatenate([grad_logit, grad_clog], 1)
    grad_gates = rows_high(logit_all, second_wide)
    gates_all = jnp.concatenate([router, const_gate], 0).astype(WIDE)
    grad_second = jnp.dot(logit_all, gates_all, precision=HIGH)
    carry = weight[:, EXPERTS + 1 : EXPERTS + 2] + jnp.sum(
        w_const * const_p[:, :, 0], -1, keepdims=True
    )
    grad_second = grad_second + carry * grad_third
    grad_second = grad_second + pick_slots(saved["both"], came_back)
    grad_first_norm, grad_gain_two = norm_back(
        saved["first"], saved["scale_two"], gains[1], grad_second
    )
    grad_first = grad_third + grad_first_norm
    grad_attn = grad_first.astype(LOWER)
    grad_mixed = plain(grad_attn, w_attn).astype(LOWER)
    grad_qkv = attend_back(saved["qkv"], grad_mixed, saved["segment"])
    grad_qkv, eout_g = lax.optimization_barrier((grad_qkv, eout_g))
    grad_normed = plain(grad_qkv, w_qkv)
    unused, grad_gain_one = norm_back(hidden, saved["scale_one"], gains[0], grad_normed)
    left = (grad_qkv, grad_attn)
    return (left, grad_gain_one, grad_gain_two, grad_cvec, grad_gates, ends, eout_g)


def fold(value):
    rows, cols = value.shape
    if rows % 8 or cols % LANES:
        return jnp.pad(jnp.sum(value * value)[None], (0, LANES - 1))
    squares = jnp.sum((value * value).reshape(rows // 8, 8, cols), 0)
    return jnp.sum(squares.reshape(8, cols // LANES, LANES), (0, 1))


def own_squares(arrays, device):
    dense, small = arrays
    width = dense.shape[1]
    front = (device * width + jnp.arange(width, dtype=jnp.int32) < 3 * D).astype(WIDE)
    lanes = (0, LANES - width)
    dense_sq = jnp.sum(dense * dense, 0)
    return [
        jnp.pad(dense_sq * front, lanes),
        jnp.pad(dense_sq * (1.0 - front), lanes),
        jnp.pad(jnp.sum(small[:5] * small[:5], 0), (0, LANES - small.shape[1])),
        jnp.pad(jnp.sum(small[5:] * small[5:], 0), (0, LANES - small.shape[1])),
    ]


def update_of(weight, first, second):
    corr = 1.0 - 0.5**STEP
    return first / corr / (jnp.sqrt(second / corr) + EPS) + 0.01 * weight


def moments(weight, first, second, grad):
    first = 0.5 * first + 0.5 * grad
    second = 0.5 * second + 0.5 * grad * grad
    return (first, second, update_of(weight, first, second))


def shared_update(weight, first, second, parts):
    first, second, update = moments(weight, first, second, add_up(parts))
    lanes = weight.shape[-1]
    return (first, second, fold(weight.reshape(-1, lanes)), fold(update.reshape(-1, lanes)))


def local(
    x_in,
    seq_lens,
    routes,
    positions,
    targets,
    dense_w,
    small_w,
    expert_in,
    expert_out,
    table,
    dense_m,
    small_m,
    expin_m,
    expout_m,
    table_m,
    dense_v,
    small_v,
    expin_v,
    expout_v,
    table_v,
):
    n_dp, n_rep = lax.axis_size("dp"), lax.axis_size("rep")
    devices = n_dp * n_rep
    own = lax.axis_index("dp")
    device = own * n_rep + lax.axis_index("rep")
    masters = (dense_w, small_w, expert_in, expert_out, table)
    width, thin = dense_w.shape[1], small_w.shape[1]
    place = jnp.stack([own, lax.axis_index("rep")]).astype(jnp.int32)
    flips = n_rep == 4 and width % 16 == 0 and thin % 8 == 0
    shared = (expert_in, expert_out, table)
    if flips:
        block, shared = lax.optimization_barrier((pack(dense_w, small_w), shared))
        w_qkv, w_attn, small_all = gather_weights(block, place, n_dp, width, thin)
    else:
        dense_t = lax.all_gather(dense_w.T.astype(LOWER), BOTH, axis=0, tiled=True)
        small_t = jnp.pad(small_w.T.astype(LOWER), ((0, 0), (0, LANES - small_w.shape[0])))
        small_all = share(small_t, BOTH, devices).reshape(-1, LANES).T
        w_qkv, w_attn = dense_t[: 3 * D], dense_t[3 * D :]
    w_in, w_out, table_all = (
        lax.all_gather(value.astype(LOWER), "rep", axis=axis, tiled=True)
        for value, axis in zip(shared, (1, 0, 0))
    )
    hidden = x_in.astype(WIDE)
    third, saved = layer_forward(
        hidden, seq_lens[0], routes, w_qkv, w_attn, small_all, w_in, w_out, own, n_dp
    )
    loss_part, terms, grad_table = head_step(
        third, positions, targets[0], table_all, saved["gains"][2], own, n_dp
    )
    grad_third, grad_gain_final, blocks = head_back(
        terms, positions, saved["slot"], third, saved["gains"][2], saved["w_slot"]
    )
    table_g = lax.psum_scatter(grad_table, "rep", scatter_dimension=0, tiled=True)
    left, gain_one, gain_two, grad_cvec, grad_gates, ends, eout_g = layer_backward(
        hidden, grad_third, saved, w_qkv, w_attn, w_in, w_out, n_dp, place, blocks
    )
    small_grad = jnp.concatenate(
        [gain_one[None], gain_two[None], grad_gain_final[None], grad_cvec, grad_gates], 0
    )
    loss_row = jnp.pad(loss_part[None], (0, LANES - 1))

    def crossed(value):
        return flip(value, "rep", 2, 4) if n_rep == 4 else value

    def table_job(done):
        made = shared_update(table, table_m, table_v, [table_g])
        return made, (crossed(ein_g[2][0]) if n_rep == 4 else None)

    def out_job(done):
        made = shared_update(expert_out, expout_m, expout_v, eout_g)
        return made, (crossed(ein_g[2][1]) if n_rep == 4 else None)

    def in_job(done):
        parts = ein_g
        if n_rep == 4:
            parts = ein_g[:2] + [jnp.stack([done[0][1], done[1][1]])]
        return shared_update(expert_in, expin_m, expin_v, parts), None

    jobs = (table_job, out_job, in_job)
    normed, mixed = saved["normed_low"], saved["mixed"]
    if flips:
        turned = jnp.pad(small_grad, ((0, LANES - small_grad.shape[0]), (0, 0))).T
        mine, other = dense_grads(place, *left, normed, mixed, turned, n_dp, width)
        ein_g, other, eout_g = sum_experts_in(*ends, other, eout_g)
        block, done = sum_weights(mine, other, n_dp, jobs)
        small_g = block[width:].reshape(8, -1, LANES)[:, : thin // 8].swapaxes(0, 1)
        small_g = small_g.reshape(thin, LANES)[:, : small_w.shape[0]].T
    else:
        dense_grad = jnp.concatenate(
            [contract_rows(left[0], normed), contract_rows(left[1], mixed)]
        )
        small_blocks = small_grad.reshape(-1, devices, thin).swapaxes(0, 1).reshape(devices, -1)
        extra = -(-small_blocks.shape[1] // (8 * D)) * 8 * D
        small_blocks = jnp.pad(small_blocks, ((0, 0), (0, extra - small_blocks.shape[1])))
        blocks = jnp.concatenate(
            [dense_grad.reshape(devices, width, D), small_blocks.reshape(devices, -1, D)], 1
        )
        block = scatter_sum(blocks.reshape((n_dp, n_rep) + blocks.shape[1:]), n_dp, n_rep)
        small_g = block[width:].reshape(-1)[: small_w.size].reshape(small_w.shape)
        ein_g, block, eout_g = sum_experts_in(*ends, block, eout_g)
        done = []
        for job in jobs:
            done.append(job(done))
    dense_g = block[:width].T
    own_results = [
        moments(w, m, v, g)
        for w, m, v, g in ((dense_w, dense_m, dense_v, dense_g), (small_w, small_m, small_v, small_g))
    ]
    made = [done[2][0], done[1][0], done[0][0]]
    rows = own_squares((dense_w, small_w), device) + [one[2] for one in made]
    rows = rows + own_squares([r[2] for r in own_results], device) + [one[3] for one in made]
    rows = jnp.stack(rows + [loss_row, loss_row * 0.0])
    sums = jnp.sum(share(rows, BOTH, devices), (0, 2))
    shared_results = [(m, v, update_of(w, m, v)) for w, (m, v, *_) in zip(masters[2:], made)]
    results = own_results + shared_results
    loss = sums[14]
    weight_sq, update_sq = sums[:7], sums[7:14]
    weight_norm = jnp.sqrt(weight_sq)
    update_norm = jnp.sqrt(update_sq)
    trust = weight_norm / update_norm
    column = device * width + jnp.arange(width, dtype=jnp.int32)
    dense_scale = jnp.where(column < 3 * D, trust[0], trust[1])[None, :]
    small_scale = jnp.where(jnp.arange(21, dtype=jnp.int32) < 5, trust[2], trust[3])[:, None]
    scales = (dense_scale, small_scale, trust[4], trust[5], trust[6])
    outs = [loss, jnp.stack([weight_norm, update_norm, trust])]
    for w, r, factor in zip(masters, results, scales):
        fresh = w - 0.2 * factor * r[2]
        outs += [r[0], r[1], fresh, fresh.astype(LOWER)]
    return tuple(outs)


def solution(mesh):
    in_specs = (
        P(("dp", "rep"), None),
        P(("dp", "rep"), None),
        P(("dp", "rep"), None),
        P(("dp", "rep")),
        P("rep", None, None),
        P(None, ("dp", "rep")),
        P(None, ("dp", "rep")),
        P(None, "rep", "dp"),
        P(("dp", "rep"), None),
        P(("dp", "rep"), None),
        P(None, ("dp", "rep")),
        P(None, ("dp", "rep")),
        P(None, "rep", "dp"),
        P(("dp", "rep"), None),
        P(("dp", "rep"), None),
        P(None, ("dp", "rep")),
        P(None, ("dp", "rep")),
        P(None, "rep", "dp"),
        P(("dp", "rep"), None),
        P(("dp", "rep"), None),
    )
    out_specs = (
        P(),
        P(),
        P(None, ("dp", "rep")),
        P(None, ("dp", "rep")),
        P(None, ("dp", "rep")),
        P(None, ("dp", "rep")),
        P(None, ("dp", "rep")),
        P(None, ("dp", "rep")),
        P(None, ("dp", "rep")),
        P(None, ("dp", "rep")),
        P(None, "rep", "dp"),
        P(None, "rep", "dp"),
        P(None, "rep", "dp"),
        P(None, "rep", "dp"),
        P(("dp", "rep"), None),
        P(("dp", "rep"), None),
        P(("dp", "rep"), None),
        P(("dp", "rep"), None),
        P(("dp", "rep"), None),
        P(("dp", "rep"), None),
        P(("dp", "rep"), None),
        P(("dp", "rep"), None),
    )
    return jax.shard_map(local, mesh=mesh, in_specs=in_specs, out_specs=out_specs, check_vma=False)
```
